32 devices in a mesh: gx: 16 (over z, y, x), gy: 2 (over core).
Axes of the slice: x: 2, y: 2, z: 4, core: 2. Of those that a mesh axis runs over, the one named last changes fastest.
Arguments:
- spectra: bfloat16 [2, 2, 512, 256], P(None, None, 'gx', 'gy'), may hold values from -1 to 7, as said below
- noise_weights: bfloat16 [2, 2, 512, 256], P(None, None, 'gx', 'gy'), may hold values from 0.049804688 to 1
- mixing: float32 [2, 2], replicated, may hold values from 0.2 to 2, as said below
Outputs:
- material: float32 [2, 2, 512, 256], P(None, None, 'gx', 'gy')
The draws below stay inside these ranges and needn't reach their ends.
Inputs may be any that keep to these rules, and one draw needn't show every extreme that they name: `spectra`: smooth water and bone structure with sharp bone edges, plus voxel noise. `mixing`: diagonal entries lie between 1 and 2, the others between 0.2 and 0.6.
All inputs are finite; a program needn't handle non-finite values.
Results may differ from the reference program's by a relative error of at most 0.0003.
Values sent between devices are 32-bit elements; how exact they have to be, the bound alone decides.
No kernel may reach another device: no remote copies, remote signals or barrier semaphores. Data moves between devices by JAX's collectives and lax.ppermute only.
A program may use at most 64 MiB of HBM per device.

```python
import math
import jax
import jax.numpy as jnp
from jax import lax

SLICES = 2
LEVELS = 6
COARSE_SWEEPS = 4
CYCLES = 2
NX = 512
NY = 256


def draw_spectra(key, part):
    subkeys = jax.random.split(key, 6)
    row_coord = (jnp.arange(NX, dtype=jnp.float32) + 0.5) / NX
    column_coord = (jnp.arange(NY, dtype=jnp.float32) + 0.5) / NY
    frequency = jax.random.randint(subkeys[0], (3, SLICES, 2), 1, 5).astype(jnp.float32)
    phases = jax.random.uniform(subkeys[1], (3, SLICES), jnp.float32, 0.0, 2.0 * math.pi)
    amplitude = jax.random.uniform(subkeys[2], (3, SLICES), jnp.float32, 0.1, 0.3)
    water_map = jnp.ones((SLICES, NX, NY), jnp.float32)
    for mode_index in range(3):
        angle_map = 2.0 * math.pi * (frequency[mode_index, :, 0][:, None, None] * row_coord[None, :, None] + frequency[mode_index, :, 1][:, None, None] * column_coord[None, None, :]) + phases[mode_index][:, None, None]
        water_map = water_map + amplitude[mode_index][:, None, None] * jnp.sin(angle_map)
    centers = jax.random.uniform(subkeys[3], (4, SLICES, 2), jnp.float32, 0.1, 0.9)
    radius = jax.random.uniform(subkeys[4], (4, SLICES), jnp.float32, 0.05, 0.2)
    bone_map = jnp.zeros((SLICES, NX, NY), jnp.float32)
    for blob_index in range(4):
        row_gap = row_coord[None, :, None] - centers[blob_index, :, 0][:, None, None]
        column_gap = column_coord[None, None, :] - centers[blob_index, :, 1][:, None, None]
        distance = jnp.sqrt(row_gap * row_gap + column_gap * column_gap)
        bone_map = bone_map + 0.6 * jax.nn.sigmoid((radius[blob_index][:, None, None] - distance) / 0.004)
    noise_map = 0.25 * jnp.clip(jax.random.normal(subkeys[5], (2, SLICES, NX, NY), jnp.float32), -4.0, 4.0)
    count_low = water_map + 1.6 * bone_map
    count_high = 0.8 * water_map + 1.1 * bone_map
    return (jnp.stack([count_low, count_high]) + noise_map).astype(jnp.bfloat16)


def draw_mixing(key, part):
    subkeys = jax.random.split(key, 2)
    diagonal_pair = jax.random.uniform(subkeys[0], (2,), jnp.float32, 1.0, 2.0)
    cross_pair = jax.random.uniform(subkeys[1], (2,), jnp.float32, 0.2, 0.6)
    return jnp.stack([jnp.stack([diagonal_pair[0], cross_pair[0]]), jnp.stack([cross_pair[1], diagonal_pair[1]])])


def block_levels(own_key, shape, pieces, smallest, largest):
    loudness = 1.0
    for dim, parts in pieces:
        draws = jax.random.uniform(jax.random.fold_in(jax.random.fold_in(own_key, 6), dim), (parts,), jnp.float32, smallest / len(pieces), largest / len(pieces))
        loudness = loudness * jnp.repeat(jnp.exp(draws), shape[dim] // parts).reshape((-1,) + (1,) * (len(shape) - 1 - dim))
    return loudness


def setup_inputs(seed: int = 0) -> dict:
    splits = jax.random.split(jax.random.key(seed), 4)
    spectra = draw_spectra(jax.random.fold_in(splits[3], 71), 0)
    noise_weights = jnp.clip(jnp.exp(math.log(1.0) - 2.9996462 * jax.random.uniform(splits[1], (2, SLICES, NX, NY), jnp.float32) ** block_levels(splits[1], (2, SLICES, NX, NY), ((2, 16), (3, 2)), -0.2, 0.2)), 0.049804688, 1.0).astype(jnp.bfloat16)
    mixing = draw_mixing(jax.random.fold_in(splits[3], 71), 0)
    return {"spectra": spectra, "noise_weights": noise_weights, "mixing": mixing}


huber_delta = 0.05
relaxation = 0.8
smoothness = 256.0


def material_data(counts, weights, mixing):
    weight_low, weight_high = weights[0], weights[1]
    count_low, count_high = counts[0], counts[1]
    data_water = weight_low * mixing[0, 0] * mixing[0, 0] + weight_high * mixing[1, 0] * mixing[1, 0]
    data_cross = weight_low * mixing[0, 0] * mixing[0, 1] + weight_high * mixing[1, 0] * mixing[1, 1]
    data_bone = weight_low * mixing[0, 1] * mixing[0, 1] + weight_high * mixing[1, 1] * mixing[1, 1]
    water_part = weight_low * mixing[0, 0] * count_low + weight_high * mixing[1, 0] * count_high
    bone_part = weight_low * mixing[0, 1] * count_low + weight_high * mixing[1, 1] * count_high
    return (data_water, data_cross, data_bone), jnp.stack([water_part, bone_part])


def edge_masks(row_start, total_rows, column_start, total_columns, tile_rows, tile_columns):
    row_place = row_start + jnp.arange(tile_rows, dtype=jnp.int32)[:, None]
    column_place = column_start + jnp.arange(tile_columns, dtype=jnp.int32)[None, :]
    extent = (tile_rows, tile_columns)
    upper_rim = jnp.broadcast_to(row_place > 0, extent).astype(jnp.float32)
    lower_rim = jnp.broadcast_to(row_place < total_rows - 1, extent).astype(jnp.float32)
    left_rim = jnp.broadcast_to(column_place > 0, extent).astype(jnp.float32)
    right_rim = jnp.broadcast_to(column_place < total_columns - 1, extent).astype(jnp.float32)
    return (upper_rim, lower_rim, left_rim, right_rim)


def edge_sums(padded, inside_masks):
    center = padded[..., 1:-1, 1:-1]
    neighbours = (padded[..., :-2, 1:-1], padded[..., 2:, 1:-1], padded[..., 1:-1, :-2], padded[..., 1:-1, 2:])
    weight_total = jnp.zeros_like(center)
    weighted_sum = jnp.zeros_like(center)
    for neighbour, inside in zip(neighbours, inside_masks):
        factor = inside * huber_delta / jnp.maximum(jnp.abs(center - neighbour), huber_delta)
        weight_total = weight_total + factor
        weighted_sum = weighted_sum + factor * neighbour
    return center, weight_total, weighted_sum


def apply_operator(padded, data_terms, penalty, inside_masks):
    center, weight_total, weighted_sum = edge_sums(padded, inside_masks)
    data_water, data_cross, data_bone = data_terms
    coupled = jnp.stack([data_water * center[0] + data_cross * center[1], data_cross * center[0] + data_bone * center[1]])
    return coupled + penalty * (weight_total * center - weighted_sum)


def relax(padded, source_term, data_terms, penalty, inside_masks):
    center, weight_total, weighted_sum = edge_sums(padded, inside_masks)
    data_water, data_cross, data_bone = data_terms
    diag_water = data_water + penalty * weight_total[0]
    diag_bone = data_bone + penalty * weight_total[1]
    right_water = source_term[0] + penalty * weighted_sum[0]
    right_bone = source_term[1] + penalty * weighted_sum[1]
    determinant = diag_water * diag_bone - data_cross * data_cross
    solved = jnp.stack([(diag_bone * right_water - data_cross * right_bone) / determinant, (diag_water * right_bone - data_cross * right_water) / determinant])
    return (1.0 - relaxation) * center + relaxation * solved


def restrict(values):
    extent = values.shape
    blocks = values.reshape(extent[:-2] + (extent[-2] // 2, 2, extent[-1] // 2, 2))
    return blocks.mean(axis=(-3, -1))


def prolong(values):
    return jnp.repeat(jnp.repeat(values, 2, axis=-2), 2, axis=-1)


def pad_zero(estimate):
    widths = [(0, 0)] * (estimate.ndim - 2) + [(1, 1), (1, 1)]
    return jnp.pad(estimate, widths)


def reference(spectra, noise_weights, mixing):
    def one_slice(slice_pair):
        counts, weights = slice_pair
        data_terms, source = material_data(counts.astype(jnp.float32), weights.astype(jnp.float32), mixing)
        level_data = [data_terms]
        level_masks = [edge_masks(0, NX, 0, NY, NX, NY)]
        for level_index in range(1, LEVELS):
            level_data.append(tuple(restrict(member) for member in level_data[-1]))
            level_rows = NX >> level_index
            level_columns = NY >> level_index
            level_masks.append(edge_masks(0, level_rows, 0, level_columns, level_rows, level_columns))

        def solve_level(level_index, estimate, source_term):
            penalty = smoothness / 4.0 ** level_index
            level_terms = level_data[level_index]
            inside = level_masks[level_index]
            if level_index == LEVELS - 1:
                for sweep_index in range(COARSE_SWEEPS):
                    estimate = relax(pad_zero(estimate), source_term, level_terms, penalty, inside)
                return estimate
            estimate = relax(pad_zero(estimate), source_term, level_terms, penalty, inside)
            residual = source_term - apply_operator(pad_zero(estimate), level_terms, penalty, inside)
            coarse_estimate = restrict(estimate)
            coarse_source = restrict(residual) + apply_operator(pad_zero(coarse_estimate), level_data[level_index + 1], smoothness / 4.0 ** (level_index + 1), level_masks[level_index + 1])
            correction = solve_level(level_index + 1, coarse_estimate, coarse_source)
            estimate = estimate + prolong(correction - coarse_estimate)
            return relax(pad_zero(estimate), source_term, level_terms, penalty, inside)

        estimate = jnp.zeros_like(source)
        for cycle_index in range(CYCLES):
            estimate = solve_level(0, estimate, source)
        return estimate

    result = lax.map(one_slice, (jnp.swapaxes(spectra, 0, 1), jnp.swapaxes(noise_weights, 0, 1)))
    return jnp.swapaxes(result, 0, 1)
```

```python
import jax
import jax.numpy as jnp
from jax import lax
from jax.experimental import pallas as pl
from jax.experimental.pallas import tpu as pltpu
from jax.sharding import PartitionSpec as P

LEVELS = 6
COARSE_SWEEPS = 4
JOIN = 3

huber_delta = 0.05
relaxation = 0.8
smoothness = 256.0

LANES = 128
SUB = 8


def penalty_of(level):
    return smoothness / 4.0**level


def lane_of(shape=(SUB, LANES)):
    return lax.broadcasted_iota(jnp.int32, shape, 1)


def row_of(shape=(SUB, LANES)):
    return lax.broadcasted_iota(jnp.int32, shape, 0)


def roll_lanes(x, shift):
    return pltpu.roll(x, shift % LANES, axis=1)


def roll_rows(x, shift):
    return pltpu.roll(x, shift % x.shape[0], axis=0)


def take_lanes(x, index):
    return jnp.take_along_axis(x, index, axis=1)


def from_right(tiles, step=1):
    rolled = [roll_lanes(tile, -step) for tile in tiles]
    if len(tiles) == 1:
        return rolled
    inside = lane_of(tiles[0].shape) < LANES - step
    return [
        jnp.where(inside, rolled[k], rolled[(k + 1) % len(tiles)]) for k in range(len(tiles))
    ]


def from_left(tiles, step=1):
    rolled = [roll_lanes(tile, step) for tile in tiles]
    if len(tiles) == 1:
        return rolled
    inside = lane_of(tiles[0].shape) >= step
    return [jnp.where(inside, rolled[k], rolled[k - 1]) for k in range(len(tiles))]


def flux(gap, with_factor):
    if not with_factor:
        return jnp.clip(gap, -huber_delta, huber_delta), None
    factor = huber_delta / jnp.maximum(jnp.abs(gap), huber_delta)
    return factor * gap, factor


def keep(mask, value):
    return value if mask is None or value is None else jnp.where(mask, value, 0.0)


def row_sums(tiles, masks, with_factor, step=1):
    right = from_right(tiles, step)
    flows, factors = [], []
    for k, tile in enumerate(tiles):
        flow, factor = flux(right[k] - tile, with_factor)
        flows.append(keep(masks[k], flow))
        factors.append(keep(masks[k], factor))
    back = from_left(flows, step)
    flow_sum = [flows[k] - back[k] for k in range(len(tiles))]
    if not with_factor:
        return flow_sum, None
    back = from_left(factors, step)
    return flow_sum, [factors[k] + back[k] for k in range(len(tiles))]


def row_sums_split(tiles, masks, with_factor):
    half = len(tiles) // 2
    even, odd = tiles[:half], tiles[half:]
    after = from_right(even)
    inner = [flux(odd[k] - even[k], with_factor) for k in range(half)]
    outer = [flux(after[k] - odd[k], with_factor) for k in range(half)]
    outer = [tuple(keep(masks[k], part) for part in outer[k]) for k in range(half)]
    back = from_left([part[0] for part in outer])
    flow_sum = [inner[k][0] - back[k] for k in range(half)]
    flow_sum += [outer[k][0] - inner[k][0] for k in range(half)]
    if not with_factor:
        return flow_sum, None
    back = from_left([part[1] for part in outer])
    factor_sum = [inner[k][1] + back[k] for k in range(half)]
    factor_sum += [inner[k][1] + outer[k][1] for k in range(half)]
    return flow_sum, factor_sum


def column_masks(tiles, width, step=1):
    masks = []
    for k in range(tiles):
        place = (lane_of() + k * LANES) % width
        ends = any((k * LANES + n) % width >= width - step for n in range(LANES))
        masks.append(place < width - step if ends else None)
    return masks


class Grid:
    def __init__(self, level, sizes):
        self.level = level
        self.penalty = penalty_of(level)
        self.own = sizes.rows >> level
        self.rows = 3 * self.own
        self.split = level == 0
        self.masks = None
        if level == 0:
            self.groups, self.tiles = sizes.slices, 2 * sizes.tiles
            self.mask_place = (sizes.tiles, sizes.tiles * LANES)
        elif level == 1:
            self.groups, self.tiles = sizes.slices, sizes.tiles
            self.mask_place = (self.tiles, sizes.tiles * LANES)
        else:
            self.groups, self.tiles = 1, sizes.slices * sizes.tiles // 2
            self.mask_place = (self.tiles, sizes.tiles * LANES // 2)

    def shape(self, members):
        return (self.groups, members, self.tiles, self.rows + SUB, LANES)

    def across(self, tiles, with_factor):
        if self.masks is None:
            self.masks = column_masks(*self.mask_place)
        if self.split:
            return row_sums_split(tiles, self.masks, with_factor)
        return row_sums(tiles, self.masks, with_factor)

    def row_mask(self, start, ends):
        mask = None
        for edge, inside in zip((self.own - 1, 2 * self.own - 1), ends):
            if start <= edge < start + SUB:
                part = jnp.logical_or(row_of() != edge - start, inside)
                mask = part if mask is None else jnp.logical_and(mask, part)
        return mask


class Sizes:
    def __init__(self, slices, rows, columns, row_devices, column_devices):
        self.slices = slices
        self.rows = rows
        self.row_devices = row_devices
        self.column_devices = column_devices
        self.columns = columns
        self.tiles = column_devices * columns // (2 * LANES)
        self.join_rows = rows >> JOIN
        self.join_tiles = slices * self.tiles // 2
        self.join_width = self.tiles * LANES >> (JOIN - 1)
        self.grids = [Grid(level, self) for level in range(JOIN)]


def sweep(grid, ends, field, first, last, with_factor, emit):
    strips = range(first, last)
    for group in range(grid.groups):

        def vertical(start, member, tile, center):
            below = field[group, member, tile, pl.ds(start + 1, SUB), :]
            flow, factor = flux(below - center, with_factor)
            mask = grid.row_mask(start, ends)
            return keep(mask, flow), keep(mask, factor)

        carry = {}
        for member in range(2):
            for tile in range(grid.tiles):
                if first > 0:
                    start = (first - 1) * SUB
                    center = field[group, member, tile, pl.ds(start, SUB), :]
                    parts = vertical(start, member, tile, center)
                    carry[member, tile] = [None if x is None else roll_rows(x, 1) for x in parts]
                else:
                    zero = jnp.zeros((SUB, LANES), jnp.float32)
                    carry[member, tile] = [zero, zero]
        top = row_of() == 0
        for strip in strips:
            start = strip * SUB
            centers, flows, factors = [], [], []
            for member in range(2):
                tiles = [
                    field[group, member, tile, pl.ds(start, SUB), :] for tile in range(grid.tiles)
                ]
                flow_sum, factor_sum = grid.across(tiles, with_factor)
                for tile in range(grid.tiles):
                    flow, factor = vertical(start, member, tile, tiles[tile])
                    rolled = roll_rows(flow, 1)
                    above = jnp.where(top, carry[member, tile][0], rolled)
                    flow_sum[tile] = flow_sum[tile] + (flow - above)
                    carry[member, tile][0] = rolled
                    if with_factor:
                        rolled = roll_rows(factor, 1)
                        above = jnp.where(top, carry[member, tile][1], rolled)
                        factor_sum[tile] = factor_sum[tile] + (factor + above)
                        carry[member, tile][1] = rolled
                centers.append(tiles)
                flows.append(flow_sum)
                factors.append(factor_sum)
            emit(group, start, centers, flows, factors)


def solve_pair(water, cross, bone, right_water, right_bone):
    scale = relaxation / (water * bone - cross * cross)
    return (
        scale * (bone * right_water - cross * right_bone),
        scale * (water * right_bone - cross * right_water),
    )


def relax_strips(grid, ends, field, source, data, first, last):
    p = grid.penalty

    def emit(group, start, centers, flows, factors):
        rows = pl.ds(start, SUB)
        for tile in range(grid.tiles):
            water, cross, bone = (data[group, m, tile, rows, :] for m in range(3))
            u, v = centers[0][tile], centers[1][tile]
            right = [
                source[group, 0, tile, rows, :] - (water * u + cross * v) + p * flows[0][tile],
                source[group, 1, tile, rows, :] - (cross * u + bone * v) + p * flows[1][tile],
            ]
            du, dv = solve_pair(
                water + p * factors[0][tile], cross, bone + p * factors[1][tile], *right
            )
            field[group, 0, tile, rows, :] = u + du
            field[group, 1, tile, rows, :] = v + dv

    sweep(grid, ends, field, first, last, True, emit)


def first_relax_strips(grid, ends, field, source, data, first, last):
    p = grid.penalty

    def emit(group, start, centers, flows, factors):
        rows = pl.ds(start, SUB)
        for tile in range(grid.tiles):
            water, cross, bone = (data[group, m, tile, rows, :] for m in range(3))
            u, v = centers[0][tile], centers[1][tile]
            right = [source[group, m, tile, rows, :] for m in range(2)]
            source[group, 0, tile, rows, :] = right[0] + (
                (water * u + cross * v) - p * flows[0][tile]
            )
            source[group, 1, tile, rows, :] = right[1] + (
                (cross * u + bone * v) - p * flows[1][tile]
            )
            du, dv = solve_pair(
                water + p * factors[0][tile], cross, bone + p * factors[1][tile], *right
            )
            field[group, 0, tile, rows, :] = u + du
            field[group, 1, tile, rows, :] = v + dv

    sweep(grid, ends, field, first, last, True, emit)


def residual_strips(grid, ends, field, source, data, out, first, last):
    p = grid.penalty

    def emit(group, start, centers, flows, factors):
        rows = pl.ds(start, SUB)
        rests = [[], []]
        for tile in range(grid.tiles):
            water, cross, bone = (data[group, m, tile, rows, :] for m in range(3))
            u, v = centers[0][tile], centers[1][tile]
            rests[0].append(
                source[group, 0, tile, rows, :] - (water * u + cross * v) + p * flows[0][tile]
            )
            rests[1].append(
                source[group, 1, tile, rows, :] - (cross * u + bone * v) + p * flows[1][tile]
            )
        for member in range(2):
            parts = rests[member]
            if grid.split:
                half = grid.tiles // 2
                parts = [parts[k] + parts[half + k] for k in range(half)]
            for tile, part in enumerate(parts):
                out[group, member, tile, rows, :] = part

    sweep(grid, ends, field, first, last, False, emit)


def pair_rows(ref, group, member, tile, start):
    upper = ref[group, member, tile, pl.ds(2 * start, SUB, stride=2), :]
    lower = ref[group, member, tile, pl.ds(2 * start + 1, SUB, stride=2), :]
    return upper + lower


def merge_pair(first, second):
    index = (2 * lane_of()) % LANES
    halves = [take_lanes(x + roll_lanes(x, -1), index) for x in (first, second)]
    return jnp.where(lane_of() < LANES // 2, halves[0], halves[1])


def split_pair(value):
    index = lane_of() // 2
    return take_lanes(value, index), take_lanes(value, index + LANES // 2)


def restrict_first(grids, ref, out, members, first, last, summed=False):
    coarse = grids[1]
    for group in range(coarse.groups):
        for member in range(members):
            for tile in range(coarse.tiles):
                for strip in range(first, last):
                    start = strip * SUB
                    total = pair_rows(ref, group, member, tile, start)
                    if not summed:
                        total = total + pair_rows(ref, group, member, coarse.tiles + tile, start)
                    for target in out:
                        target[group, member, tile, pl.ds(start, SUB), :] = 0.25 * total


def restrict_second(grids, ref, out, members, first, last):
    fine, coarse = grids[1], grids[2]
    places = [(group, tile) for group in range(fine.groups) for tile in range(fine.tiles)]
    for member in range(members):
        for tile in range(coarse.tiles):
            for strip in range(first, last):
                start = strip * SUB
                pair = [
                    pair_rows(ref, g, member, t, start) for g, t in places[2 * tile : 2 * tile + 2]
                ]
                merged = 0.25 * merge_pair(*pair)
                for target in out:
                    target[0, member, tile, pl.ds(start, SUB), :] = merged


def join_tiles(grids, ref, members):
    grid = grids[2]
    flat = [
        pair_rows(ref, 0, member, tile, grid.own // 2)
        for member in members
        for tile in range(grid.tiles)
    ]
    return [0.25 * merge_pair(flat[2 * k], flat[2 * k + 1]) for k in range(len(flat) // 2)]


def descend(sizes, ends, state, message_fields, message, first_rows):
    grids = sizes.grids
    u, f, d, uc, rest = state
    (a0, z0), (a1, z1) = first_rows
    residual_strips(grids[0], ends, u[0], f[0], d[0], rest[0], a0, z0)
    restrict_first(grids, u[0], (u[1], uc[1]), 2, a1, z1)
    restrict_first(grids, rest[0], (f[1],), 2, a1, z1, summed=True)
    first_relax_strips(grids[1], ends, u[1], f[1], d[1], a1, z1)
    residual_strips(grids[1], ends, u[1], f[1], d[1], rest[1], a1, z1)
    strips = grids[2].rows // SUB
    restrict_second(grids, u[1], (u[2], uc[2]), 2, 0, strips)
    restrict_second(grids, rest[1], (f[2],), 2, 0, strips)
    first_relax_strips(grids[2], ends, u[2], f[2], d[2], 0, strips)
    residual_strips(grids[2], ends, u[2], f[2], d[2], rest[2], 0, strips)
    h = sizes.join_rows
    fields = [join_tiles(grids, u[2], (0, 1)), join_tiles(grids, rest[2], (0, 1))]
    if message_fields == 4:
        fields += [join_tiles(grids, d[2], (0, 2)), join_tiles(grids, d[2], (1, 1))]
    for place, tiles in enumerate(fields):
        for k, tile in enumerate(tiles):
            for target in range(sizes.row_devices):
                message[target, k, pl.ds(place * h, h), :] = tile[:h]


def coarse_correction(sizes, fields):
    tiles = sizes.join_tiles
    rows = sizes.row_devices * sizes.join_rows
    width = sizes.join_width
    shape = (rows, LANES)
    row, lane = row_of(shape), lane_of(shape)

    def partner(values):
        if len(values) == 1:
            return [roll_lanes(values[0], LANES // 2)]
        half = len(values) // 2
        return values[half:] + values[:half]

    def mean(values, step):
        pair = (lane & step) == 0
        right, left = from_right(values, step), from_left(values, step)
        values = [x + jnp.where(pair, r, s) for x, r, s in zip(values, right, left)]
        pair = (row & step) == 0
        return [
            0.25 * (x + jnp.where(pair, roll_rows(x, -step), roll_rows(x, step))) for x in values
        ]

    estimate, rest, diagonal, cross = fields
    diagonals, crosses = [diagonal], [cross]
    for level in range(JOIN + 1, LEVELS):
        step = 1 << (level - JOIN - 1)
        diagonals.append(mean(diagonals[-1], step))
        crosses.append(mean(crosses[-1], step))

    def sums(level, values, with_factor):
        step = 1 << (level - JOIN)
        masks = [(lane + k * LANES) % width < width - step for k in range(tiles)]
        flow_sum, factor_sum = row_sums(values, masks, with_factor, step)
        below = row < rows - step
        for k, value in enumerate(values):
            flow, factor = flux(roll_rows(value, -step) - value, with_factor)
            flow = keep(below, flow)
            flow_sum[k] = flow_sum[k] + (flow - roll_rows(flow, step))
            if with_factor:
                factor = keep(below, factor)
                factor_sum[k] = factor_sum[k] + (factor + roll_rows(factor, step))
        return flow_sum, factor_sum

    def apply(level, values, flow_sum):
        p = penalty_of(level)
        other = partner(values)
        d, x = diagonals[level - JOIN], crosses[level - JOIN]
        return [
            d[k] * values[k] + x[k] * other[k] - p * flow_sum[k] for k in range(tiles)
        ]

    def solve(level, values, factor_sum, right):
        p = penalty_of(level)
        d, x = diagonals[level - JOIN], crosses[level - JOIN]
        h = [d[k] + p * factor_sum[k] for k in range(tiles)]
        h_other, r_other = partner(h), partner(right)
        return [
            values[k]
            + relaxation
            / (h[k] * h_other[k] - x[k] * x[k])
            * (h_other[k] * right[k] - x[k] * r_other[k])
            for k in range(tiles)
        ]

    def relax(level, values, source):
        flow_sum, factor_sum = sums(level, values, True)
        image = apply(level, values, flow_sum)
        return solve(level, values, factor_sum, [a - b for a, b in zip(source, image)])

    def cycle(level, values, rest):
        flow_sum, factor_sum = sums(level, values, True)
        image = apply(level, values, flow_sum)
        source = [a + b for a, b in zip(rest, image)]
        start = values
        values = solve(level, values, factor_sum, rest)
        if level == LEVELS - 1:
            for _ in range(COARSE_SWEEPS - 1):
                values = relax(level, values, source)
        else:
            step = 1 << (level - JOIN)
            image = apply(level, values, sums(level, values, False)[0])
            coarse_rest = mean([a - b for a, b in zip(source, image)], step)
            correction = cycle(level + 1, mean(values, step), coarse_rest)
            values = relax(level, [a + b for a, b in zip(values, correction)], source)
        return [a - b for a, b in zip(values, start)]

    return cycle(JOIN, estimate, rest)


def ascend(sizes, ends, row_index, received, state, scratch, level_rows):
    grids = sizes.grids
    u, f, d, uc = state
    gathered, correction, raised = scratch
    h = sizes.join_rows
    whole = sizes.row_devices * h
    fields = []
    for place, (ref, field) in enumerate(received):
        tiles = []
        for k in range(sizes.join_tiles):
            for source in range(sizes.row_devices):
                gathered[place, k, pl.ds(source * h, h), :] = ref[source, k, pl.ds(field * h, h), :]
            tiles.append(gathered[place, k])
        fields.append(tiles)
    values = coarse_correction(sizes, fields)
    for k in range(sizes.join_tiles):
        correction[k, :SUB, :] = jnp.zeros((SUB, LANES), jnp.float32)
        correction[k, pl.ds(SUB, whole), :] = values[k]
        correction[k, pl.ds(SUB + whole, 2 * SUB), :] = jnp.zeros((2 * SUB, LANES), jnp.float32)

    grid = grids[2]
    strips = grid.rows // SUB
    base = row_index * h + SUB - h
    for k in range(sizes.join_tiles):
        for start in range(0, 3 * h, SUB):
            parts = split_pair(correction[k, pl.ds(base + start, SUB), :])
            for side, part in enumerate(parts):
                member, tile = divmod(2 * k + side, grid.tiles)
                for odd in range(2):
                    raised[2][0, member, tile, pl.ds(2 * start + odd, SUB, stride=2), :] = part
    add_raised(grid, u[2], raised[2], 0, strips)
    relax_strips(grid, ends, u[2], f[2], d[2], 0, strips)

    fine = grids[1]
    places = [(group, tile) for group in range(fine.groups) for tile in range(fine.tiles)]
    for member in range(2):
        for tile in range(grid.tiles):
            for strip in range(strips):
                start = strip * SUB
                rows = pl.ds(start, SUB)
                parts = split_pair(u[2][0, member, tile, rows, :] - uc[2][0, member, tile, rows, :])
                for (g, t), part in zip(places[2 * tile : 2 * tile + 2], parts):
                    for odd in range(2):
                        raised[1][g, member, t, pl.ds(2 * start + odd, SUB, stride=2), :] = part
    (a0, z0), (a1, z1) = level_rows
    add_raised(fine, u[1], raised[1], 0, fine.rows // SUB)
    relax_strips(fine, ends, u[1], f[1], d[1], a1, z1)

    for group in range(fine.groups):
        for member in range(2):
            for tile in range(fine.tiles):
                for strip in range(a1, z1):
                    start = strip * SUB
                    rows = pl.ds(start, SUB)
                    part = u[1][group, member, tile, rows, :] - uc[1][group, member, tile, rows, :]
                    for odd in range(2):
                        raised[0][group, member, tile, pl.ds(2 * start + odd, SUB, stride=2), :] = part
    add_raised(grids[0], u[0], raised[0], 2 * a1, 2 * z1)
    relax_strips(grids[0], ends, u[0], f[0], d[0], a0, z0)


def add_raised(grid, field, raised, first, last):
    period = grid.tiles // 2 if grid.split else grid.tiles
    for group in range(grid.groups):
        for member in range(2):
            for tile in range(grid.tiles):
                for strip in range(first, last):
                    rows = pl.ds(strip * SUB, SUB)
                    field[group, member, tile, rows, :] = (
                        field[group, member, tile, rows, :]
                        + raised[group, member, tile % period, rows, :]
                    )


def zero_margin(grid, ref):
    for group in range(grid.groups):
        for member in range(2):
            for tile in range(grid.tiles):
                ref[group, member, tile, pl.ds(grid.rows, SUB), :] = jnp.zeros(
                    (SUB, LANES), jnp.float32
                )


def domain_ends(sizes):
    row_index = lax.axis_index("gx")
    return row_index, (row_index > 0, row_index < sizes.row_devices - 1)


def start_kernel(sizes, mixing, raw, u0, u1, u2, f0, f1, f2, d0, d1, d2, uc1, uc2, message, *rest):
    grids = sizes.grids
    row_index, ends = domain_ends(sizes)
    for grid, ref in zip(grids, (u0, u1, u2)):
        zero_margin(grid, ref)
    m = [[mixing[i, j] for j in range(2)] for i in range(2)]
    water = [m[0][0] * m[0][0], m[1][0] * m[1][0]]
    cross = [m[0][0] * m[0][1], m[1][0] * m[1][1]]
    bone = [m[0][1] * m[0][1], m[1][1] * m[1][1]]
    odd_device = row_index % 2
    parts = (2 - odd_device, 0, 1 + odd_device)
    beyond = (
        jnp.where(ends[0], 0.0, 1.0),
        None,
        jnp.where(ends[1], 0.0, 1.0),
    )
    grid = grids[0]
    lane, row = lane_of(), row_of()
    low = lane < LANES // 2
    even_first = jnp.where(low, 2 * lane, 2 * lane - LANES + 1)
    odd_first = jnp.where(low, 2 * lane + 1, 2 * lane - LANES)
    half = sizes.tiles
    p = grid.penalty
    for group in range(grid.groups):
        for strip in range(grid.rows // SUB):
            start = strip * SUB
            part, inner = divmod(start, sizes.rows)

            def load(kind, energy, tile):
                plane = (2 * kind + energy) * sizes.slices + group
                pieces = [
                    raw[2 * tile + side, parts[part], plane, pl.ds(inner, SUB), :]
                    for side in range(2)
                ]
                if kind == 1 and beyond[part] is not None:
                    pieces = [piece + beyond[part] for piece in pieces]
                first = take_lanes(pieces[0], even_first)
                second = take_lanes(pieces[1], odd_first)
                return (
                    jnp.where(low, first, second),
                    roll_lanes(jnp.where(low, second, first), LANES // 2),
                )

            vertical = jnp.full((SUB, LANES), 2.0, jnp.float32)
            for edge, inside in zip((grid.own - 1, 2 * grid.own - 1), ends):
                for place in (edge, edge + 1):
                    if start <= place < start + SUB:
                        missing = jnp.logical_and(row == place - start, jnp.logical_not(inside))
                        vertical = jnp.where(missing, vertical - 1.0, vertical)
            for tile in range(half):
                counts = [load(0, energy, tile) for energy in range(2)]
                weights = [load(1, energy, tile) for energy in range(2)]
                for parity in range(2):
                    y = [counts[energy][parity] for energy in range(2)]
                    w = [weights[energy][parity] for energy in range(2)]
                    dw = w[0] * water[0] + w[1] * water[1]
                    dx = w[0] * cross[0] + w[1] * cross[1]
                    db = w[0] * bone[0] + w[1] * bone[1]
                    t = [w[energy] * y[energy] for energy in range(2)]
                    fw = t[0] * m[0][0] + t[1] * m[1][0]
                    fb = t[0] * m[0][1] + t[1] * m[1][1]
                    total = vertical + 2.0
                    if parity == 0 and tile == 0:
                        total = jnp.where(lane == 0, total - 1.0, total)
                    if parity == 1 and tile == half - 1:
                        total = jnp.where(lane == LANES - 1, total - 1.0, total)
                    total = p * total
                    uw, ub = solve_pair(dw + total, dx, db + total, fw, fb)
                    k = parity * half + tile
                    rows = pl.ds(start, SUB)
                    for member, value in enumerate((dw, dx, db)):
                        d0[group, member, k, rows, :] = value
                    for member, value in enumerate((fw, fb)):
                        f0[group, member, k, rows, :] = value
                    for member, value in enumerate((uw, ub)):
                        u0[group, member, k, rows, :] = value
    restrict_first(grids, d0, (d1,), 3, 0, grids[1].rows // SUB)
    restrict_second(grids, d1, (d2,), 3, 0, grids[2].rows // SUB)
    state = ((u0, u1, u2), (f0, f1, f2), (d0, d1, d2), (None, uc1, uc2), rest)
    all_rows = ((0, grids[0].rows // SUB), (0, grids[1].rows // SUB))
    descend(sizes, ends, state, 4, message, all_rows)


def middle_rows(sizes):
    return (
        (sizes.rows // 2 // SUB, 5 * sizes.rows // 2 // SUB),
        (sizes.rows // 4 // SUB, 5 * sizes.rows // 4 // SUB),
    )


def middle_kernel(
    sizes, received, u0i, u1i, u2i, f0, f1i, f2i, d0, d1, d2, uc1i, uc2i,
    u0, u1, u2, f1, f2, uc1, uc2, message,
    gathered, correction, raised0, raised1, raised2, *rest,
):
    grids = sizes.grids
    row_index, ends = domain_ends(sizes)
    for source, target in ((u0i, u0), (u1i, u1), (u2i, u2)):
        target[...] = source[...]
    scratch = (gathered, correction, (raised0, raised1, raised2))
    fields = [(received, k) for k in range(4)]
    span = middle_rows(sizes)
    state = ((u0, u1, u2), (f0, f1i, f2i), (d0, d1, d2), (None, uc1i, uc2i))
    ascend(sizes, ends, row_index, fields, state, scratch, span)
    (a0, z0), _ = span
    relax_strips(grids[0], ends, u0, f0, d0, a0, z0)
    zero_margin(grids[1], u1)
    zero_margin(grids[2], u2)
    state = ((u0, u1, u2), (f0, f1, f2), (d0, d1, d2), (None, uc1, uc2), rest)
    descend(sizes, ends, state, 2, message, span)


def last_kernel(
    sizes, received, first_received, u0, u1, u2, f0, f1, f2, d0, d1, d2, uc1, uc2,
    out,
    v0, v1, v2, gathered, correction, raised0, raised1, raised2,
):
    grids = sizes.grids
    row_index, ends = domain_ends(sizes)
    for source, target in ((u0, v0), (u1, v1), (u2, v2)):
        target[...] = source[...]
    scratch = (gathered, correction, (raised0, raised1, raised2))
    fields = [(received, 0), (received, 1), (first_received, 2), (first_received, 3)]
    own = (sizes.rows // SUB, 2 * sizes.rows // SUB)
    span = (own, middle_rows(sizes)[1])
    state = ((v0, v1, v2), (f0, f1, f2), (d0, d1, d2), (None, uc1, uc2))
    ascend(sizes, ends, row_index, fields, state, scratch, span)
    column_index = lax.axis_index("gy")
    lane = lane_of()
    tile = column_index // 2
    index = (column_index % 2) * (LANES // 2) + lane // 2
    even = lane % 2 == 0
    for group in range(grids[0].groups):
        for member in range(2):
            for strip in range(*own):
                rows = pl.ds(strip * SUB, SUB)
                first = v0[group, member, tile, rows, :]
                second = v0[group, member, tile + sizes.tiles, rows, :]
                out[member, group, pl.ds(strip * SUB - sizes.rows, SUB), :] = jnp.where(
                    even, take_lanes(first, index), take_lanes(second, index)
                )


def shaped(shape):
    return jax.ShapeDtypeStruct(shape, jnp.float32)


def local(spectra, noise_weights, mixing):
    row_devices, column_devices = lax.axis_size("gx"), lax.axis_size("gy")
    _, slices, rows, columns = spectra.shape
    extents = (slices, rows, columns, row_devices, column_devices)
    sizes = Sizes(*extents)
    grids = sizes.grids
    flat = (2 * slices, rows, columns)
    raw = jnp.concatenate(
        [
            spectra.astype(jnp.float32).reshape(flat),
            noise_weights.astype(jnp.float32).reshape(flat),
        ]
    )
    near, far = [], []
    for i in range(row_devices - 1):
        (far if i % 2 else near).extend([(i, i + 1), (i + 1, i)])
    beside = [lax.ppermute(raw, "gx", far), lax.ppermute(raw, "gx", near)][::-1]
    whole = lax.all_gather(jnp.stack([raw] + beside), "gy")

    def vmem(shape):
        return pltpu.VMEM(shape, jnp.float32)

    def message_shape(fields):
        return (row_devices, sizes.join_tiles, fields * sizes.join_rows, LANES)

    fields = [grid.shape(2) for grid in grids]
    datas = [grid.shape(3) for grid in grids]

    def halved(shape):
        return shape[:2] + (shape[2] // 2,) + shape[3:]

    rests = [vmem(halved(fields[0])), vmem(fields[1]), vmem(fields[2])]
    join_whole = row_devices * sizes.join_rows
    coarse = [
        vmem((4, sizes.join_tiles, join_whole, LANES)),
        vmem((sizes.join_tiles, join_whole + 3 * SUB, LANES)),
        vmem(halved(fields[0])),
        vmem(fields[1]),
        vmem(fields[2]),
    ]

    def call(body, outs, scratch, in_specs=None):
        kernel = lambda *refs: body(Sizes(*extents), *refs)
        extra = {} if in_specs is None else {"in_specs": in_specs}
        return pl.pallas_call(
            kernel,
            out_shape=[shaped(shape) for shape in outs],
            scratch_shapes=scratch,
            name=body.__name__,
            **extra,
        )

    outs = fields + fields + datas + fields[1:] + [message_shape(4)]
    specs = [pl.BlockSpec(memory_space=pltpu.SMEM), pl.BlockSpec(memory_space=pltpu.VMEM)]
    u0, u1, u2, f0, f1, f2, d0, d1, d2, uc1, uc2, message = call(
        start_kernel, outs, rests, specs
    )(mixing, whole)
    first_received = lax.all_to_all(message, "gx", 0, 0, tiled=True)
    outs = fields + fields[1:] + fields[1:] + [message_shape(2)]
    u0, u1, u2, f1, f2, uc1, uc2, message = call(middle_kernel, outs, coarse + rests)(
        first_received, u0, u1, u2, f0, f1, f2, d0, d1, d2, uc1, uc2
    )
    received = lax.all_to_all(message, "gx", 0, 0, tiled=True)
    outs = [(2, slices, rows, columns)]
    return call(last_kernel, outs, [vmem(shape) for shape in fields] + coarse)(
        received, first_received, u0, u1, u2, f0, f1, f2, d0, d1, d2, uc1, uc2
    )[0]


def solution(mesh):
    return jax.shard_map(
        local,
        mesh=mesh,
        in_specs=(P(None, None, "gx", "gy"), P(None, None, "gx", "gy"), P()),
        out_specs=P(None, None, "gx", "gy"),
        check_vma=False,
    )
```

```python
import jax
import jax.numpy as jnp
from jax import lax
from jax.experimental import pallas as pl
from jax.experimental.pallas import tpu as pltpu
from jax.sharding import PartitionSpec as P

LEVELS = 6
COARSE_SWEEPS = 4
JOIN = 3

huber_delta = 0.05
relaxation = 0.8
smoothness = 256.0

LANES = 128
SUB = 8


def penalty_of(level):
    return smoothness / 4.0**level


def lane_of(shape=(SUB, LANES)):
    return lax.broadcasted_iota(jnp.int32, shape, 1)


def row_of(shape=(SUB, LANES)):
    return lax.broadcasted_iota(jnp.int32, shape, 0)


def roll_lanes(x, shift):
    return pltpu.roll(x, shift % LANES, axis=1)


def roll_rows(x, shift):
    return pltpu.roll(x, shift % x.shape[0], axis=0)


def take_lanes(x, index):
    return jnp.take_along_axis(x, index, axis=1)


def from_right(tiles, step=1):
    rolled = [roll_lanes(tile, -step) for tile in tiles]
    if len(tiles) == 1:
        return rolled
    inside = lane_of(tiles[0].shape) < LANES - step
    return [
        jnp.where(inside, rolled[k], rolled[(k + 1) % len(tiles)]) for k in range(len(tiles))
    ]


def from_left(tiles, step=1):
    rolled = [roll_lanes(tile, step) for tile in tiles]
    if len(tiles) == 1:
        return rolled
    inside = lane_of(tiles[0].shape) >= step
    return [jnp.where(inside, rolled[k], rolled[k - 1]) for k in range(len(tiles))]


def flux(gap, with_factor):
    if not with_factor:
        return jnp.clip(gap, -huber_delta, huber_delta), None
    factor = huber_delta / jnp.maximum(jnp.abs(gap), huber_delta)
    return factor * gap, factor


def keep(mask, value):
    return value if mask is None or value is None else jnp.where(mask, value, 0.0)


def row_sums(tiles, masks, with_factor, step=1):
    right = from_right(tiles, step)
    flows, factors = [], []
    for k, tile in enumerate(tiles):
        flow, factor = flux(right[k] - tile, with_factor)
        flows.append(keep(masks[k], flow))
        factors.append(keep(masks[k], factor))
    back = from_left(flows, step)
    flow_sum = [flows[k] - back[k] for k in range(len(tiles))]
    if not with_factor:
        return flow_sum, None
    back = from_left(factors, step)
    return flow_sum, [factors[k] + back[k] for k in range(len(tiles))]


def row_sums_split(tiles, masks, with_factor):
    half = len(tiles) // 2
    even, odd = tiles[:half], tiles[half:]
    after = from_right(even)
    inner = [flux(odd[k] - even[k], with_factor) for k in range(half)]
    outer = [flux(after[k] - odd[k], with_factor) for k in range(half)]
    outer = [tuple(keep(masks[k], part) for part in outer[k]) for k in range(half)]
    back = from_left([part[0] for part in outer])
    flow_sum = [inner[k][0] - back[k] for k in range(half)]
    flow_sum += [outer[k][0] - inner[k][0] for k in range(half)]
    if not with_factor:
        return flow_sum, None
    back = from_left([part[1] for part in outer])
    factor_sum = [inner[k][1] + back[k] for k in range(half)]
    factor_sum += [inner[k][1] + outer[k][1] for k in range(half)]
    return flow_sum, factor_sum


def column_masks(tiles, width, step=1):
    masks = []
    for k in range(tiles):
        place = (lane_of() + k * LANES) % width
        ends = any((k * LANES + n) % width >= width - step for n in range(LANES))
        masks.append(place < width - step if ends else None)
    return masks


class Grid:
    def __init__(self, level, sizes):
        self.level = level
        self.penalty = penalty_of(level)
        self.own = sizes.rows >> level
        self.rows = 3 * self.own
        self.split = level == 0
        self.masks = None
        if level == 0:
            self.groups, self.tiles = sizes.slices, 2 * sizes.tiles
            self.mask_place = (sizes.tiles, sizes.tiles * LANES)
        elif level == 1:
            self.groups, self.tiles = sizes.slices, sizes.tiles
            self.mask_place = (self.tiles, sizes.tiles * LANES)
        else:
            self.groups, self.tiles = 1, sizes.slices * sizes.tiles // 2
            self.mask_place = (self.tiles, sizes.tiles * LANES // 2)

    def shape(self, members):
        return (self.groups, members, self.tiles, self.rows + SUB, LANES)

    def across(self, tiles, with_factor):
        if self.masks is None:
            self.masks = column_masks(*self.mask_place)
        if self.split:
            return row_sums_split(tiles, self.masks, with_factor)
        return row_sums(tiles, self.masks, with_factor)

    def row_mask(self, start, ends):
        mask = None
        for edge, inside in zip((self.own - 1, 2 * self.own - 1), ends):
            if start <= edge < start + SUB:
                part = jnp.logical_or(row_of() != edge - start, inside)
                mask = part if mask is None else jnp.logical_and(mask, part)
        return mask


class Sizes:
    def __init__(self, slices, rows, columns, row_devices, column_devices):
        self.slices = slices
        self.rows = rows
        self.row_devices = row_devices
        self.column_devices = column_devices
        self.columns = columns
        self.tiles = column_devices * columns // (2 * LANES)
        self.join_rows = rows >> JOIN
        self.join_tiles = slices * self.tiles // 2
        self.join_width = self.tiles * LANES >> (JOIN - 1)
        self.grids = [Grid(level, self) for level in range(JOIN)]


def sweep(grid, ends, field, first, last, with_factor, emit):
    strips = range(first, last)
    for group in range(grid.groups):

        def vertical(start, member, tile, center):
            below = field[group, member, tile, pl.ds(start + 1, SUB), :]
            flow, factor = flux(below - center, with_factor)
            mask = grid.row_mask(start, ends)
            return keep(mask, flow), keep(mask, factor)

        carry = {}
        for member in range(2):
            for tile in range(grid.tiles):
                if first > 0:
                    start = (first - 1) * SUB
                    center = field[group, member, tile, pl.ds(start, SUB), :]
                    parts = vertical(start, member, tile, center)
                    carry[member, tile] = [None if x is None else roll_rows(x, 1) for x in parts]
                else:
                    zero = jnp.zeros((SUB, LANES), jnp.float32)
                    carry[member, tile] = [zero, zero]
        top = row_of() == 0
        for strip in strips:
            start = strip * SUB
            centers, flows, factors = [], [], []
            for member in range(2):
                tiles = [
                    field[group, member, tile, pl.ds(start, SUB), :] for tile in range(grid.tiles)
                ]
                flow_sum, factor_sum = grid.across(tiles, with_factor)
                for tile in range(grid.tiles):
                    flow, factor = vertical(start, member, tile, tiles[tile])
                    rolled = roll_rows(flow, 1)
                    above = jnp.where(top, carry[member, tile][0], rolled)
                    flow_sum[tile] = flow_sum[tile] + (flow - above)
                    carry[member, tile][0] = rolled
                    if with_factor:
                        rolled = roll_rows(factor, 1)
                        above = jnp.where(top, carry[member, tile][1], rolled)
                        factor_sum[tile] = factor_sum[tile] + (factor + above)
                        carry[member, tile][1] = rolled
                centers.append(tiles)
                flows.append(flow_sum)
                factors.append(factor_sum)
            emit(group, start, centers, flows, factors)


def solve_pair(water, cross, bone, right_water, right_bone):
    scale = relaxation / (water * bone - cross * cross)
    return (
        scale * (bone * right_water - cross * right_bone),
        scale * (water * right_bone - cross * right_water),
    )


def relax_strips(grid, ends, field, source, data, first, last):
    p = grid.penalty

    def emit(group, start, centers, flows, factors):
        rows = pl.ds(start, SUB)
        for tile in range(grid.tiles):
            water, cross, bone = (data[group, m, tile, rows, :] for m in range(3))
            u, v = centers[0][tile], centers[1][tile]
            right = [
                source[group, 0, tile, rows, :] - (water * u + cross * v) + p * flows[0][tile],
                source[group, 1, tile, rows, :] - (cross * u + bone * v) + p * flows[1][tile],
            ]
            du, dv = solve_pair(
                water + p * factors[0][tile], cross, bone + p * factors[1][tile], *right
            )
            field[group, 0, tile, rows, :] = u + du
            field[group, 1, tile, rows, :] = v + dv

    sweep(grid, ends, field, first, last, True, emit)


def first_relax_strips(grid, ends, field, source, data, first, last):
    p = grid.penalty

    def emit(group, start, centers, flows, factors):
        rows = pl.ds(start, SUB)
        for tile in range(grid.tiles):
            water, cross, bone = (data[group, m, tile, rows, :] for m in range(3))
            u, v = centers[0][tile], centers[1][tile]
            right = [source[group, m, tile, rows, :] for m in range(2)]
            source[group, 0, tile, rows, :] = right[0] + (
                (water * u + cross * v) - p * flows[0][tile]
            )
            source[group, 1, tile, rows, :] = right[1] + (
                (cross * u + bone * v) - p * flows[1][tile]
            )
            du, dv = solve_pair(
                water + p * factors[0][tile], cross, bone + p * factors[1][tile], *right
            )
            field[group, 0, tile, rows, :] = u + du
            field[group, 1, tile, rows, :] = v + dv

    sweep(grid, ends, field, first, last, True, emit)


def residual_strips(grid, ends, field, source, data, out, first, last):
    p = grid.penalty

    def emit(group, start, centers, flows, factors):
        rows = pl.ds(start, SUB)
        rests = [[], []]
        for tile in range(grid.tiles):
            water, cross, bone = (data[group, m, tile, rows, :] for m in range(3))
            u, v = centers[0][tile], centers[1][tile]
            rests[0].append(
                source[group, 0, tile, rows, :] - (water * u + cross * v) + p * flows[0][tile]
            )
            rests[1].append(
                source[group, 1, tile, rows, :] - (cross * u + bone * v) + p * flows[1][tile]
            )
        for member in range(2):
            parts = rests[member]
            if grid.split:
                half = grid.tiles // 2
                parts = [parts[k] + parts[half + k] for k in range(half)]
            for tile, part in enumerate(parts):
                out[group, member, tile, rows, :] = part

    sweep(grid, ends, field, first, last, False, emit)


def pair_rows(ref, group, member, tile, start):
    upper = ref[group, member, tile, pl.ds(2 * start, SUB, stride=2), :]
    lower = ref[group, member, tile, pl.ds(2 * start + 1, SUB, stride=2), :]
    return upper + lower


def merge_pair(first, second):
    index = (2 * lane_of()) % LANES
    halves = [take_lanes(x + roll_lanes(x, -1), index) for x in (first, second)]
    return jnp.where(lane_of() < LANES // 2, halves[0], halves[1])


def split_pair(value):
    index = lane_of() // 2
    return take_lanes(value, index), take_lanes(value, index + LANES // 2)


def restrict_first(grids, ref, out, members, first, last, summed=False):
    coarse = grids[1]
    for group in range(coarse.groups):
        for member in range(members):
            for tile in range(coarse.tiles):
                for strip in range(first, last):
                    start = strip * SUB
                    total = pair_rows(ref, group, member, tile, start)
                    if not summed:
                        total = total + pair_rows(ref, group, member, coarse.tiles + tile, start)
                    for target in out:
                        target[group, member, tile, pl.ds(start, SUB), :] = 0.25 * total


def restrict_second(grids, ref, out, members, first, last):
    fine, coarse = grids[1], grids[2]
    places = [(group, tile) for group in range(fine.groups) for tile in range(fine.tiles)]
    for member in range(members):
        for tile in range(coarse.tiles):
            for strip in range(first, last):
                start = strip * SUB
                pair = [
                    pair_rows(ref, g, member, t, start) for g, t in places[2 * tile : 2 * tile + 2]
                ]
                merged = 0.25 * merge_pair(*pair)
                for target in out:
                    target[0, member, tile, pl.ds(start, SUB), :] = merged


def join_tiles(grids, ref, members):
    grid = grids[2]
    flat = [
        pair_rows(ref, 0, member, tile, grid.own // 2)
        for member in members
        for tile in range(grid.tiles)
    ]
    return [0.25 * merge_pair(flat[2 * k], flat[2 * k + 1]) for k in range(len(flat) // 2)]


def descend(sizes, ends, state, message_fields, message, first_rows):
    grids = sizes.grids
    u, f, d, uc, rest = state
    (a0, z0), (a1, z1) = first_rows
    residual_strips(grids[0], ends, u[0], f[0], d[0], rest[0], a0, z0)
    restrict_first(grids, u[0], (u[1], uc[1]), 2, a1, z1)
    restrict_first(grids, rest[0], (f[1],), 2, a1, z1, summed=True)
    first_relax_strips(grids[1], ends, u[1], f[1], d[1], a1, z1)
    residual_strips(grids[1], ends, u[1], f[1], d[1], rest[1], a1, z1)
    strips = grids[2].rows // SUB
    restrict_second(grids, u[1], (u[2], uc[2]), 2, 0, strips)
    restrict_second(grids, rest[1], (f[2],), 2, 0, strips)
    first_relax_strips(grids[2], ends, u[2], f[2], d[2], 0, strips)
    residual_strips(grids[2], ends, u[2], f[2], d[2], rest[2], 0, strips)
    h = sizes.join_rows
    fields = [join_tiles(grids, u[2], (0, 1)), join_tiles(grids, rest[2], (0, 1))]
    if message_fields == 4:
        fields += [join_tiles(grids, d[2], (0, 2)), join_tiles(grids, d[2], (1, 1))]
    for place, tiles in enumerate(fields):
        for k, tile in enumerate(tiles):
            for target in range(sizes.row_devices):
                message[target, k, pl.ds(place * h, h), :] = tile[:h]


def coarse_correction(sizes, fields):
    tiles = sizes.join_tiles
    rows = sizes.row_devices * sizes.join_rows
    width = sizes.join_width
    shape = (rows, LANES)
    row, lane = row_of(shape), lane_of(shape)

    def partner(values):
        if len(values) == 1:
            return [roll_lanes(values[0], LANES // 2)]
        half = len(values) // 2
        return values[half:] + values[:half]

    def mean(values, step):
        pair = (lane & step) == 0
        right, left = from_right(values, step), from_left(values, step)
        values = [x + jnp.where(pair, r, s) for x, r, s in zip(values, right, left)]
        pair = (row & step) == 0
        return [
            0.25 * (x + jnp.where(pair, roll_rows(x, -step), roll_rows(x, step))) for x in values
        ]

    estimate, rest, diagonal, cross = fields
    diagonals, crosses = [diagonal], [cross]
    for level in range(JOIN + 1, LEVELS):
        step = 1 << (level - JOIN - 1)
        diagonals.append(mean(diagonals[-1], step))
        crosses.append(mean(crosses[-1], step))

    def sums(level, values, with_factor):
        step = 1 << (level - JOIN)
        masks = [(lane + k * LANES) % width < width - step for k in range(tiles)]
        flow_sum, factor_sum = row_sums(values, masks, with_factor, step)
        below = row < rows - step
        for k, value in enumerate(values):
            flow, factor = flux(roll_rows(value, -step) - value, with_factor)
            flow = keep(below, flow)
            flow_sum[k] = flow_sum[k] + (flow - roll_rows(flow, step))
            if with_factor:
                factor = keep(below, factor)
                factor_sum[k] = factor_sum[k] + (factor + roll_rows(factor, step))
        return flow_sum, factor_sum

    def apply(level, values, flow_sum):
        p = penalty_of(level)
        other = partner(values)
        d, x = diagonals[level - JOIN], crosses[level - JOIN]
        return [
            d[k] * values[k] + x[k] * other[k] - p * flow_sum[k] for k in range(tiles)
        ]

    def solve(level, values, factor_sum, right):
        p = penalty_of(level)
        d, x = diagonals[level - JOIN], crosses[level - JOIN]
        h = [d[k] + p * factor_sum[k] for k in range(tiles)]
        h_other, r_other = partner(h), partner(right)
        return [
            values[k]
            + relaxation
            / (h[k] * h_other[k] - x[k] * x[k])
            * (h_other[k] * right[k] - x[k] * r_other[k])
            for k in range(tiles)
        ]

    def relax(level, values, source):
        flow_sum, factor_sum = sums(level, values, True)
        image = apply(level, values, flow_sum)
        return solve(level, values, factor_sum, [a - b for a, b in zip(source, image)])

    def cycle(level, values, rest):
        flow_sum, factor_sum = sums(level, values, True)
        image = apply(level, values, flow_sum)
        source = [a + b for a, b in zip(rest, image)]
        start = values
        values = solve(level, values, factor_sum, rest)
        if level == LEVELS - 1:
            for _ in range(COARSE_SWEEPS - 1):
                values = relax(level, values, source)
        else:
            step = 1 << (level - JOIN)
            image = apply(level, values, sums(level, values, False)[0])
            coarse_rest = mean([a - b for a, b in zip(source, image)], step)
            correction = cycle(level + 1, mean(values, step), coarse_rest)
            values = relax(level, [a + b for a, b in zip(values, correction)], source)
        return [a - b for a, b in zip(values, start)]

    return cycle(JOIN, estimate, rest)


def ascend(sizes, ends, row_index, received, state, scratch, level_rows):
    grids = sizes.grids
    u, f, d, uc = state
    gathered, correction, raised = scratch
    h = sizes.join_rows
    whole = sizes.row_devices * h
    fields = []
    for place, (ref, field) in enumerate(received):
        tiles = []
        for k in range(sizes.join_tiles):
            for source in range(sizes.row_devices):
                gathered[place, k, pl.ds(source * h, h), :] = ref[source, k, pl.ds(field * h, h), :]
            tiles.append(gathered[place, k])
        fields.append(tiles)
    values = coarse_correction(sizes, fields)
    for k in range(sizes.join_tiles):
        correction[k, :SUB, :] = jnp.zeros((SUB, LANES), jnp.float32)
        correction[k, pl.ds(SUB, whole), :] = values[k]
        correction[k, pl.ds(SUB + whole, 2 * SUB), :] = jnp.zeros((2 * SUB, LANES), jnp.float32)

    grid = grids[2]
    strips = grid.rows // SUB
    base = row_index * h + SUB - h
    for k in range(sizes.join_tiles):
        for start in range(0, 3 * h, SUB):
            parts = split_pair(correction[k, pl.ds(base + start, SUB), :])
            for side, part in enumerate(parts):
                member, tile = divmod(2 * k + side, grid.tiles)
                for odd in range(2):
                    raised[2][0, member, tile, pl.ds(2 * start + odd, SUB, stride=2), :] = part
    add_raised(grid, u[2], raised[2], 0, strips)
    relax_strips(grid, ends, u[2], f[2], d[2], 0, strips)

    fine = grids[1]
    places = [(group, tile) for group in range(fine.groups) for tile in range(fine.tiles)]
    for member in range(2):
        for tile in range(grid.tiles):
            for strip in range(strips):
                start = strip * SUB
                rows = pl.ds(start, SUB)
                parts = split_pair(u[2][0, member, tile, rows, :] - uc[2][0, member, tile, rows, :])
                for (g, t), part in zip(places[2 * tile : 2 * tile + 2], parts):
                    for odd in range(2):
                        raised[1][g, member, t, pl.ds(2 * start + odd, SUB, stride=2), :] = part
    (a0, z0), (a1, z1) = level_rows
    add_raised(fine, u[1], raised[1], 0, fine.rows // SUB)
    relax_strips(fine, ends, u[1], f[1], d[1], a1, z1)

    for group in range(fine.groups):
        for member in range(2):
            for tile in range(fine.tiles):
                for strip in range(a1, z1):
                    start = strip * SUB
                    rows = pl.ds(start, SUB)
                    part = u[1][group, member, tile, rows, :] - uc[1][group, member, tile, rows, :]
                    for odd in range(2):
                        raised[0][group, member, tile, pl.ds(2 * start + odd, SUB, stride=2), :] = part
    add_raised(grids[0], u[0], raised[0], 2 * a1, 2 * z1)
    relax_strips(grids[0], ends, u[0], f[0], d[0], a0, z0)


def add_raised(grid, field, raised, first, last):
    period = grid.tiles // 2 if grid.split else grid.tiles
    for group in range(grid.groups):
        for member in range(2):
            for tile in range(grid.tiles):
                for strip in range(first, last):
                    rows = pl.ds(strip * SUB, SUB)
                    field[group, member, tile, rows, :] = (
                        field[group, member, tile, rows, :]
                        + raised[group, member, tile % period, rows, :]
                    )


def zero_margin(grid, ref):
    for group in range(grid.groups):
        for member in range(2):
            for tile in range(grid.tiles):
                ref[group, member, tile, pl.ds(grid.rows, SUB), :] = jnp.zeros(
                    (SUB, LANES), jnp.float32
                )


def domain_ends(sizes):
    row_index = lax.axis_index("gx")
    return row_index, (row_index > 0, row_index < sizes.row_devices - 1)


def start_kernel(sizes, mixing, raw, u0, u1, u2, f0, f1, f2, d0, d1, d2, uc1, uc2, message, *rest):
    grids = sizes.grids
    row_index, ends = domain_ends(sizes)
    for grid, ref in zip(grids, (u0, u1, u2)):
        zero_margin(grid, ref)
    m = [[mixing[2 * i + j] for j in range(2)] for i in range(2)]
    water = [m[0][0] * m[0][0], m[1][0] * m[1][0]]
    cross = [m[0][0] * m[0][1], m[1][0] * m[1][1]]
    bone = [m[0][1] * m[0][1], m[1][1] * m[1][1]]
    odd_device = row_index % 2
    parts = (2 - odd_device, 0, 1 + odd_device)
    beyond = (
        jnp.where(ends[0], 0.0, 1.0),
        None,
        jnp.where(ends[1], 0.0, 1.0),
    )
    grid = grids[0]
    lane, row = lane_of(), row_of()
    low = lane < LANES // 2
    even_first = jnp.where(low, 2 * lane, 2 * lane - LANES + 1)
    odd_first = jnp.where(low, 2 * lane + 1, 2 * lane - LANES)
    half = sizes.tiles
    p = grid.penalty
    for group in range(grid.groups):
        for strip in range(grid.rows // SUB):
            start = strip * SUB
            part, inner = divmod(start, sizes.rows)

            def load(kind, energy, tile):
                plane = (2 * kind + energy) * sizes.slices + group
                pieces = [
                    raw[2 * tile + side, parts[part], plane, pl.ds(inner, SUB), :]
                    for side in range(2)
                ]
                if kind == 1 and beyond[part] is not None:
                    pieces = [piece + beyond[part] for piece in pieces]
                first = take_lanes(pieces[0], even_first)
                second = take_lanes(pieces[1], odd_first)
                return (
                    jnp.where(low, first, second),
                    roll_lanes(jnp.where(low, second, first), LANES // 2),
                )

            vertical = jnp.full((SUB, LANES), 2.0, jnp.float32)
            for edge, inside in zip((grid.own - 1, 2 * grid.own - 1), ends):
                for place in (edge, edge + 1):
                    if start <= place < start + SUB:
                        missing = jnp.logical_and(row == place - start, jnp.logical_not(inside))
                        vertical = jnp.where(missing, vertical - 1.0, vertical)
            for tile in range(half):
                counts = [load(0, energy, tile) for energy in range(2)]
                weights = [load(1, energy, tile) for energy in range(2)]
                for parity in range(2):
                    y = [counts[energy][parity] for energy in range(2)]
                    w = [weights[energy][parity] for energy in range(2)]
                    dw = w[0] * water[0] + w[1] * water[1]
                    dx = w[0] * cross[0] + w[1] * cross[1]
                    db = w[0] * bone[0] + w[1] * bone[1]
                    t = [w[energy] * y[energy] for energy in range(2)]
                    fw = t[0] * m[0][0] + t[1] * m[1][0]
                    fb = t[0] * m[0][1] + t[1] * m[1][1]
                    total = vertical + 2.0
                    if parity == 0 and tile == 0:
                        total = jnp.where(lane == 0, total - 1.0, total)
                    if parity == 1 and tile == half - 1:
                        total = jnp.where(lane == LANES - 1, total - 1.0, total)
                    total = p * total
                    uw, ub = solve_pair(dw + total, dx, db + total, fw, fb)
                    k = parity * half + tile
                    rows = pl.ds(start, SUB)
                    for member, value in enumerate((dw, dx, db)):
                        d0[group, member, k, rows, :] = value
                    for member, value in enumerate((fw, fb)):
                        f0[group, member, k, rows, :] = value
                    for member, value in enumerate((uw, ub)):
                        u0[group, member, k, rows, :] = value
    restrict_first(grids, d0, (d1,), 3, 0, grids[1].rows // SUB)
    restrict_second(grids, d1, (d2,), 3, 0, grids[2].rows // SUB)
    state = ((u0, u1, u2), (f0, f1, f2), (d0, d1, d2), (None, uc1, uc2), rest)
    all_rows = ((0, grids[0].rows // SUB), (0, grids[1].rows // SUB))
    descend(sizes, ends, state, 4, message, all_rows)


def middle_rows(sizes):
    return (
        (sizes.rows // 2 // SUB, 5 * sizes.rows // 2 // SUB),
        (sizes.rows // 4 // SUB, 5 * sizes.rows // 4 // SUB),
    )


def middle_kernel(
    sizes, received, u0i, u1i, u2i, f0, f1i, f2i, d0, d1, d2, uc1i, uc2i,
    u0, u1, u2, f1, f2, uc1, uc2, message,
    gathered, correction, raised0, raised1, raised2, *rest,
):
    grids = sizes.grids
    row_index, ends = domain_ends(sizes)
    for source, target in ((u0i, u0), (u1i, u1), (u2i, u2)):
        target[...] = source[...]
    scratch = (gathered, correction, (raised0, raised1, raised2))
    fields = [(received, k) for k in range(4)]
    span = middle_rows(sizes)
    state = ((u0, u1, u2), (f0, f1i, f2i), (d0, d1, d2), (None, uc1i, uc2i))
    ascend(sizes, ends, row_index, fields, state, scratch, span)
    (a0, z0), _ = span
    relax_strips(grids[0], ends, u0, f0, d0, a0, z0)
    zero_margin(grids[1], u1)
    zero_margin(grids[2], u2)
    state = ((u0, u1, u2), (f0, f1, f2), (d0, d1, d2), (None, uc1, uc2), rest)
    descend(sizes, ends, state, 2, message, span)


def last_kernel(
    sizes, received, first_received, u0, u1, u2, f0, f1, f2, d0, d1, d2, uc1, uc2,
    out,
    v0, v1, v2, gathered, correction, raised0, raised1, raised2,
):
    grids = sizes.grids
    row_index, ends = domain_ends(sizes)
    for source, target in ((u0, v0), (u1, v1), (u2, v2)):
        target[...] = source[...]
    scratch = (gathered, correction, (raised0, raised1, raised2))
    fields = [(received, 0), (received, 1), (first_received, 2), (first_received, 3)]
    own = (sizes.rows // SUB, 2 * sizes.rows // SUB)
    span = (own, middle_rows(sizes)[1])
    state = ((v0, v1, v2), (f0, f1, f2), (d0, d1, d2), (None, uc1, uc2))
    ascend(sizes, ends, row_index, fields, state, scratch, span)
    column_index = lax.axis_index("gy")
    lane = lane_of()
    tile = column_index // 2
    index = (column_index % 2) * (LANES // 2) + lane // 2
    even = lane % 2 == 0
    for group in range(grids[0].groups):
        for member in range(2):
            for strip in range(*own):
                rows = pl.ds(strip * SUB, SUB)
                first = v0[group, member, tile, rows, :]
                second = v0[group, member, tile + sizes.tiles, rows, :]
                out[member, group, pl.ds(strip * SUB - sizes.rows, SUB), :] = jnp.where(
                    even, take_lanes(first, index), take_lanes(second, index)
                )


def shaped(shape):
    return jax.ShapeDtypeStruct(shape, jnp.float32)


def local(spectra, noise_weights, mixing):
    row_devices, column_devices = lax.axis_size("gx"), lax.axis_size("gy")
    _, slices, rows, columns = spectra.shape
    extents = (slices, rows, columns, row_devices, column_devices)
    sizes = Sizes(*extents)
    grids = sizes.grids
    flat = (2 * slices, rows, columns)
    raw = jnp.concatenate(
        [
            spectra.astype(jnp.float32).reshape(flat),
            noise_weights.astype(jnp.float32).reshape(flat),
        ]
    )
    near, far = [], []
    for i in range(row_devices - 1):
        (far if i % 2 else near).extend([(i, i + 1), (i + 1, i)])
    beside = [lax.ppermute(raw, "gx", far), lax.ppermute(raw, "gx", near)][::-1]
    whole = lax.all_gather(jnp.stack([raw] + beside), "gy")

    def vmem(shape):
        return pltpu.VMEM(shape, jnp.float32)

    def message_shape(fields):
        return (row_devices, sizes.join_tiles, fields * sizes.join_rows, LANES)

    fields = [grid.shape(2) for grid in grids]
    datas = [grid.shape(3) for grid in grids]

    def halved(shape):
        return shape[:2] + (shape[2] // 2,) + shape[3:]

    rests = [vmem(halved(fields[0])), vmem(fields[1]), vmem(fields[2])]
    join_whole = row_devices * sizes.join_rows
    coarse = [
        vmem((4, sizes.join_tiles, join_whole, LANES)),
        vmem((sizes.join_tiles, join_whole + 3 * SUB, LANES)),
        vmem(halved(fields[0])),
        vmem(fields[1]),
        vmem(fields[2]),
    ]

    vmem_limit = min(16 * max(1, sizes.tiles), 60) << 20

    def call(body, outs, scratch):
        kernel = lambda *refs: body(Sizes(*extents), *refs)
        return pl.pallas_call(
            kernel,
            out_shape=[shaped(shape) for shape in outs],
            scratch_shapes=scratch,
            name=body.__name__,
            compiler_params=pltpu.CompilerParams(vmem_limit_bytes=vmem_limit),
        )

    outs = fields + fields + datas + fields[1:] + [message_shape(4)]
    spread = jnp.broadcast_to(mixing.reshape(-1, 1, 1), (mixing.size, SUB, LANES))
    u0, u1, u2, f0, f1, f2, d0, d1, d2, uc1, uc2, message = call(
        start_kernel, outs, rests
    )(spread, whole)
    first_received = lax.all_to_all(message, "gx", 0, 0, tiled=True)
    outs = fields + fields[1:] + fields[1:] + [message_shape(2)]
    u0, u1, u2, f1, f2, uc1, uc2, message = call(middle_kernel, outs, coarse + rests)(
        first_received, u0, u1, u2, f0, f1, f2, d0, d1, d2, uc1, uc2
    )
    received = lax.all_to_all(message, "gx", 0, 0, tiled=True)
    outs = [(2, slices, rows, columns)]
    return call(last_kernel, outs, [vmem(shape) for shape in fields] + coarse)(
        received, first_received, u0, u1, u2, f0, f1, f2, d0, d1, d2, uc1, uc2
    )[0]


def solution(mesh):
    return jax.shard_map(
        local,
        mesh=mesh,
        in_specs=(P(None, None, "gx", "gy"), P(None, None, "gx", "gy"), P()),
        out_specs=P(None, None, "gx", "gy"),
        check_vma=False,
    )
```

```python
import jax
import jax.numpy as jnp
from jax import lax
from jax.experimental import pallas as pl
from jax.experimental.pallas import tpu as pltpu
from jax.sharding import PartitionSpec as P

LEVELS = 6
COARSE_SWEEPS = 4
JOIN = 3

huber_delta = 0.05
relaxation = 0.8
smoothness = 256.0

LANES = 128
SUB = 8


def penalty_of(level):
    return smoothness / 4.0**level


def lane_of(shape=(SUB, LANES)):
    return lax.broadcasted_iota(jnp.int32, shape, 1)


def row_of(shape=(SUB, LANES)):
    return lax.broadcasted_iota(jnp.int32, shape, 0)


def roll_lanes(x, shift):
    return pltpu.roll(x, shift % LANES, axis=1)


def roll_rows(x, shift):
    return pltpu.roll(x, shift % x.shape[0], axis=0)


def take_lanes(x, index):
    return jnp.take_along_axis(x, index, axis=1)


def from_right(tiles, step=1):
    rolled = [roll_lanes(tile, -step) for tile in tiles]
    if len(tiles) == 1:
        return rolled
    inside = lane_of(tiles[0].shape) < LANES - step
    return [
        jnp.where(inside, rolled[k], rolled[(k + 1) % len(tiles)]) for k in range(len(tiles))
    ]


def from_left(tiles, step=1):
    rolled = [roll_lanes(tile, step) for tile in tiles]
    if len(tiles) == 1:
        return rolled
    inside = lane_of(tiles[0].shape) >= step
    return [jnp.where(inside, rolled[k], rolled[k - 1]) for k in range(len(tiles))]


def flux(gap, with_factor):
    if not with_factor:
        return jnp.clip(gap, -huber_delta, huber_delta), None
    factor = 1.0 / jnp.maximum(jnp.abs(gap), huber_delta)
    return factor * gap, factor


def scaled_penalty(level, with_factor):
    return penalty_of(level) * huber_delta if with_factor else penalty_of(level)


def keep(mask, value):
    return value if mask is None or value is None else jnp.where(mask, value, 0.0)


def row_sums(tiles, masks, with_factor, step=1):
    right = from_right(tiles, step)
    flows, factors = [], []
    for k, tile in enumerate(tiles):
        flow, factor = flux(right[k] - tile, with_factor)
        flows.append(keep(masks[k], flow))
        factors.append(keep(masks[k], factor))
    back = from_left(flows, step)
    flow_sum = [flows[k] - back[k] for k in range(len(tiles))]
    if not with_factor:
        return flow_sum, None
    back = from_left(factors, step)
    return flow_sum, [factors[k] + back[k] for k in range(len(tiles))]


def row_sums_split(tiles, masks, with_factor):
    half = len(tiles) // 2
    even, odd = tiles[:half], tiles[half:]
    after = from_right(even)
    inner = [flux(odd[k] - even[k], with_factor) for k in range(half)]
    outer = [flux(after[k] - odd[k], with_factor) for k in range(half)]
    outer = [tuple(keep(masks[k], part) for part in outer[k]) for k in range(half)]
    back = from_left([part[0] for part in outer])
    flow_sum = [inner[k][0] - back[k] for k in range(half)]
    flow_sum += [outer[k][0] - inner[k][0] for k in range(half)]
    if not with_factor:
        return flow_sum, None
    back = from_left([part[1] for part in outer])
    factor_sum = [inner[k][1] + back[k] for k in range(half)]
    factor_sum += [inner[k][1] + outer[k][1] for k in range(half)]
    return flow_sum, factor_sum


def column_masks(tiles, width, step=1):
    masks = []
    for k in range(tiles):
        place = (lane_of() + k * LANES) % width
        ends = any((k * LANES + n) % width >= width - step for n in range(LANES))
        masks.append(place < width - step if ends else None)
    return masks


class Grid:
    def __init__(self, level, sizes):
        self.level = level
        self.penalty = penalty_of(level)
        self.own = sizes.rows >> level
        self.rows = 3 * self.own
        self.split = level == 0
        self.masks = None
        if level == 0:
            self.groups, self.tiles = sizes.slices, 2 * sizes.tiles
            self.mask_place = (sizes.tiles, sizes.tiles * LANES)
        elif level == 1:
            self.groups, self.tiles = sizes.slices, sizes.tiles
            self.mask_place = (self.tiles, sizes.tiles * LANES)
        else:
            self.groups, self.tiles = 1, sizes.slices * sizes.tiles // 2
            self.mask_place = (self.tiles, sizes.tiles * LANES // 2)

    def shape(self, members):
        return (self.groups, members, self.tiles, self.rows + SUB, LANES)

    def across(self, tiles, with_factor):
        if self.masks is None:
            self.masks = column_masks(*self.mask_place)
        if self.split:
            return row_sums_split(tiles, self.masks, with_factor)
        return row_sums(tiles, self.masks, with_factor)

    def row_mask(self, start, ends):
        mask = None
        for edge, inside in zip((self.own - 1, 2 * self.own - 1), ends):
            if start <= edge < start + SUB:
                part = jnp.logical_or(row_of() != edge - start, inside)
                mask = part if mask is None else jnp.logical_and(mask, part)
        return mask


class Sizes:
    def __init__(self, slices, rows, columns, row_devices, column_devices):
        self.slices = slices
        self.rows = rows
        self.row_devices = row_devices
        self.column_devices = column_devices
        self.columns = columns
        self.tiles = column_devices * columns // (2 * LANES)
        self.join_rows = rows >> JOIN
        self.join_tiles = slices * self.tiles // 2
        self.join_width = self.tiles * LANES >> (JOIN - 1)
        self.grids = [Grid(level, self) for level in range(JOIN)]


def sweep(grid, ends, field, first, last, with_factor, emit):
    strips = range(first, last)
    for group in range(grid.groups):

        def vertical(start, member, tile, center):
            below = field[group, member, tile, pl.ds(start + 1, SUB), :]
            flow, factor = flux(below - center, with_factor)
            mask = grid.row_mask(start, ends)
            return keep(mask, flow), keep(mask, factor)

        carry = {}
        for member in range(2):
            for tile in range(grid.tiles):
                if first > 0:
                    start = (first - 1) * SUB
                    center = field[group, member, tile, pl.ds(start, SUB), :]
                    parts = vertical(start, member, tile, center)
                    carry[member, tile] = [None if x is None else roll_rows(x, 1) for x in parts]
                else:
                    zero = jnp.zeros((SUB, LANES), jnp.float32)
                    carry[member, tile] = [zero, zero]
        top = row_of() == 0
        for strip in strips:
            start = strip * SUB
            centers, flows, factors = [], [], []
            for member in range(2):
                tiles = [
                    field[group, member, tile, pl.ds(start, SUB), :] for tile in range(grid.tiles)
                ]
                flow_sum, factor_sum = grid.across(tiles, with_factor)
                for tile in range(grid.tiles):
                    flow, factor = vertical(start, member, tile, tiles[tile])
                    rolled = roll_rows(flow, 1)
                    above = jnp.where(top, carry[member, tile][0], rolled)
                    flow_sum[tile] = flow_sum[tile] + (flow - above)
                    carry[member, tile][0] = rolled
                    if with_factor:
                        rolled = roll_rows(factor, 1)
                        above = jnp.where(top, carry[member, tile][1], rolled)
                        factor_sum[tile] = factor_sum[tile] + (factor + above)
                        carry[member, tile][1] = rolled
                centers.append(tiles)
                flows.append(flow_sum)
                factors.append(factor_sum)
            emit(group, start, centers, flows, factors)


def solve_pair(water, cross, bone, right_water, right_bone):
    scale = relaxation / (water * bone - cross * cross)
    return (
        scale * (bone * right_water - cross * right_bone),
        scale * (water * right_bone - cross * right_water),
    )


def relax_strips(grid, ends, field, source, data, first, last):
    p = scaled_penalty(grid.level, True)

    def emit(group, start, centers, flows, factors):
        rows = pl.ds(start, SUB)
        for tile in range(grid.tiles):
            water, cross, bone = (data[group, m, tile, rows, :] for m in range(3))
            u, v = centers[0][tile], centers[1][tile]
            right = [
                source[group, 0, tile, rows, :] - (water * u + cross * v) + p * flows[0][tile],
                source[group, 1, tile, rows, :] - (cross * u + bone * v) + p * flows[1][tile],
            ]
            du, dv = solve_pair(
                water + p * factors[0][tile], cross, bone + p * factors[1][tile], *right
            )
            field[group, 0, tile, rows, :] = u + du
            field[group, 1, tile, rows, :] = v + dv

    sweep(grid, ends, field, first, last, True, emit)


def first_relax_strips(grid, ends, field, source, data, first, last):
    p = scaled_penalty(grid.level, True)

    def emit(group, start, centers, flows, factors):
        rows = pl.ds(start, SUB)
        for tile in range(grid.tiles):
            water, cross, bone = (data[group, m, tile, rows, :] for m in range(3))
            u, v = centers[0][tile], centers[1][tile]
            right = [source[group, m, tile, rows, :] for m in range(2)]
            source[group, 0, tile, rows, :] = right[0] + (
                (water * u + cross * v) - p * flows[0][tile]
            )
            source[group, 1, tile, rows, :] = right[1] + (
                (cross * u + bone * v) - p * flows[1][tile]
            )
            du, dv = solve_pair(
                water + p * factors[0][tile], cross, bone + p * factors[1][tile], *right
            )
            field[group, 0, tile, rows, :] = u + du
            field[group, 1, tile, rows, :] = v + dv

    sweep(grid, ends, field, first, last, True, emit)


def residual_strips(grid, ends, field, source, data, out, first, last):
    p = scaled_penalty(grid.level, False)

    def emit(group, start, centers, flows, factors):
        rows = pl.ds(start, SUB)
        rests = [[], []]
        for tile in range(grid.tiles):
            water, cross, bone = (data[group, m, tile, rows, :] for m in range(3))
            u, v = centers[0][tile], centers[1][tile]
            rests[0].append(
                source[group, 0, tile, rows, :] - (water * u + cross * v) + p * flows[0][tile]
            )
            rests[1].append(
                source[group, 1, tile, rows, :] - (cross * u + bone * v) + p * flows[1][tile]
            )
        for member in range(2):
            parts = rests[member]
            if grid.split:
                half = grid.tiles // 2
                parts = [parts[k] + parts[half + k] for k in range(half)]
            for tile, part in enumerate(parts):
                out[group, member, tile, rows, :] = part

    sweep(grid, ends, field, first, last, False, emit)


def pair_rows(ref, group, member, tile, start):
    upper = ref[group, member, tile, pl.ds(2 * start, SUB, stride=2), :]
    lower = ref[group, member, tile, pl.ds(2 * start + 1, SUB, stride=2), :]
    return upper + lower


def merge_pair(first, second):
    index = (2 * lane_of()) % LANES
    halves = [take_lanes(x + roll_lanes(x, -1), index) for x in (first, second)]
    return jnp.where(lane_of() < LANES // 2, halves[0], halves[1])


def split_pair(value):
    index = lane_of() // 2
    return take_lanes(value, index), take_lanes(value, index + LANES // 2)


def restrict_first(grids, ref, out, members, first, last, summed=False):
    coarse = grids[1]
    for group in range(coarse.groups):
        for member in range(members):
            for tile in range(coarse.tiles):
                for strip in range(first, last):
                    start = strip * SUB
                    total = pair_rows(ref, group, member, tile, start)
                    if not summed:
                        total = total + pair_rows(ref, group, member, coarse.tiles + tile, start)
                    for target in out:
                        target[group, member, tile, pl.ds(start, SUB), :] = 0.25 * total


def restrict_second(grids, ref, out, members, first, last):
    fine, coarse = grids[1], grids[2]
    places = [(group, tile) for group in range(fine.groups) for tile in range(fine.tiles)]
    for member in range(members):
        for tile in range(coarse.tiles):
            for strip in range(first, last):
                start = strip * SUB
                pair = [
                    pair_rows(ref, g, member, t, start) for g, t in places[2 * tile : 2 * tile + 2]
                ]
                merged = 0.25 * merge_pair(*pair)
                for target in out:
                    target[0, member, tile, pl.ds(start, SUB), :] = merged


def join_tiles(grids, ref, members):
    grid = grids[2]
    flat = [
        pair_rows(ref, 0, member, tile, grid.own // 2)
        for member in members
        for tile in range(grid.tiles)
    ]
    return [0.25 * merge_pair(flat[2 * k], flat[2 * k + 1]) for k in range(len(flat) // 2)]


def descend(sizes, ends, state, message_fields, message, first_rows):
    grids = sizes.grids
    u, f, d, uc, rest = state
    (a0, z0), (a1, z1) = first_rows
    residual_strips(grids[0], ends, u[0], f[0], d[0], rest[0], a0, z0)
    restrict_first(grids, u[0], (u[1], uc[1]), 2, a1, z1)
    restrict_first(grids, rest[0], (f[1],), 2, a1, z1, summed=True)
    first_relax_strips(grids[1], ends, u[1], f[1], d[1], a1, z1)
    residual_strips(grids[1], ends, u[1], f[1], d[1], rest[1], a1, z1)
    strips = grids[2].rows // SUB
    restrict_second(grids, u[1], (u[2], uc[2]), 2, 0, strips)
    restrict_second(grids, rest[1], (f[2],), 2, 0, strips)
    first_relax_strips(grids[2], ends, u[2], f[2], d[2], 0, strips)
    residual_strips(grids[2], ends, u[2], f[2], d[2], rest[2], 0, strips)
    h = sizes.join_rows
    fields = [join_tiles(grids, u[2], (0, 1)), join_tiles(grids, rest[2], (0, 1))]
    if message_fields == 4:
        fields += [join_tiles(grids, d[2], (0, 2)), join_tiles(grids, d[2], (1, 1))]
    for place, tiles in enumerate(fields):
        for k, tile in enumerate(tiles):
            for target in range(sizes.row_devices):
                message[target, k, pl.ds(place * h, h), :] = tile[:h]


def coarse_correction(sizes, fields):
    tiles = max(1, sizes.join_tiles // 2)
    width = sizes.join_width
    lane, row = lane_of(), row_of()
    low = lane < LANES // 2

    def each(function, *values):
        return [
            [function(*(value[k][v] for value in values)) for v in range(len(values[0][0]))]
            for k in range(tiles)
        ]

    def split(values):
        if sizes.join_tiles > 1:
            return values[:tiles], values[tiles:]
        other = each(lambda x: roll_lanes(x, LANES // 2), values)
        return (
            each(lambda x, y: jnp.where(low, x, y), values, other),
            each(lambda x, y: jnp.where(low, y, x), values, other),
        )

    def join(first, second):
        if sizes.join_tiles > 1:
            return first + second
        return each(lambda x, y: jnp.where(low, x, y), first, second)

    def mean(values, step):
        pair = (lane & step) == 0
        result = [[] for _ in range(tiles)]
        for v in range(0, len(values[0]), 2):
            added = [value[v] + value[v + 1] for value in values]
            right, left = from_right(added, step), from_left(added, step)
            for k in range(tiles):
                result[k].append(0.25 * (added[k] + jnp.where(pair, right[k], left[k])))
        return result

    def add(first, second):
        return each(lambda a, b: a + b, first, second)

    def subtract(first, second):
        return each(lambda a, b: a - b, first, second)

    estimate, rest, diagonal, cross = fields
    matrices = [(*split(diagonal), cross[:tiles])]
    for level in range(JOIN + 1, LEVELS):
        step = 1 << (level - JOIN - 1)
        matrices.append(tuple(mean(part, step) for part in matrices[-1]))

    def sums(level, values, with_factor):
        step = 1 << (level - JOIN)
        count = len(values[0])
        totals = [[[None] * count for _ in range(tiles)] for _ in range(2)]
        for v in range(count):
            line = [value[v] for value in values]
            for shifted, side in ((from_right(line, step), 1), (from_left(line, step), 0)):
                for k in range(tiles):
                    place = (lane + k * LANES) % width
                    inside = place < width - step if side else place >= step
                    for total, part in zip(totals, flux(shifted[k] - line[k], with_factor)):
                        part = keep(inside, part)
                        total[k][v] = part if side or part is None else total[k][v] + part
        for k, value in enumerate(values):
            edges = [
                flux(b - a, with_factor) for a, b in zip(value, value[1:])
            ]
            first = flux(roll_rows(value[-1], 1) - value[0], with_factor)
            last = flux(roll_rows(value[0], -1) - value[-1], with_factor)
            for place in range(2 if with_factor else 1):
                total = totals[place][k]
                for v, edge in enumerate(edges):
                    total[v] = total[v] + edge[place]
                    opposite = edge[place] if place else -edge[place]
                    total[v + 1] = total[v + 1] + opposite
                total[0] = total[0] + keep(row > 0, first[place])
                total[-1] = total[-1] + keep(row < SUB - 1, last[place])
        return totals

    def apply(level, values, flows, with_factor):
        p = scaled_penalty(level, with_factor)
        water, bone, cross = matrices[level - JOIN]
        take = lambda d, x, own, other, flow: d * own + x * other - p * flow
        return (
            each(take, water, cross, values[0], values[1], flows[0]),
            each(take, bone, cross, values[1], values[0], flows[1]),
        )

    def solve(level, values, factors, right):
        p = scaled_penalty(level, True)
        water, bone, cross = matrices[level - JOIN]
        water = each(lambda d, factor: d + p * factor, water, factors[0])
        bone = each(lambda d, factor: d + p * factor, bone, factors[1])
        scale = each(lambda a, b, x: relaxation / (a * b - x * x), water, bone, cross)
        move = lambda own, s, b, x, r, q: own + s * (b * r - x * q)
        return (
            each(move, values[0], scale, bone, cross, right[0], right[1]),
            each(move, values[1], scale, water, cross, right[1], right[0]),
        )

    def both(function, *pairs):
        return tuple(function(*(pair[m] for pair in pairs)) for m in range(2))

    def image_of(level, values, with_factor):
        totals = [sums(level, value, with_factor) for value in values]
        image = apply(level, values, [total[0] for total in totals], with_factor)
        return image, [total[1] for total in totals]

    def relax(level, values, source):
        image, factors = image_of(level, values, True)
        return solve(level, values, factors, both(subtract, source, image))

    def cycle(level, values, rest):
        image, factors = image_of(level, values, True)
        source = both(add, rest, image)
        start = values
        values = solve(level, values, factors, rest)
        if level == LEVELS - 1:
            for _ in range(COARSE_SWEEPS - 1):
                values = relax(level, values, source)
        else:
            step = 1 << (level - JOIN)
            image, _ = image_of(level, values, False)
            coarse_rest = [mean(part, step) for part in both(subtract, source, image)]
            coarse = [mean(part, step) for part in values]
            correction = cycle(level + 1, coarse, coarse_rest)
            raised = [
                [[part[v // 2] for v in range(2 * len(part))] for part in member]
                for member in correction
            ]
            values = relax(level, both(add, values, raised), source)
        return both(subtract, values, start)

    return join(*cycle(JOIN, split(estimate), split(rest)))


def ascend(sizes, ends, row_index, received, state, scratch, level_rows):
    grids = sizes.grids
    u, f, d, uc = state
    correction, raised = scratch
    h = sizes.join_rows
    whole = sizes.row_devices * h
    count = whole // SUB
    fields = []
    for ref, field, total in received:
        block = sizes.join_tiles * total * h
        fields.append(
            [
                [
                    ref[
                        pl.ds(
                            v // h * block + (k * total + field) * h + v % h,
                            SUB,
                            stride=count // h * block,
                        ),
                        :,
                    ]
                    for v in range(count)
                ]
                for k in range(sizes.join_tiles)
            ]
        )
    values = coarse_correction(sizes, fields)
    for k in range(sizes.join_tiles):
        correction[k, :SUB, :] = jnp.zeros((SUB, LANES), jnp.float32)
        correction[k, pl.ds(SUB + whole, 2 * SUB), :] = jnp.zeros((2 * SUB, LANES), jnp.float32)
        for v in range(count):
            correction[k, pl.ds(SUB + v, SUB, stride=count), :] = values[k][v]

    grid = grids[2]
    strips = grid.rows // SUB
    base = row_index * h + SUB - h
    for k in range(sizes.join_tiles):
        for start in range(0, 3 * h, SUB):
            parts = split_pair(correction[k, pl.ds(base + start, SUB), :])
            for side, part in enumerate(parts):
                member, tile = divmod(2 * k + side, grid.tiles)
                for odd in range(2):
                    raised[2][0, member, tile, pl.ds(2 * start + odd, SUB, stride=2), :] = part
    add_raised(grid, u[2], raised[2], 0, strips)
    relax_strips(grid, ends, u[2], f[2], d[2], 0, strips)

    fine = grids[1]
    places = [(group, tile) for group in range(fine.groups) for tile in range(fine.tiles)]
    for member in range(2):
        for tile in range(grid.tiles):
            for strip in range(strips):
                start = strip * SUB
                rows = pl.ds(start, SUB)
                parts = split_pair(u[2][0, member, tile, rows, :] - uc[2][0, member, tile, rows, :])
                for (g, t), part in zip(places[2 * tile : 2 * tile + 2], parts):
                    for odd in range(2):
                        raised[1][g, member, t, pl.ds(2 * start + odd, SUB, stride=2), :] = part
    (a0, z0), (a1, z1) = level_rows
    add_raised(fine, u[1], raised[1], 0, fine.rows // SUB)
    relax_strips(fine, ends, u[1], f[1], d[1], a1, z1)

    for group in range(fine.groups):
        for member in range(2):
            for tile in range(fine.tiles):
                for strip in range(a1, z1):
                    start = strip * SUB
                    rows = pl.ds(start, SUB)
                    part = u[1][group, member, tile, rows, :] - uc[1][group, member, tile, rows, :]
                    for odd in range(2):
                        raised[0][group, member, tile, pl.ds(2 * start + odd, SUB, stride=2), :] = part
    add_raised(grids[0], u[0], raised[0], 2 * a1, 2 * z1)
    relax_strips(grids[0], ends, u[0], f[0], d[0], a0, z0)


def add_raised(grid, field, raised, first, last):
    period = grid.tiles // 2 if grid.split else grid.tiles
    for group in range(grid.groups):
        for member in range(2):
            for tile in range(grid.tiles):
                for strip in range(first, last):
                    rows = pl.ds(strip * SUB, SUB)
                    field[group, member, tile, rows, :] = (
                        field[group, member, tile, rows, :]
                        + raised[group, member, tile % period, rows, :]
                    )


def zero_margin(grid, ref):
    for group in range(grid.groups):
        for member in range(2):
            for tile in range(grid.tiles):
                ref[group, member, tile, pl.ds(grid.rows, SUB), :] = jnp.zeros(
                    (SUB, LANES), jnp.float32
                )


def domain_ends(sizes):
    row_index = lax.axis_index("gx")
    return row_index, (row_index > 0, row_index < sizes.row_devices - 1)


def split_columns(sizes, pieces, swapped, out):
    shape = (2 * LANES, 2 * LANES)
    source, target = row_of(shape), lane_of(shape)
    source = jnp.bitwise_xor(source, swapped * LANES)
    wanted = jnp.where(target < LANES, 2 * target, 2 * (target - LANES) + 1)
    select = (source == wanted).astype(jnp.float32).astype(jnp.bfloat16)
    for tile in range(sizes.tiles):
        for part in range(3):
            sides = [piece[part] for piece in pieces[2 * tile : 2 * tile + 2]]
            sides = [side.reshape(-1, LANES).astype(jnp.bfloat16) for side in sides]
            both = jnp.concatenate(sides, axis=1)
            result = jnp.dot(both, select, preferred_element_type=jnp.float32)
            out[tile, part] = result.reshape(out.shape[2:])


def start_kernel(sizes, mixing, *refs):
    if sizes.column_devices == 2:
        pieces, refs = refs[:2], refs[2:]
        swapped = lax.axis_index("gy")
    else:
        pieces, refs = [refs[0].at[k] for k in range(sizes.column_devices)], refs[1:]
        swapped = 0
    u0, u1, u2, f0, f1, f2, d0, d1, d2, uc1, uc2, message, ordered, *rest = refs
    split_columns(sizes, pieces, swapped, ordered)
    grids = sizes.grids
    row_index, ends = domain_ends(sizes)
    for grid, ref in zip(grids, (u0, u1, u2)):
        zero_margin(grid, ref)
    m = [[mixing[2 * i + j] for j in range(2)] for i in range(2)]
    water = [m[0][0] * m[0][0], m[1][0] * m[1][0]]
    cross = [m[0][0] * m[0][1], m[1][0] * m[1][1]]
    bone = [m[0][1] * m[0][1], m[1][1] * m[1][1]]
    odd_device = row_index % 2
    parts = (2 - odd_device, 0, 1 + odd_device)
    beyond = (
        jnp.where(ends[0], 0.0, 1.0),
        None,
        jnp.where(ends[1], 0.0, 1.0),
    )
    grid = grids[0]
    lane, row = lane_of(), row_of()
    half = sizes.tiles
    p = grid.penalty
    for group in range(grid.groups):
        for strip in range(grid.rows // SUB):
            start = strip * SUB
            part, inner = divmod(start, sizes.rows)

            def load(kind, energy, tile):
                plane = (2 * kind + energy) * sizes.slices + group
                rows = pl.ds(inner, SUB)
                sides = [
                    ordered[tile, parts[part], plane, rows, pl.ds(side * LANES, LANES)]
                    for side in range(2)
                ]
                if kind == 1 and beyond[part] is not None:
                    sides = [side + beyond[part] for side in sides]
                return sides

            vertical = jnp.full((SUB, LANES), 2.0, jnp.float32)
            for edge, inside in zip((grid.own - 1, 2 * grid.own - 1), ends):
                for place in (edge, edge + 1):
                    if start <= place < start + SUB:
                        missing = jnp.logical_and(row == place - start, jnp.logical_not(inside))
                        vertical = jnp.where(missing, vertical - 1.0, vertical)
            for tile in range(half):
                counts = [load(0, energy, tile) for energy in range(2)]
                weights = [load(1, energy, tile) for energy in range(2)]
                for parity in range(2):
                    y = [counts[energy][parity] for energy in range(2)]
                    w = [weights[energy][parity] for energy in range(2)]
                    dw = w[0] * water[0] + w[1] * water[1]
                    dx = w[0] * cross[0] + w[1] * cross[1]
                    db = w[0] * bone[0] + w[1] * bone[1]
                    t = [w[energy] * y[energy] for energy in range(2)]
                    fw = t[0] * m[0][0] + t[1] * m[1][0]
                    fb = t[0] * m[0][1] + t[1] * m[1][1]
                    total = vertical + 2.0
                    if parity == 0 and tile == 0:
                        total = jnp.where(lane == 0, total - 1.0, total)
                    if parity == 1 and tile == half - 1:
                        total = jnp.where(lane == LANES - 1, total - 1.0, total)
                    total = p * total
                    uw, ub = solve_pair(dw + total, dx, db + total, fw, fb)
                    k = parity * half + tile
                    rows = pl.ds(start, SUB)
                    for member, value in enumerate((dw, dx, db)):
                        d0[group, member, k, rows, :] = value
                    for member, value in enumerate((fw, fb)):
                        f0[group, member, k, rows, :] = value
                    for member, value in enumerate((uw, ub)):
                        u0[group, member, k, rows, :] = value
    restrict_first(grids, d0, (d1,), 3, 0, grids[1].rows // SUB)
    restrict_second(grids, d1, (d2,), 3, 0, grids[2].rows // SUB)
    state = ((u0, u1, u2), (f0, f1, f2), (d0, d1, d2), (None, uc1, uc2), rest)
    all_rows = ((0, grids[0].rows // SUB), (0, grids[1].rows // SUB))
    descend(sizes, ends, state, 4, message, all_rows)


def middle_rows(sizes):
    return (
        (sizes.rows // 2 // SUB, 5 * sizes.rows // 2 // SUB),
        (sizes.rows // 4 // SUB, 5 * sizes.rows // 4 // SUB),
    )


def middle_kernel(
    sizes, received, u0i, u1i, u2i, f0, f1i, f2i, d0, d1, d2, uc1i, uc2i,
    u0, u1, u2, f1, f2, uc1, uc2, message,
    correction, raised0, raised1, raised2, *rest,
):
    grids = sizes.grids
    row_index, ends = domain_ends(sizes)
    for source, target in ((u0i, u0), (u1i, u1), (u2i, u2)):
        target[...] = source[...]
    scratch = (correction, (raised0, raised1, raised2))
    fields = [(received, k, 4) for k in range(4)]
    span = middle_rows(sizes)
    state = ((u0, u1, u2), (f0, f1i, f2i), (d0, d1, d2), (None, uc1i, uc2i))
    ascend(sizes, ends, row_index, fields, state, scratch, span)
    (a0, z0), _ = span
    relax_strips(grids[0], ends, u0, f0, d0, a0, z0)
    zero_margin(grids[1], u1)
    zero_margin(grids[2], u2)
    state = ((u0, u1, u2), (f0, f1, f2), (d0, d1, d2), (None, uc1, uc2), rest)
    descend(sizes, ends, state, 2, message, span)


def last_kernel(
    sizes, received, first_received, u0, u1, u2, f0, f1, f2, d0, d1, d2, uc1, uc2,
    out,
    v0, v1, v2, correction, raised0, raised1, raised2,
):
    grids = sizes.grids
    row_index, ends = domain_ends(sizes)
    for source, target in ((u0, v0), (u1, v1), (u2, v2)):
        target[...] = source[...]
    scratch = (correction, (raised0, raised1, raised2))
    fields = [(received, k, 2) for k in range(2)] + [(first_received, k, 4) for k in (2, 3)]
    own = (sizes.rows // SUB, 2 * sizes.rows // SUB)
    span = (own, middle_rows(sizes)[1])
    state = ((v0, v1, v2), (f0, f1, f2), (d0, d1, d2), (None, uc1, uc2))
    ascend(sizes, ends, row_index, fields, state, scratch, span)
    column_index = lax.axis_index("gy")
    lane = lane_of()
    tile = column_index // 2
    index = (column_index % 2) * (LANES // 2) + lane // 2
    even = lane % 2 == 0
    for group in range(grids[0].groups):
        for member in range(2):
            for strip in range(*own):
                rows = pl.ds(strip * SUB, SUB)
                first = v0[group, member, tile, rows, :]
                second = v0[group, member, tile + sizes.tiles, rows, :]
                out[member, group, pl.ds(strip * SUB - sizes.rows, SUB), :] = jnp.where(
                    even, take_lanes(first, index), take_lanes(second, index)
                )


def shaped(shape):
    return jax.ShapeDtypeStruct(shape, jnp.float32)


def local(spectra, noise_weights, mixing):
    row_devices, column_devices = lax.axis_size("gx"), lax.axis_size("gy")
    _, slices, rows, columns = spectra.shape
    extents = (slices, rows, columns, row_devices, column_devices)
    sizes = Sizes(*extents)
    grids = sizes.grids
    flat = (2 * slices, rows, columns)
    raw = jnp.concatenate(
        [
            spectra.astype(jnp.float32).reshape(flat),
            noise_weights.astype(jnp.float32).reshape(flat),
        ]
    )
    near, far = [], []
    for i in range(row_devices - 1):
        (far if i % 2 else near).extend([(i, i + 1), (i + 1, i)])
    beside = [lax.ppermute(raw, "gx", far), lax.ppermute(raw, "gx", near)][::-1]
    tiles = jnp.stack([raw] + beside)
    if column_devices == 2:
        pieces = (tiles, lax.ppermute(tiles, "gy", [(0, 1), (1, 0)]))
    else:
        pieces = (lax.all_gather(tiles, "gy"),)

    def vmem(shape):
        return pltpu.VMEM(shape, jnp.float32)

    def message_shape(fields):
        return (row_devices, sizes.join_tiles, fields * sizes.join_rows, LANES)

    fields = [grid.shape(2) for grid in grids]
    datas = [grid.shape(3) for grid in grids]

    def halved(shape):
        return shape[:2] + (shape[2] // 2,) + shape[3:]

    rests = [vmem(halved(fields[0])), vmem(fields[1]), vmem(fields[2])]
    join_whole = row_devices * sizes.join_rows
    coarse = [
        vmem((sizes.join_tiles, join_whole + 3 * SUB, LANES)),
        vmem(halved(fields[0])),
        vmem(fields[1]),
        vmem(fields[2]),
    ]

    vmem_limit = min(16 * max(1, sizes.tiles), 60) << 20

    def call(body, outs, scratch):
        kernel = lambda *refs: body(Sizes(*extents), *refs)
        return pl.pallas_call(
            kernel,
            out_shape=[shaped(shape) for shape in outs],
            scratch_shapes=scratch,
            name=body.__name__,
            compiler_params=pltpu.CompilerParams(vmem_limit_bytes=vmem_limit),
        )

    outs = fields + fields + datas + fields[1:] + [message_shape(4)]
    spread = jnp.broadcast_to(mixing.reshape(-1, 1, 1), (mixing.size, SUB, LANES))
    u0, u1, u2, f0, f1, f2, d0, d1, d2, uc1, uc2, message = call(
        start_kernel, outs, [vmem((sizes.tiles,) + tiles.shape[:3] + (2 * LANES,))] + rests
    )(spread, *pieces)
    first_received = lax.all_to_all(message, "gx", 0, 0, tiled=True).reshape(-1, LANES)
    outs = fields + fields[1:] + fields[1:] + [message_shape(2)]
    u0, u1, u2, f1, f2, uc1, uc2, message = call(middle_kernel, outs, coarse + rests)(
        first_received, u0, u1, u2, f0, f1, f2, d0, d1, d2, uc1, uc2
    )
    received = lax.all_to_all(message, "gx", 0, 0, tiled=True).reshape(-1, LANES)
    outs = [(2, slices, rows, columns)]
    return call(last_kernel, outs, [vmem(shape) for shape in fields] + coarse)(
        received, first_received, u0, u1, u2, f0, f1, f2, d0, d1, d2, uc1, uc2
    )[0]


def solution(mesh):
    return jax.shard_map(
        local,
        mesh=mesh,
        in_specs=(P(None, None, "gx", "gy"), P(None, None, "gx", "gy"), P()),
        out_specs=P(None, None, "gx", "gy"),
        check_vma=False,
    )
```

```python
import jax
import jax.numpy as jnp
from jax import lax
from jax.experimental import pallas as pl
from jax.experimental.pallas import tpu as pltpu
from jax.sharding import PartitionSpec as P

LEVELS = 6
COARSE_SWEEPS = 4
JOIN = 3

huber_delta = 0.05
relaxation = 0.8
smoothness = 256.0

LANES = 128
SUB = 8


def penalty_of(level):
    return smoothness / 4.0**level


def lane_of(shape=(SUB, LANES)):
    return lax.broadcasted_iota(jnp.int32, shape, 1)


def row_of(shape=(SUB, LANES)):
    return lax.broadcasted_iota(jnp.int32, shape, 0)


def roll_lanes(x, shift):
    return pltpu.roll(x, shift % LANES, axis=1)


def roll_rows(x, shift):
    return pltpu.roll(x, shift % x.shape[0], axis=0)


def take_lanes(x, index):
    return jnp.take_along_axis(x, index, axis=1)


def from_right(tiles, step=1):
    rolled = [roll_lanes(tile, -step) for tile in tiles]
    if len(tiles) == 1:
        return rolled
    inside = lane_of(tiles[0].shape) < LANES - step
    return [
        jnp.where(inside, rolled[k], rolled[(k + 1) % len(tiles)]) for k in range(len(tiles))
    ]


def from_left(tiles, step=1):
    rolled = [roll_lanes(tile, step) for tile in tiles]
    if len(tiles) == 1:
        return rolled
    inside = lane_of(tiles[0].shape) >= step
    return [jnp.where(inside, rolled[k], rolled[k - 1]) for k in range(len(tiles))]


def flux(gap, with_factor):
    if not with_factor:
        return jnp.clip(gap, -huber_delta, huber_delta), None
    factor = 1.0 / jnp.maximum(jnp.abs(gap), huber_delta)
    return factor * gap, factor


def scaled_penalty(level, with_factor):
    return penalty_of(level) * huber_delta if with_factor else penalty_of(level)


def keep(mask, value):
    return value if mask is None or value is None else jnp.where(mask, value, 0.0)


def row_sums(tiles, masks, with_factor, step=1):
    right = from_right(tiles, step)
    flows, factors = [], []
    for k, tile in enumerate(tiles):
        flow, factor = flux(right[k] - tile, with_factor)
        flows.append(keep(masks[k], flow))
        factors.append(keep(masks[k], factor))
    back = from_left(flows, step)
    flow_sum = [flows[k] - back[k] for k in range(len(tiles))]
    if not with_factor:
        return flow_sum, None
    back = from_left(factors, step)
    return flow_sum, [factors[k] + back[k] for k in range(len(tiles))]


def row_sums_split(tiles, masks, with_factor):
    half = len(tiles) // 2
    even, odd = tiles[:half], tiles[half:]
    after = from_right(even)
    inner = [flux(odd[k] - even[k], with_factor) for k in range(half)]
    outer = [flux(after[k] - odd[k], with_factor) for k in range(half)]
    outer = [tuple(keep(masks[k], part) for part in outer[k]) for k in range(half)]
    back = from_left([part[0] for part in outer])
    flow_sum = [inner[k][0] - back[k] for k in range(half)]
    flow_sum += [outer[k][0] - inner[k][0] for k in range(half)]
    if not with_factor:
        return flow_sum, None
    back = from_left([part[1] for part in outer])
    factor_sum = [inner[k][1] + back[k] for k in range(half)]
    factor_sum += [inner[k][1] + outer[k][1] for k in range(half)]
    return flow_sum, factor_sum


def column_masks(tiles, width, step=1):
    masks = []
    for k in range(tiles):
        place = (lane_of() + k * LANES) % width
        ends = any((k * LANES + n) % width >= width - step for n in range(LANES))
        masks.append(place < width - step if ends else None)
    return masks


class Grid:
    def __init__(self, level, sizes):
        self.level = level
        self.penalty = penalty_of(level)
        self.own = sizes.rows >> level
        self.rows = 3 * self.own
        self.split = level == 0
        self.masks = None
        if level == 0:
            self.groups, self.tiles = sizes.slices, 2 * sizes.tiles
            self.mask_place = (sizes.tiles, sizes.tiles * LANES)
        elif level == 1:
            self.groups, self.tiles = sizes.slices, sizes.tiles
            self.mask_place = (self.tiles, sizes.tiles * LANES)
        else:
            self.groups, self.tiles = 1, sizes.slices * sizes.tiles // 2
            self.mask_place = (self.tiles, sizes.tiles * LANES // 2)

    def shape(self, members):
        return (self.groups, members, self.tiles, self.rows + SUB, LANES)

    def across(self, tiles, with_factor):
        if self.masks is None:
            self.masks = column_masks(*self.mask_place)
        if self.split:
            return row_sums_split(tiles, self.masks, with_factor)
        return row_sums(tiles, self.masks, with_factor)

    def row_mask(self, start, ends):
        mask = None
        for edge, inside in zip((self.own - 1, 2 * self.own - 1), ends):
            if start <= edge < start + SUB:
                part = jnp.logical_or(row_of() != edge - start, inside)
                mask = part if mask is None else jnp.logical_and(mask, part)
        return mask


class Sizes:
    def __init__(self, slices, rows, columns, row_devices, column_devices):
        self.slices = slices
        self.rows = rows
        self.row_devices = row_devices
        self.column_devices = column_devices
        self.columns = columns
        self.tiles = column_devices * columns // (2 * LANES)
        self.join_rows = rows >> JOIN
        self.join_tiles = slices * self.tiles // 2
        self.join_width = self.tiles * LANES >> (JOIN - 1)
        self.grids = [Grid(level, self) for level in range(JOIN)]


def sweep(grid, ends, field, first, last, with_factor, emit):
    strips = range(first, last)
    for group in range(grid.groups):

        def vertical(start, member, tile, center):
            below = field[group, member, tile, pl.ds(start + 1, SUB), :]
            flow, factor = flux(below - center, with_factor)
            mask = grid.row_mask(start, ends)
            return keep(mask, flow), keep(mask, factor)

        carry = {}
        for member in range(2):
            for tile in range(grid.tiles):
                if first > 0:
                    start = (first - 1) * SUB
                    center = field[group, member, tile, pl.ds(start, SUB), :]
                    parts = vertical(start, member, tile, center)
                    carry[member, tile] = [None if x is None else roll_rows(x, 1) for x in parts]
                else:
                    zero = jnp.zeros((SUB, LANES), jnp.float32)
                    carry[member, tile] = [zero, zero]
        top = row_of() == 0
        for strip in strips:
            start = strip * SUB
            centers, flows, factors = [], [], []
            for member in range(2):
                tiles = [
                    field[group, member, tile, pl.ds(start, SUB), :] for tile in range(grid.tiles)
                ]
                flow_sum, factor_sum = grid.across(tiles, with_factor)
                for tile in range(grid.tiles):
                    flow, factor = vertical(start, member, tile, tiles[tile])
                    rolled = roll_rows(flow, 1)
                    above = jnp.where(top, carry[member, tile][0], rolled)
                    flow_sum[tile] = flow_sum[tile] + (flow - above)
                    carry[member, tile][0] = rolled
                    if with_factor:
                        rolled = roll_rows(factor, 1)
                        above = jnp.where(top, carry[member, tile][1], rolled)
                        factor_sum[tile] = factor_sum[tile] + (factor + above)
                        carry[member, tile][1] = rolled
                centers.append(tiles)
                flows.append(flow_sum)
                factors.append(factor_sum)
            emit(group, start, centers, flows, factors)


def solve_pair(water, cross, bone, right_water, right_bone):
    scale = relaxation / (water * bone - cross * cross)
    return (
        scale * (bone * right_water - cross * right_bone),
        scale * (water * right_bone - cross * right_water),
    )


def relax_strips(grid, ends, field, source, data, first, last):
    p = scaled_penalty(grid.level, True)

    def emit(group, start, centers, flows, factors):
        rows = pl.ds(start, SUB)
        for tile in range(grid.tiles):
            water, cross, bone = (data[group, m, tile, rows, :] for m in range(3))
            u, v = centers[0][tile], centers[1][tile]
            right = [
                source[group, 0, tile, rows, :] - (water * u + cross * v) + p * flows[0][tile],
                source[group, 1, tile, rows, :] - (cross * u + bone * v) + p * flows[1][tile],
            ]
            du, dv = solve_pair(
                water + p * factors[0][tile], cross, bone + p * factors[1][tile], *right
            )
            field[group, 0, tile, rows, :] = u + du
            field[group, 1, tile, rows, :] = v + dv

    sweep(grid, ends, field, first, last, True, emit)


def first_relax_strips(grid, ends, field, source, data, first, last):
    p = scaled_penalty(grid.level, True)

    def emit(group, start, centers, flows, factors):
        rows = pl.ds(start, SUB)
        for tile in range(grid.tiles):
            water, cross, bone = (data[group, m, tile, rows, :] for m in range(3))
            u, v = centers[0][tile], centers[1][tile]
            right = [source[group, m, tile, rows, :] for m in range(2)]
            source[group, 0, tile, rows, :] = right[0] + (
                (water * u + cross * v) - p * flows[0][tile]
            )
            source[group, 1, tile, rows, :] = right[1] + (
                (cross * u + bone * v) - p * flows[1][tile]
            )
            du, dv = solve_pair(
                water + p * factors[0][tile], cross, bone + p * factors[1][tile], *right
            )
            field[group, 0, tile, rows, :] = u + du
            field[group, 1, tile, rows, :] = v + dv

    sweep(grid, ends, field, first, last, True, emit)


def residual_strips(grid, ends, field, source, data, out, first, last):
    p = scaled_penalty(grid.level, False)

    def emit(group, start, centers, flows, factors):
        rows = pl.ds(start, SUB)
        rests = [[], []]
        for tile in range(grid.tiles):
            water, cross, bone = (data[group, m, tile, rows, :] for m in range(3))
            u, v = centers[0][tile], centers[1][tile]
            rests[0].append(
                source[group, 0, tile, rows, :] - (water * u + cross * v) + p * flows[0][tile]
            )
            rests[1].append(
                source[group, 1, tile, rows, :] - (cross * u + bone * v) + p * flows[1][tile]
            )
        for member in range(2):
            parts = rests[member]
            if grid.split:
                half = grid.tiles // 2
                parts = [parts[k] + parts[half + k] for k in range(half)]
            for tile, part in enumerate(parts):
                out[group, member, tile, rows, :] = part

    sweep(grid, ends, field, first, last, False, emit)


def pair_rows(ref, group, member, tile, start):
    upper = ref[group, member, tile, pl.ds(2 * start, SUB, stride=2), :]
    lower = ref[group, member, tile, pl.ds(2 * start + 1, SUB, stride=2), :]
    return upper + lower


def merge_pair(first, second):
    index = (2 * lane_of()) % LANES
    halves = [take_lanes(x + roll_lanes(x, -1), index) for x in (first, second)]
    return jnp.where(lane_of() < LANES // 2, halves[0], halves[1])


def split_pair(value):
    index = lane_of() // 2
    return take_lanes(value, index), take_lanes(value, index + LANES // 2)


def restrict_first(grids, ref, out, members, first, last, summed=False):
    coarse = grids[1]
    for group in range(coarse.groups):
        for member in range(members):
            for tile in range(coarse.tiles):
                for strip in range(first, last):
                    start = strip * SUB
                    total = pair_rows(ref, group, member, tile, start)
                    if not summed:
                        total = total + pair_rows(ref, group, member, coarse.tiles + tile, start)
                    for target in out:
                        target[group, member, tile, pl.ds(start, SUB), :] = 0.25 * total


def restrict_second(grids, ref, out, members, first, last):
    fine, coarse = grids[1], grids[2]
    places = [(group, tile) for group in range(fine.groups) for tile in range(fine.tiles)]
    for member in range(members):
        for tile in range(coarse.tiles):
            for strip in range(first, last):
                start = strip * SUB
                pair = [
                    pair_rows(ref, g, member, t, start) for g, t in places[2 * tile : 2 * tile + 2]
                ]
                merged = 0.25 * merge_pair(*pair)
                for target in out:
                    target[0, member, tile, pl.ds(start, SUB), :] = merged


def join_tiles(grids, ref, members):
    grid = grids[2]
    flat = [
        pair_rows(ref, 0, member, tile, grid.own // 2)
        for member in members
        for tile in range(grid.tiles)
    ]
    return [0.25 * merge_pair(flat[2 * k], flat[2 * k + 1]) for k in range(len(flat) // 2)]


def descend(sizes, ends, state, message_fields, message, first_rows):
    grids = sizes.grids
    u, f, d, uc, (*rest, outgoing) = state
    (a0, z0), (a1, z1) = first_rows
    residual_strips(grids[0], ends, u[0], f[0], d[0], rest[0], a0, z0)
    restrict_first(grids, u[0], (u[1], uc[1]), 2, a1, z1)
    restrict_first(grids, rest[0], (f[1],), 2, a1, z1, summed=True)
    first_relax_strips(grids[1], ends, u[1], f[1], d[1], a1, z1)
    residual_strips(grids[1], ends, u[1], f[1], d[1], rest[1], a1, z1)
    strips = grids[2].rows // SUB
    restrict_second(grids, u[1], (u[2], uc[2]), 2, 0, strips)
    restrict_second(grids, rest[1], (f[2],), 2, 0, strips)
    first_relax_strips(grids[2], ends, u[2], f[2], d[2], 0, strips)
    residual_strips(grids[2], ends, u[2], f[2], d[2], rest[2], 0, strips)
    h = sizes.join_rows
    fields = [join_tiles(grids, u[2], (0, 1)), join_tiles(grids, rest[2], (0, 1))]
    if message_fields == 4:
        fields += [join_tiles(grids, d[2], (0, 2)), join_tiles(grids, d[2], (1, 1))]
    for place, tiles in enumerate(fields):
        for k, tile in enumerate(tiles):
            outgoing[pl.ds((k * message_fields + place) * h, h), :] = tile[:h]
    targets, share, _ = message.shape
    part = outgoing[pl.ds(lax.axis_index("gy") * share, share), :]
    for target in range(targets):
        message[target] = part


def coarse_correction(sizes, fields):
    tiles = max(1, sizes.join_tiles // 2)
    width = sizes.join_width
    lane, row = lane_of(), row_of()
    low = lane < LANES // 2

    def each(function, *values):
        return [
            [function(*(value[k][v] for value in values)) for v in range(len(values[0][0]))]
            for k in range(tiles)
        ]

    def split(values):
        if sizes.join_tiles > 1:
            return values[:tiles], values[tiles:]
        other = each(lambda x: roll_lanes(x, LANES // 2), values)
        return (
            each(lambda x, y: jnp.where(low, x, y), values, other),
            each(lambda x, y: jnp.where(low, y, x), values, other),
        )

    def join(first, second):
        if sizes.join_tiles > 1:
            return first + second
        return each(lambda x, y: jnp.where(low, x, y), first, second)

    def mean(values, step):
        pair = (lane & step) == 0
        result = [[] for _ in range(tiles)]
        for v in range(0, len(values[0]), 2):
            added = [value[v] + value[v + 1] for value in values]
            right, left = from_right(added, step), from_left(added, step)
            for k in range(tiles):
                result[k].append(0.25 * (added[k] + jnp.where(pair, right[k], left[k])))
        return result

    def add(first, second):
        return each(lambda a, b: a + b, first, second)

    def subtract(first, second):
        return each(lambda a, b: a - b, first, second)

    estimate, rest, diagonal, cross = fields
    matrices = [(*split(diagonal), cross[:tiles])]
    for level in range(JOIN + 1, LEVELS):
        step = 1 << (level - JOIN - 1)
        matrices.append(tuple(mean(part, step) for part in matrices[-1]))

    def sums(level, values, with_factor):
        step = 1 << (level - JOIN)
        count = len(values[0])
        totals = [[[None] * count for _ in range(tiles)] for _ in range(2)]
        for v in range(count):
            line = [value[v] for value in values]
            for shifted, side in ((from_right(line, step), 1), (from_left(line, step), 0)):
                for k in range(tiles):
                    place = (lane + k * LANES) % width
                    inside = place < width - step if side else place >= step
                    for total, part in zip(totals, flux(shifted[k] - line[k], with_factor)):
                        part = keep(inside, part)
                        total[k][v] = part if side or part is None else total[k][v] + part
        for k, value in enumerate(values):
            edges = [
                flux(b - a, with_factor) for a, b in zip(value, value[1:])
            ]
            first = flux(roll_rows(value[-1], 1) - value[0], with_factor)
            last = flux(roll_rows(value[0], -1) - value[-1], with_factor)
            for place in range(2 if with_factor else 1):
                total = totals[place][k]
                for v, edge in enumerate(edges):
                    total[v] = total[v] + edge[place]
                    opposite = edge[place] if place else -edge[place]
                    total[v + 1] = total[v + 1] + opposite
                total[0] = total[0] + keep(row > 0, first[place])
                total[-1] = total[-1] + keep(row < SUB - 1, last[place])
        return totals

    def apply(level, values, flows, with_factor):
        p = scaled_penalty(level, with_factor)
        water, bone, cross = matrices[level - JOIN]
        take = lambda d, x, own, other, flow: d * own + x * other - p * flow
        return (
            each(take, water, cross, values[0], values[1], flows[0]),
            each(take, bone, cross, values[1], values[0], flows[1]),
        )

    def solve(level, values, factors, right):
        p = scaled_penalty(level, True)
        water, bone, cross = matrices[level - JOIN]
        water = each(lambda d, factor: d + p * factor, water, factors[0])
        bone = each(lambda d, factor: d + p * factor, bone, factors[1])
        scale = each(lambda a, b, x: relaxation / (a * b - x * x), water, bone, cross)
        move = lambda own, s, b, x, r, q: own + s * (b * r - x * q)
        return (
            each(move, values[0], scale, bone, cross, right[0], right[1]),
            each(move, values[1], scale, water, cross, right[1], right[0]),
        )

    def both(function, *pairs):
        return tuple(function(*(pair[m] for pair in pairs)) for m in range(2))

    def image_of(level, values, with_factor):
        totals = [sums(level, value, with_factor) for value in values]
        image = apply(level, values, [total[0] for total in totals], with_factor)
        return image, [total[1] for total in totals]

    def relax(level, values, source):
        image, factors = image_of(level, values, True)
        return solve(level, values, factors, both(subtract, source, image))

    def cycle(level, values, rest):
        image, factors = image_of(level, values, True)
        source = both(add, rest, image)
        start = values
        values = solve(level, values, factors, rest)
        if level == LEVELS - 1:
            for _ in range(COARSE_SWEEPS - 1):
                values = relax(level, values, source)
        else:
            step = 1 << (level - JOIN)
            image, _ = image_of(level, values, False)
            coarse_rest = [mean(part, step) for part in both(subtract, source, image)]
            coarse = [mean(part, step) for part in values]
            correction = cycle(level + 1, coarse, coarse_rest)
            raised = [
                [[part[v // 2] for v in range(2 * len(part))] for part in member]
                for member in correction
            ]
            values = relax(level, both(add, values, raised), source)
        return both(subtract, values, start)

    return join(*cycle(JOIN, split(estimate), split(rest)))


def ascend(sizes, ends, row_index, received, state, scratch, level_rows):
    grids = sizes.grids
    u, f, d, uc = state
    correction, raised = scratch
    h = sizes.join_rows
    whole = sizes.row_devices * h
    count = whole // SUB
    fields = []
    for ref, field, total in received:
        block = sizes.join_tiles * total * h
        fields.append(
            [
                [
                    ref[
                        pl.ds(
                            v // h * block + (k * total + field) * h + v % h,
                            SUB,
                            stride=count // h * block,
                        ),
                        :,
                    ]
                    for v in range(count)
                ]
                for k in range(sizes.join_tiles)
            ]
        )
    values = coarse_correction(sizes, fields)
    for k in range(sizes.join_tiles):
        correction[k, :SUB, :] = jnp.zeros((SUB, LANES), jnp.float32)
        correction[k, pl.ds(SUB + whole, 2 * SUB), :] = jnp.zeros((2 * SUB, LANES), jnp.float32)
        for v in range(count):
            correction[k, pl.ds(SUB + v, SUB, stride=count), :] = values[k][v]

    grid = grids[2]
    strips = grid.rows // SUB
    base = row_index * h + SUB - h
    for k in range(sizes.join_tiles):
        for start in range(0, 3 * h, SUB):
            parts = split_pair(correction[k, pl.ds(base + start, SUB), :])
            for side, part in enumerate(parts):
                member, tile = divmod(2 * k + side, grid.tiles)
                for odd in range(2):
                    raised[2][0, member, tile, pl.ds(2 * start + odd, SUB, stride=2), :] = part
    add_raised(grid, u[2], raised[2], 0, strips)
    relax_strips(grid, ends, u[2], f[2], d[2], 0, strips)

    fine = grids[1]
    places = [(group, tile) for group in range(fine.groups) for tile in range(fine.tiles)]
    for member in range(2):
        for tile in range(grid.tiles):
            for strip in range(strips):
                start = strip * SUB
                rows = pl.ds(start, SUB)
                parts = split_pair(u[2][0, member, tile, rows, :] - uc[2][0, member, tile, rows, :])
                for (g, t), part in zip(places[2 * tile : 2 * tile + 2], parts):
                    for odd in range(2):
                        raised[1][g, member, t, pl.ds(2 * start + odd, SUB, stride=2), :] = part
    (a0, z0), (a1, z1) = level_rows
    add_raised(fine, u[1], raised[1], 0, fine.rows // SUB)
    relax_strips(fine, ends, u[1], f[1], d[1], a1, z1)

    for group in range(fine.groups):
        for member in range(2):
            for tile in range(fine.tiles):
                for strip in range(a1, z1):
                    start = strip * SUB
                    rows = pl.ds(start, SUB)
                    part = u[1][group, member, tile, rows, :] - uc[1][group, member, tile, rows, :]
                    for odd in range(2):
                        raised[0][group, member, tile, pl.ds(2 * start + odd, SUB, stride=2), :] = part
    add_raised(grids[0], u[0], raised[0], 2 * a1, 2 * z1)
    relax_strips(grids[0], ends, u[0], f[0], d[0], a0, z0)


def add_raised(grid, field, raised, first, last):
    period = grid.tiles // 2 if grid.split else grid.tiles
    for group in range(grid.groups):
        for member in range(2):
            for tile in range(grid.tiles):
                for strip in range(first, last):
                    rows = pl.ds(strip * SUB, SUB)
                    field[group, member, tile, rows, :] = (
                        field[group, member, tile, rows, :]
                        + raised[group, member, tile % period, rows, :]
                    )


def zero_margin(grid, ref):
    for group in range(grid.groups):
        for member in range(2):
            for tile in range(grid.tiles):
                ref[group, member, tile, pl.ds(grid.rows, SUB), :] = jnp.zeros(
                    (SUB, LANES), jnp.float32
                )


def domain_ends(sizes):
    row_index = lax.axis_index("gx")
    return row_index, (row_index > 0, row_index < sizes.row_devices - 1)


def split_columns(sizes, pieces, swapped, out):
    shape = (2 * LANES, 2 * LANES)
    source, target = row_of(shape), lane_of(shape)
    source = jnp.bitwise_xor(source, swapped * LANES)
    wanted = jnp.where(target < LANES, 2 * target, 2 * (target - LANES) + 1)
    select = (source == wanted).astype(jnp.float32).astype(jnp.bfloat16)
    for tile in range(sizes.tiles):
        for part in range(3):
            sides = [piece[part] for piece in pieces[2 * tile : 2 * tile + 2]]
            sides = [side.reshape(-1, LANES).astype(jnp.bfloat16) for side in sides]
            both = jnp.concatenate(sides, axis=1)
            result = jnp.dot(both, select, preferred_element_type=jnp.float32)
            out[tile, part] = result.reshape(out.shape[2:])


def start_kernel(sizes, mixing, *refs):
    if sizes.column_devices == 2:
        pieces, refs = refs[:2], refs[2:]
        swapped = lax.axis_index("gy")
    else:
        pieces, refs = [refs[0].at[k] for k in range(sizes.column_devices)], refs[1:]
        swapped = 0
    u0, u1, u2, f0, f1, f2, d0, d1, d2, uc1, uc2, message, ordered, *rest = refs
    split_columns(sizes, pieces, swapped, ordered)
    grids = sizes.grids
    row_index, ends = domain_ends(sizes)
    for grid, ref in zip(grids, (u0, u1, u2)):
        zero_margin(grid, ref)
    m = [[mixing[2 * i + j] for j in range(2)] for i in range(2)]
    water = [m[0][0] * m[0][0], m[1][0] * m[1][0]]
    cross = [m[0][0] * m[0][1], m[1][0] * m[1][1]]
    bone = [m[0][1] * m[0][1], m[1][1] * m[1][1]]
    odd_device = row_index % 2
    parts = (2 - odd_device, 0, 1 + odd_device)
    beyond = (
        jnp.where(ends[0], 0.0, 1.0),
        None,
        jnp.where(ends[1], 0.0, 1.0),
    )
    grid = grids[0]
    lane, row = lane_of(), row_of()
    half = sizes.tiles
    p = grid.penalty
    for group in range(grid.groups):
        for strip in range(grid.rows // SUB):
            start = strip * SUB
            part, inner = divmod(start, sizes.rows)

            def load(kind, energy, tile):
                plane = (2 * kind + energy) * sizes.slices + group
                rows = pl.ds(inner, SUB)
                sides = [
                    ordered[tile, parts[part], plane, rows, pl.ds(side * LANES, LANES)]
                    for side in range(2)
                ]
                if kind == 1 and beyond[part] is not None:
                    sides = [side + beyond[part] for side in sides]
                return sides

            vertical = jnp.full((SUB, LANES), 2.0, jnp.float32)
            for edge, inside in zip((grid.own - 1, 2 * grid.own - 1), ends):
                for place in (edge, edge + 1):
                    if start <= place < start + SUB:
                        missing = jnp.logical_and(row == place - start, jnp.logical_not(inside))
                        vertical = jnp.where(missing, vertical - 1.0, vertical)
            for tile in range(half):
                counts = [load(0, energy, tile) for energy in range(2)]
                weights = [load(1, energy, tile) for energy in range(2)]
                for parity in range(2):
                    y = [counts[energy][parity] for energy in range(2)]
                    w = [weights[energy][parity] for energy in range(2)]
                    dw = w[0] * water[0] + w[1] * water[1]
                    dx = w[0] * cross[0] + w[1] * cross[1]
                    db = w[0] * bone[0] + w[1] * bone[1]
                    t = [w[energy] * y[energy] for energy in range(2)]
                    fw = t[0] * m[0][0] + t[1] * m[1][0]
                    fb = t[0] * m[0][1] + t[1] * m[1][1]
                    total = vertical + 2.0
                    if parity == 0 and tile == 0:
                        total = jnp.where(lane == 0, total - 1.0, total)
                    if parity == 1 and tile == half - 1:
                        total = jnp.where(lane == LANES - 1, total - 1.0, total)
                    total = p * total
                    uw, ub = solve_pair(dw + total, dx, db + total, fw, fb)
                    k = parity * half + tile
                    rows = pl.ds(start, SUB)
                    for member, value in enumerate((dw, dx, db)):
                        d0[group, member, k, rows, :] = value
                    for member, value in enumerate((fw, fb)):
                        f0[group, member, k, rows, :] = value
                    for member, value in enumerate((uw, ub)):
                        u0[group, member, k, rows, :] = value
    restrict_first(grids, d0, (d1,), 3, 0, grids[1].rows // SUB)
    restrict_second(grids, d1, (d2,), 3, 0, grids[2].rows // SUB)
    state = ((u0, u1, u2), (f0, f1, f2), (d0, d1, d2), (None, uc1, uc2), rest)
    all_rows = ((0, grids[0].rows // SUB), (0, grids[1].rows // SUB))
    descend(sizes, ends, state, 4, message, all_rows)


def middle_rows(sizes):
    return (
        (sizes.rows // 2 // SUB, 5 * sizes.rows // 2 // SUB),
        (sizes.rows // 4 // SUB, 5 * sizes.rows // 4 // SUB),
    )


def middle_kernel(
    sizes, received, u0i, u1i, u2i, f0, f1i, f2i, d0, d1, d2, uc1i, uc2i,
    u0, u1, u2, f1, f2, uc1, uc2, message,
    correction, raised0, raised1, raised2, *rest,
):
    grids = sizes.grids
    row_index, ends = domain_ends(sizes)
    for source, target in ((u0i, u0), (u1i, u1), (u2i, u2)):
        target[...] = source[...]
    scratch = (correction, (raised0, raised1, raised2))
    fields = [(received, k, 4) for k in range(4)]
    span = middle_rows(sizes)
    state = ((u0, u1, u2), (f0, f1i, f2i), (d0, d1, d2), (None, uc1i, uc2i))
    ascend(sizes, ends, row_index, fields, state, scratch, span)
    (a0, z0), _ = span
    relax_strips(grids[0], ends, u0, f0, d0, a0, z0)
    zero_margin(grids[1], u1)
    zero_margin(grids[2], u2)
    state = ((u0, u1, u2), (f0, f1, f2), (d0, d1, d2), (None, uc1, uc2), rest)
    descend(sizes, ends, state, 2, message, span)


def last_kernel(
    sizes, received, first_received, u0, u1, u2, f0, f1, f2, d0, d1, d2, uc1, uc2,
    out,
    v0, v1, v2, correction, raised0, raised1, raised2,
):
    grids = sizes.grids
    row_index, ends = domain_ends(sizes)
    for source, target in ((u0, v0), (u1, v1), (u2, v2)):
        target[...] = source[...]
    scratch = (correction, (raised0, raised1, raised2))
    fields = [(received, k, 2) for k in range(2)] + [(first_received, k, 4) for k in (2, 3)]
    own = (sizes.rows // SUB, 2 * sizes.rows // SUB)
    span = (own, middle_rows(sizes)[1])
    state = ((v0, v1, v2), (f0, f1, f2), (d0, d1, d2), (None, uc1, uc2))
    ascend(sizes, ends, row_index, fields, state, scratch, span)
    column_index = lax.axis_index("gy")
    lane = lane_of()
    tile = column_index // 2
    index = (column_index % 2) * (LANES // 2) + lane // 2
    even = lane % 2 == 0
    for group in range(grids[0].groups):
        for member in range(2):
            for strip in range(*own):
                rows = pl.ds(strip * SUB, SUB)
                first = v0[group, member, tile, rows, :]
                second = v0[group, member, tile + sizes.tiles, rows, :]
                out[member, group, pl.ds(strip * SUB - sizes.rows, SUB), :] = jnp.where(
                    even, take_lanes(first, index), take_lanes(second, index)
                )


def shaped(shape):
    return jax.ShapeDtypeStruct(shape, jnp.float32)


def local(spectra, noise_weights, mixing):
    row_devices, column_devices = lax.axis_size("gx"), lax.axis_size("gy")
    _, slices, rows, columns = spectra.shape
    extents = (slices, rows, columns, row_devices, column_devices)
    sizes = Sizes(*extents)
    grids = sizes.grids
    flat = (2 * slices, rows, columns)
    raw = jnp.concatenate(
        [
            spectra.astype(jnp.float32).reshape(flat),
            noise_weights.astype(jnp.float32).reshape(flat),
        ]
    )
    near, far = [], []
    for i in range(row_devices - 1):
        (far if i % 2 else near).extend([(i, i + 1), (i + 1, i)])
    beside = [lax.ppermute(raw, "gx", far), lax.ppermute(raw, "gx", near)][::-1]
    tiles = jnp.stack([raw] + beside)
    if column_devices == 2:
        pieces = (tiles, lax.ppermute(tiles, "gy", [(0, 1), (1, 0)]))
    else:
        pieces = (lax.all_gather(tiles, "gy"),)

    def vmem(shape):
        return pltpu.VMEM(shape, jnp.float32)

    def message_shape(fields):
        share = sizes.join_tiles * fields * sizes.join_rows // column_devices
        return (row_devices * column_devices, share, LANES)

    fields = [grid.shape(2) for grid in grids]
    datas = [grid.shape(3) for grid in grids]

    def halved(shape):
        return shape[:2] + (shape[2] // 2,) + shape[3:]

    rests = [vmem(halved(fields[0])), vmem(fields[1]), vmem(fields[2])]
    rests.append(vmem((sizes.join_tiles * 4 * sizes.join_rows, LANES)))
    join_whole = row_devices * sizes.join_rows
    coarse = [
        vmem((sizes.join_tiles, join_whole + 3 * SUB, LANES)),
        vmem(halved(fields[0])),
        vmem(fields[1]),
        vmem(fields[2]),
    ]

    vmem_limit = min(16 * max(1, sizes.tiles), 60) << 20

    def call(body, outs, scratch):
        kernel = lambda *refs: body(Sizes(*extents), *refs)
        return pl.pallas_call(
            kernel,
            out_shape=[shaped(shape) for shape in outs],
            scratch_shapes=scratch,
            name=body.__name__,
            compiler_params=pltpu.CompilerParams(vmem_limit_bytes=vmem_limit),
        )

    outs = fields + fields + datas + fields[1:] + [message_shape(4)]
    spread = jnp.broadcast_to(mixing.reshape(-1, 1, 1), (mixing.size, SUB, LANES))
    u0, u1, u2, f0, f1, f2, d0, d1, d2, uc1, uc2, message = call(
        start_kernel, outs, [vmem((sizes.tiles,) + tiles.shape[:3] + (2 * LANES,))] + rests
    )(spread, *pieces)
    first_received = lax.all_to_all(message, ("gx", "gy"), 0, 0, tiled=True).reshape(-1, LANES)
    outs = fields + fields[1:] + fields[1:] + [message_shape(2)]
    u0, u1, u2, f1, f2, uc1, uc2, message = call(middle_kernel, outs, coarse + rests)(
        first_received, u0, u1, u2, f0, f1, f2, d0, d1, d2, uc1, uc2
    )
    received = lax.all_to_all(message, ("gx", "gy"), 0, 0, tiled=True).reshape(-1, LANES)
    outs = [(2, slices, rows, columns)]
    return call(last_kernel, outs, [vmem(shape) for shape in fields] + coarse)(
        received, first_received, u0, u1, u2, f0, f1, f2, d0, d1, d2, uc1, uc2
    )[0]


def solution(mesh):
    return jax.shard_map(
        local,
        mesh=mesh,
        in_specs=(P(None, None, "gx", "gy"), P(None, None, "gx", "gy"), P()),
        out_specs=P(None, None, "gx", "gy"),
        check_vma=False,
    )
```

```python
import jax
import jax.numpy as jnp
from jax import lax
from jax.experimental import pallas as pl
from jax.experimental.pallas import tpu as pltpu
from jax.sharding import PartitionSpec as P

LEVELS = 6
COARSE_SWEEPS = 4
JOIN = 3

huber_delta = 0.05
relaxation = 0.8
smoothness = 256.0

LANES = 128
SUB = 8


def penalty_of(level):
    return smoothness / 4.0**level


def lane_of(shape=(SUB, LANES)):
    return lax.broadcasted_iota(jnp.int32, shape, 1)


def row_of(shape=(SUB, LANES)):
    return lax.broadcasted_iota(jnp.int32, shape, 0)


def roll_lanes(x, shift):
    return pltpu.roll(x, shift % LANES, axis=1)


def roll_rows(x, shift):
    return pltpu.roll(x, shift % x.shape[0], axis=0)


def take_lanes(x, index):
    return jnp.take_along_axis(x, index, axis=1)


def from_right(tiles, step=1):
    rolled = [roll_lanes(tile, -step) for tile in tiles]
    if len(tiles) == 1:
        return rolled
    inside = lane_of(tiles[0].shape) < LANES - step
    return [
        jnp.where(inside, rolled[k], rolled[(k + 1) % len(tiles)]) for k in range(len(tiles))
    ]


def from_left(tiles, step=1):
    rolled = [roll_lanes(tile, step) for tile in tiles]
    if len(tiles) == 1:
        return rolled
    inside = lane_of(tiles[0].shape) >= step
    return [jnp.where(inside, rolled[k], rolled[k - 1]) for k in range(len(tiles))]


def flux(gap, with_factor):
    if not with_factor:
        return jnp.clip(gap, -huber_delta, huber_delta), None
    factor = 1.0 / jnp.maximum(jnp.abs(gap), huber_delta)
    return factor * gap, factor


def scaled_penalty(level, with_factor):
    return penalty_of(level) * huber_delta if with_factor else penalty_of(level)


def keep(mask, value):
    return value if mask is None or value is None else jnp.where(mask, value, 0.0)


def row_sums(tiles, masks, with_factor, step=1):
    right = from_right(tiles, step)
    flows, factors = [], []
    for k, tile in enumerate(tiles):
        flow, factor = flux(right[k] - tile, with_factor)
        flows.append(keep(masks[k], flow))
        factors.append(keep(masks[k], factor))
    back = from_left(flows, step)
    flow_sum = [flows[k] - back[k] for k in range(len(tiles))]
    if not with_factor:
        return flow_sum, None
    back = from_left(factors, step)
    return flow_sum, [factors[k] + back[k] for k in range(len(tiles))]


def row_sums_split(tiles, masks, with_factor):
    half = len(tiles) // 2
    even, odd = tiles[:half], tiles[half:]
    after = from_right(even)
    inner = [flux(odd[k] - even[k], with_factor) for k in range(half)]
    outer = [flux(after[k] - odd[k], with_factor) for k in range(half)]
    outer = [tuple(keep(masks[k], part) for part in outer[k]) for k in range(half)]
    back = from_left([part[0] for part in outer])
    flow_sum = [inner[k][0] - back[k] for k in range(half)]
    flow_sum += [outer[k][0] - inner[k][0] for k in range(half)]
    if not with_factor:
        return flow_sum, None
    back = from_left([part[1] for part in outer])
    factor_sum = [inner[k][1] + back[k] for k in range(half)]
    factor_sum += [inner[k][1] + outer[k][1] for k in range(half)]
    return flow_sum, factor_sum


def column_masks(tiles, width, step=1):
    masks = []
    for k in range(tiles):
        place = (lane_of() + k * LANES) % width
        ends = any((k * LANES + n) % width >= width - step for n in range(LANES))
        masks.append(place < width - step if ends else None)
    return masks


class Grid:
    def __init__(self, level, sizes):
        self.level = level
        self.penalty = penalty_of(level)
        self.own = sizes.rows >> level
        self.rows = 3 * self.own
        self.split = level == 0
        self.masks = None
        if level == 0:
            self.groups, self.tiles = sizes.slices, 2 * sizes.tiles
            self.mask_place = (sizes.tiles, sizes.tiles * LANES)
        elif level == 1:
            self.groups, self.tiles = sizes.slices, sizes.tiles
            self.mask_place = (self.tiles, sizes.tiles * LANES)
        else:
            self.groups, self.tiles = 1, sizes.slices * sizes.tiles // 2
            self.mask_place = (self.tiles, sizes.tiles * LANES // 2)

    def shape(self, members):
        return (self.groups, members, self.tiles, self.rows + SUB, LANES)

    def across(self, tiles, with_factor):
        if self.masks is None:
            self.masks = column_masks(*self.mask_place)
        if self.split:
            return row_sums_split(tiles, self.masks, with_factor)
        return row_sums(tiles, self.masks, with_factor)

    def row_mask(self, start, ends):
        mask = None
        for edge, inside in zip((self.own - 1, 2 * self.own - 1), ends):
            if start <= edge < start + SUB:
                part = jnp.logical_or(row_of() != edge - start, inside)
                mask = part if mask is None else jnp.logical_and(mask, part)
        return mask


class Sizes:
    def __init__(self, slices, rows, columns, row_devices, column_devices):
        self.slices = slices
        self.rows = rows
        self.row_devices = row_devices
        self.column_devices = column_devices
        self.columns = columns
        self.tiles = column_devices * columns // (2 * LANES)
        self.join_rows = rows >> JOIN
        self.join_tiles = slices * self.tiles // 2
        self.join_width = self.tiles * LANES >> (JOIN - 1)
        self.grids = [Grid(level, self) for level in range(JOIN)]


def sweep(grid, ends, field, first, last, with_factor, emit):
    strips = range(first, last)
    for group in range(grid.groups):

        def vertical(start, member, tile, center):
            below = field[group, member, tile, pl.ds(start + 1, SUB), :]
            flow, factor = flux(below - center, with_factor)
            mask = grid.row_mask(start, ends)
            return keep(mask, flow), keep(mask, factor)

        carry = {}
        for member in range(2):
            for tile in range(grid.tiles):
                if first > 0:
                    start = (first - 1) * SUB
                    center = field[group, member, tile, pl.ds(start, SUB), :]
                    parts = vertical(start, member, tile, center)
                    carry[member, tile] = [None if x is None else roll_rows(x, 1) for x in parts]
                else:
                    zero = jnp.zeros((SUB, LANES), jnp.float32)
                    carry[member, tile] = [zero, zero]
        top = row_of() == 0
        for strip in strips:
            start = strip * SUB
            centers, flows, factors = [], [], []
            for member in range(2):
                tiles = [
                    field[group, member, tile, pl.ds(start, SUB), :] for tile in range(grid.tiles)
                ]
                flow_sum, factor_sum = grid.across(tiles, with_factor)
                for tile in range(grid.tiles):
                    flow, factor = vertical(start, member, tile, tiles[tile])
                    rolled = roll_rows(flow, 1)
                    above = jnp.where(top, carry[member, tile][0], rolled)
                    flow_sum[tile] = flow_sum[tile] + (flow - above)
                    carry[member, tile][0] = rolled
                    if with_factor:
                        rolled = roll_rows(factor, 1)
                        above = jnp.where(top, carry[member, tile][1], rolled)
                        factor_sum[tile] = factor_sum[tile] + (factor + above)
                        carry[member, tile][1] = rolled
                centers.append(tiles)
                flows.append(flow_sum)
                factors.append(factor_sum)
            emit(group, start, centers, flows, factors)


def solve_pair(water, cross, bone, right_water, right_bone):
    scale = relaxation / (water * bone - cross * cross)
    return (
        scale * (bone * right_water - cross * right_bone),
        scale * (water * right_bone - cross * right_water),
    )


def relax_strips(grid, ends, field, source, data, first, last):
    p = scaled_penalty(grid.level, True)

    def emit(group, start, centers, flows, factors):
        rows = pl.ds(start, SUB)
        for tile in range(grid.tiles):
            water, cross, bone = (data[group, m, tile, rows, :] for m in range(3))
            u, v = centers[0][tile], centers[1][tile]
            right = [
                source[group, 0, tile, rows, :] - (water * u + cross * v) + p * flows[0][tile],
                source[group, 1, tile, rows, :] - (cross * u + bone * v) + p * flows[1][tile],
            ]
            du, dv = solve_pair(
                water + p * factors[0][tile], cross, bone + p * factors[1][tile], *right
            )
            field[group, 0, tile, rows, :] = u + du
            field[group, 1, tile, rows, :] = v + dv

    sweep(grid, ends, field, first, last, True, emit)


def first_relax_strips(grid, ends, field, source, data, first, last):
    p = scaled_penalty(grid.level, True)

    def emit(group, start, centers, flows, factors):
        rows = pl.ds(start, SUB)
        for tile in range(grid.tiles):
            water, cross, bone = (data[group, m, tile, rows, :] for m in range(3))
            u, v = centers[0][tile], centers[1][tile]
            right = [source[group, m, tile, rows, :] for m in range(2)]
            source[group, 0, tile, rows, :] = right[0] + (
                (water * u + cross * v) - p * flows[0][tile]
            )
            source[group, 1, tile, rows, :] = right[1] + (
                (cross * u + bone * v) - p * flows[1][tile]
            )
            du, dv = solve_pair(
                water + p * factors[0][tile], cross, bone + p * factors[1][tile], *right
            )
            field[group, 0, tile, rows, :] = u + du
            field[group, 1, tile, rows, :] = v + dv

    sweep(grid, ends, field, first, last, True, emit)


def residual_strips(grid, ends, field, source, data, out, first, last):
    p = scaled_penalty(grid.level, False)

    def emit(group, start, centers, flows, factors):
        rows = pl.ds(start, SUB)
        rests = [[], []]
        for tile in range(grid.tiles):
            water, cross, bone = (data[group, m, tile, rows, :] for m in range(3))
            u, v = centers[0][tile], centers[1][tile]
            rests[0].append(
                source[group, 0, tile, rows, :] - (water * u + cross * v) + p * flows[0][tile]
            )
            rests[1].append(
                source[group, 1, tile, rows, :] - (cross * u + bone * v) + p * flows[1][tile]
            )
        for member in range(2):
            parts = rests[member]
            if grid.split:
                half = grid.tiles // 2
                parts = [parts[k] + parts[half + k] for k in range(half)]
            for tile, part in enumerate(parts):
                out[group, member, tile, rows, :] = part

    sweep(grid, ends, field, first, last, False, emit)


def pair_rows(ref, group, member, tile, start):
    upper = ref[group, member, tile, pl.ds(2 * start, SUB, stride=2), :]
    lower = ref[group, member, tile, pl.ds(2 * start + 1, SUB, stride=2), :]
    return upper + lower


def merge_pair(first, second):
    index = (2 * lane_of()) % LANES
    halves = [take_lanes(x + roll_lanes(x, -1), index) for x in (first, second)]
    return jnp.where(lane_of() < LANES // 2, halves[0], halves[1])


def split_pair(value):
    index = lane_of() // 2
    return take_lanes(value, index), take_lanes(value, index + LANES // 2)


def restrict_first(grids, ref, out, members, first, last, summed=False):
    coarse = grids[1]
    for group in range(coarse.groups):
        for member in range(members):
            for tile in range(coarse.tiles):
                for strip in range(first, last):
                    start = strip * SUB
                    total = pair_rows(ref, group, member, tile, start)
                    if not summed:
                        total = total + pair_rows(ref, group, member, coarse.tiles + tile, start)
                    for target in out:
                        target[group, member, tile, pl.ds(start, SUB), :] = 0.25 * total


def restrict_second(grids, ref, out, members, first, last):
    fine, coarse = grids[1], grids[2]
    places = [(group, tile) for group in range(fine.groups) for tile in range(fine.tiles)]
    for member in range(members):
        for tile in range(coarse.tiles):
            for strip in range(first, last):
                start = strip * SUB
                pair = [
                    pair_rows(ref, g, member, t, start) for g, t in places[2 * tile : 2 * tile + 2]
                ]
                merged = 0.25 * merge_pair(*pair)
                for target in out:
                    target[0, member, tile, pl.ds(start, SUB), :] = merged


def join_tiles(grids, ref, start):
    grid = grids[2]
    flat = [
        pair_rows(ref, 0, member, tile, start) for member in range(2) for tile in range(grid.tiles)
    ]
    return [0.25 * merge_pair(flat[2 * k], flat[2 * k + 1]) for k in range(len(flat) // 2)]


def descend(sizes, ends, state, weights, message, first_rows):
    grids = sizes.grids
    u, f, d, uc, (*rest, outgoing) = state
    (a0, z0), (a1, z1) = first_rows
    residual_strips(grids[0], ends, u[0], f[0], d[0], rest[0], a0, z0)
    restrict_first(grids, u[0], (u[1], uc[1]), 2, a1, z1)
    restrict_first(grids, rest[0], (f[1],), 2, a1, z1, summed=True)
    first_relax_strips(grids[1], ends, u[1], f[1], d[1], a1, z1)
    residual_strips(grids[1], ends, u[1], f[1], d[1], rest[1], a1, z1)
    strips = grids[2].rows // SUB
    restrict_second(grids, u[1], (u[2], uc[2]), 2, 0, strips)
    restrict_second(grids, rest[1], (f[2],), 2, 0, strips)
    first_relax_strips(grids[2], ends, u[2], f[2], d[2], 0, strips)
    residual_strips(grids[2], ends, u[2], f[2], d[2], rest[2], 0, strips)
    h = sizes.join_rows
    fields = [join_tiles(grids, ref, grids[2].own // 2) for ref in (u[2], rest[2])]
    if weights is not None:
        fields.append(weights)
    for place, tiles in enumerate(fields):
        for k, tile in enumerate(tiles):
            outgoing[pl.ds((k * len(fields) + place) * h, h), :] = tile[:h]
    targets, parts, share, _ = message.shape
    base = lax.axis_index("gy") * (parts * share)
    for place in range(parts):
        part = outgoing[pl.ds(base + place * share, share), :]
        for target in range(targets):
            message[target, place] = part


def coarse_correction(sizes, mixing, fields):
    tiles = max(1, sizes.join_tiles // 2)
    width = sizes.join_width
    lane, row = lane_of(), row_of()
    low = lane < LANES // 2

    def each(function, *values):
        return [
            [function(*(value[k][v] for value in values)) for v in range(len(values[0][0]))]
            for k in range(tiles)
        ]

    def split(values):
        if sizes.join_tiles > 1:
            return values[:tiles], values[tiles:]
        other = each(lambda x: roll_lanes(x, LANES // 2), values)
        return (
            each(lambda x, y: jnp.where(low, x, y), values, other),
            each(lambda x, y: jnp.where(low, y, x), values, other),
        )

    def join(first, second):
        if sizes.join_tiles > 1:
            return first + second
        return each(lambda x, y: jnp.where(low, x, y), first, second)

    def mean(values, step):
        pair = (lane & step) == 0
        result = [[] for _ in range(tiles)]
        for v in range(0, len(values[0]), 2):
            added = [value[v] + value[v + 1] for value in values]
            right, left = from_right(added, step), from_left(added, step)
            for k in range(tiles):
                result[k].append(0.25 * (added[k] + jnp.where(pair, right[k], left[k])))
        return result

    def add(first, second):
        return each(lambda a, b: a + b, first, second)

    def subtract(first, second):
        return each(lambda a, b: a - b, first, second)

    estimate, rest, weights = fields
    _, *factors = normal_factors(mixing)
    means = split(weights)
    matrices = []
    for level in range(JOIN, LEVELS):
        if level > JOIN:
            means = [mean(part, 1 << (level - JOIN - 1)) for part in means]
        water, cross, bone = (
            each(lambda a, b, pair=pair: a * pair[0] + b * pair[1], *means) for pair in factors
        )
        matrices.append((water, bone, cross))

    def sums(level, values, with_factor):
        step = 1 << (level - JOIN)
        count = len(values[0])
        totals = [[[None] * count for _ in range(tiles)] for _ in range(2)]
        for v in range(count):
            line = [value[v] for value in values]
            for shifted, side in ((from_right(line, step), 1), (from_left(line, step), 0)):
                for k in range(tiles):
                    place = (lane + k * LANES) % width
                    inside = place < width - step if side else place >= step
                    for total, part in zip(totals, flux(shifted[k] - line[k], with_factor)):
                        part = keep(inside, part)
                        total[k][v] = part if side or part is None else total[k][v] + part
        for k, value in enumerate(values):
            edges = [
                flux(b - a, with_factor) for a, b in zip(value, value[1:])
            ]
            first = flux(roll_rows(value[-1], 1) - value[0], with_factor)
            last = flux(roll_rows(value[0], -1) - value[-1], with_factor)
            for place in range(2 if with_factor else 1):
                total = totals[place][k]
                for v, edge in enumerate(edges):
                    total[v] = total[v] + edge[place]
                    opposite = edge[place] if place else -edge[place]
                    total[v + 1] = total[v + 1] + opposite
                total[0] = total[0] + keep(row > 0, first[place])
                total[-1] = total[-1] + keep(row < SUB - 1, last[place])
        return totals

    def apply(level, values, flows, with_factor):
        p = scaled_penalty(level, with_factor)
        water, bone, cross = matrices[level - JOIN]
        take = lambda d, x, own, other, flow: d * own + x * other - p * flow
        return (
            each(take, water, cross, values[0], values[1], flows[0]),
            each(take, bone, cross, values[1], values[0], flows[1]),
        )

    def solve(level, values, factors, right):
        p = scaled_penalty(level, True)
        water, bone, cross = matrices[level - JOIN]
        water = each(lambda d, factor: d + p * factor, water, factors[0])
        bone = each(lambda d, factor: d + p * factor, bone, factors[1])
        scale = each(lambda a, b, x: relaxation / (a * b - x * x), water, bone, cross)
        move = lambda own, s, b, x, r, q: own + s * (b * r - x * q)
        return (
            each(move, values[0], scale, bone, cross, right[0], right[1]),
            each(move, values[1], scale, water, cross, right[1], right[0]),
        )

    def both(function, *pairs):
        return tuple(function(*(pair[m] for pair in pairs)) for m in range(2))

    def image_of(level, values, with_factor):
        totals = [sums(level, value, with_factor) for value in values]
        image = apply(level, values, [total[0] for total in totals], with_factor)
        return image, [total[1] for total in totals]

    def relax(level, values, source):
        image, factors = image_of(level, values, True)
        return solve(level, values, factors, both(subtract, source, image))

    def cycle(level, values, rest):
        image, factors = image_of(level, values, True)
        source = both(add, rest, image)
        start = values
        values = solve(level, values, factors, rest)
        if level == LEVELS - 1:
            for _ in range(COARSE_SWEEPS - 1):
                values = relax(level, values, source)
        else:
            step = 1 << (level - JOIN)
            image, _ = image_of(level, values, False)
            coarse_rest = [mean(part, step) for part in both(subtract, source, image)]
            coarse = [mean(part, step) for part in values]
            correction = cycle(level + 1, coarse, coarse_rest)
            raised = [
                [[part[v // 2] for v in range(2 * len(part))] for part in member]
                for member in correction
            ]
            values = relax(level, both(add, values, raised), source)
        return both(subtract, values, start)

    return join(*cycle(JOIN, split(estimate), split(rest)))


def ascend(sizes, ends, row_index, mixing, received, state, scratch, level_rows):
    grids = sizes.grids
    u, f, d, uc = state
    correction, raised = scratch
    h = sizes.join_rows
    whole = sizes.row_devices * h
    count = whole // SUB
    fields = []
    for ref, field, total in received:
        block = sizes.join_tiles * total * h
        fields.append(
            [
                [
                    ref[
                        pl.ds(
                            v // h * block + (k * total + field) * h + v % h,
                            SUB,
                            stride=count // h * block,
                        ),
                        :,
                    ]
                    for v in range(count)
                ]
                for k in range(sizes.join_tiles)
            ]
        )
    values = coarse_correction(sizes, mixing, fields)
    for k in range(sizes.join_tiles):
        correction[k, :SUB, :] = jnp.zeros((SUB, LANES), jnp.float32)
        correction[k, pl.ds(SUB + whole, 2 * SUB), :] = jnp.zeros((2 * SUB, LANES), jnp.float32)
        for v in range(count):
            correction[k, pl.ds(SUB + v, SUB, stride=count), :] = values[k][v]

    grid = grids[2]
    strips = grid.rows // SUB
    base = row_index * h + SUB - h
    for k in range(sizes.join_tiles):
        for start in range(0, 3 * h, SUB):
            parts = split_pair(correction[k, pl.ds(base + start, SUB), :])
            for side, part in enumerate(parts):
                member, tile = divmod(2 * k + side, grid.tiles)
                for odd in range(2):
                    raised[2][0, member, tile, pl.ds(2 * start + odd, SUB, stride=2), :] = part
    add_raised(grid, u[2], raised[2], 0, strips)
    relax_strips(grid, ends, u[2], f[2], d[2], 0, strips)

    fine = grids[1]
    places = [(group, tile) for group in range(fine.groups) for tile in range(fine.tiles)]
    for member in range(2):
        for tile in range(grid.tiles):
            for strip in range(strips):
                start = strip * SUB
                rows = pl.ds(start, SUB)
                parts = split_pair(u[2][0, member, tile, rows, :] - uc[2][0, member, tile, rows, :])
                for (g, t), part in zip(places[2 * tile : 2 * tile + 2], parts):
                    for odd in range(2):
                        raised[1][g, member, t, pl.ds(2 * start + odd, SUB, stride=2), :] = part
    (a0, z0), (a1, z1) = level_rows
    add_raised(fine, u[1], raised[1], 0, fine.rows // SUB)
    relax_strips(fine, ends, u[1], f[1], d[1], a1, z1)

    for group in range(fine.groups):
        for member in range(2):
            for tile in range(fine.tiles):
                for strip in range(a1, z1):
                    start = strip * SUB
                    rows = pl.ds(start, SUB)
                    part = u[1][group, member, tile, rows, :] - uc[1][group, member, tile, rows, :]
                    for odd in range(2):
                        raised[0][group, member, tile, pl.ds(2 * start + odd, SUB, stride=2), :] = part
    add_raised(grids[0], u[0], raised[0], 2 * a1, 2 * z1)
    relax_strips(grids[0], ends, u[0], f[0], d[0], a0, z0)


def add_raised(grid, field, raised, first, last):
    period = grid.tiles // 2 if grid.split else grid.tiles
    for group in range(grid.groups):
        for member in range(2):
            for tile in range(grid.tiles):
                for strip in range(first, last):
                    rows = pl.ds(strip * SUB, SUB)
                    field[group, member, tile, rows, :] = (
                        field[group, member, tile, rows, :]
                        + raised[group, member, tile % period, rows, :]
                    )


def zero_margin(grid, ref):
    for group in range(grid.groups):
        for member in range(2):
            for tile in range(grid.tiles):
                ref[group, member, tile, pl.ds(grid.rows, SUB), :] = jnp.zeros(
                    (SUB, LANES), jnp.float32
                )


def domain_ends(sizes):
    row_index = lax.axis_index("gx")
    return row_index, (row_index > 0, row_index < sizes.row_devices - 1)


def normal_factors(mixing):
    m = [[mixing[2 * i + j] for j in range(2)] for i in range(2)]
    water = [m[0][0] * m[0][0], m[1][0] * m[1][0]]
    cross = [m[0][0] * m[0][1], m[1][0] * m[1][1]]
    bone = [m[0][1] * m[0][1], m[1][1] * m[1][1]]
    return m, water, cross, bone


def split_columns(sizes, pieces, swapped, out):
    shape = (2 * LANES, 2 * LANES)
    source, target = row_of(shape), lane_of(shape)
    source = jnp.bitwise_xor(source, swapped * LANES)
    wanted = jnp.where(target < LANES, 2 * target, 2 * (target - LANES) + 1)
    select = (source == wanted).astype(jnp.float32).astype(jnp.bfloat16)
    for tile in range(sizes.tiles):
        for part in range(3):
            sides = [piece[part] for piece in pieces[2 * tile : 2 * tile + 2]]
            sides = [side.reshape(-1, LANES).astype(jnp.bfloat16) for side in sides]
            both = jnp.concatenate(sides, axis=1)
            result = jnp.dot(both, select, preferred_element_type=jnp.float32)
            out[tile, part] = result.reshape(out.shape[2:])


def start_kernel(sizes, mixing, *refs):
    if sizes.column_devices == 2:
        pieces, refs = refs[:2], refs[2:]
        swapped = lax.axis_index("gy")
    else:
        pieces, refs = [refs[0].at[k] for k in range(sizes.column_devices)], refs[1:]
        swapped = 0
    u0, u1, u2, f0, f1, f2, d0, d1, d2, uc1, uc2, message, ordered, w0, w1, w2, *rest = refs
    split_columns(sizes, pieces, swapped, ordered)
    grids = sizes.grids
    row_index, ends = domain_ends(sizes)
    for grid, ref in zip(grids, (u0, u1, u2)):
        zero_margin(grid, ref)
    m, water, cross, bone = normal_factors(mixing)
    odd_device = row_index % 2
    parts = (2 - odd_device, 0, 1 + odd_device)
    beyond = (
        jnp.where(ends[0], 0.0, 1.0),
        None,
        jnp.where(ends[1], 0.0, 1.0),
    )
    grid = grids[0]
    lane, row = lane_of(), row_of()
    half = sizes.tiles
    p = grid.penalty
    for group in range(grid.groups):
        for strip in range(grid.rows // SUB):
            start = strip * SUB
            part, inner = divmod(start, sizes.rows)

            def load(kind, energy, tile):
                plane = (2 * kind + energy) * sizes.slices + group
                rows = pl.ds(inner, SUB)
                sides = [
                    ordered[tile, parts[part], plane, rows, pl.ds(side * LANES, LANES)]
                    for side in range(2)
                ]
                if kind == 1 and beyond[part] is not None:
                    sides = [side + beyond[part] for side in sides]
                return sides

            vertical = jnp.full((SUB, LANES), 2.0, jnp.float32)
            for edge, inside in zip((grid.own - 1, 2 * grid.own - 1), ends):
                for place in (edge, edge + 1):
                    if start <= place < start + SUB:
                        missing = jnp.logical_and(row == place - start, jnp.logical_not(inside))
                        vertical = jnp.where(missing, vertical - 1.0, vertical)
            for tile in range(half):
                counts = [load(0, energy, tile) for energy in range(2)]
                weights = [load(1, energy, tile) for energy in range(2)]
                if part == 1:
                    for energy, pair in enumerate(weights):
                        w0[group, energy, tile, pl.ds(inner, SUB), :] = pair[0] + pair[1]
                for parity in range(2):
                    y = [counts[energy][parity] for energy in range(2)]
                    w = [weights[energy][parity] for energy in range(2)]
                    dw = w[0] * water[0] + w[1] * water[1]
                    dx = w[0] * cross[0] + w[1] * cross[1]
                    db = w[0] * bone[0] + w[1] * bone[1]
                    t = [w[energy] * y[energy] for energy in range(2)]
                    fw = t[0] * m[0][0] + t[1] * m[1][0]
                    fb = t[0] * m[0][1] + t[1] * m[1][1]
                    total = vertical + 2.0
                    if parity == 0 and tile == 0:
                        total = jnp.where(lane == 0, total - 1.0, total)
                    if parity == 1 and tile == half - 1:
                        total = jnp.where(lane == LANES - 1, total - 1.0, total)
                    total = p * total
                    uw, ub = solve_pair(dw + total, dx, db + total, fw, fb)
                    k = parity * half + tile
                    rows = pl.ds(start, SUB)
                    for member, value in enumerate((dw, dx, db)):
                        d0[group, member, k, rows, :] = value
                    for member, value in enumerate((fw, fb)):
                        f0[group, member, k, rows, :] = value
                    for member, value in enumerate((uw, ub)):
                        u0[group, member, k, rows, :] = value
    restrict_first(grids, d0, (d1,), 3, 0, grids[1].rows // SUB)
    restrict_second(grids, d1, (d2,), 3, 0, grids[2].rows // SUB)
    state = ((u0, u1, u2), (f0, f1, f2), (d0, d1, d2), (None, uc1, uc2), rest)
    all_rows = ((0, grids[0].rows // SUB), (0, grids[1].rows // SUB))
    restrict_first(grids, w0, (w1,), 2, 0, grids[1].own // SUB, summed=True)
    restrict_second(grids, w1, (w2,), 2, 0, grids[2].own // SUB)
    descend(sizes, ends, state, join_tiles(grids, w2, 0), message, all_rows)


def middle_rows(sizes):
    return (
        (sizes.rows // 2 // SUB, 5 * sizes.rows // 2 // SUB),
        (sizes.rows // 4 // SUB, 5 * sizes.rows // 4 // SUB),
    )


def middle_kernel(
    sizes, mixing, received, u0i, u1i, u2i, f0, f1i, f2i, d0, d1, d2, uc1i, uc2i,
    u0, u1, u2, f1, f2, uc1, uc2, message,
    correction, raised0, raised1, raised2, *rest,
):
    grids = sizes.grids
    row_index, ends = domain_ends(sizes)
    for source, target in ((u0i, u0), (u1i, u1), (u2i, u2)):
        target[...] = source[...]
    scratch = (correction, (raised0, raised1, raised2))
    fields = [(received, k, 3) for k in range(3)]
    span = middle_rows(sizes)
    state = ((u0, u1, u2), (f0, f1i, f2i), (d0, d1, d2), (None, uc1i, uc2i))
    ascend(sizes, ends, row_index, mixing, fields, state, scratch, span)
    (a0, z0), _ = span
    relax_strips(grids[0], ends, u0, f0, d0, a0, z0)
    zero_margin(grids[1], u1)
    zero_margin(grids[2], u2)
    state = ((u0, u1, u2), (f0, f1, f2), (d0, d1, d2), (None, uc1, uc2), rest)
    descend(sizes, ends, state, None, message, span)


def last_kernel(
    sizes, mixing, received, first_received, u0, u1, u2, f0, f1, f2, d0, d1, d2, uc1, uc2,
    out,
    v0, v1, v2, correction, raised0, raised1, raised2,
):
    grids = sizes.grids
    row_index, ends = domain_ends(sizes)
    for source, target in ((u0, v0), (u1, v1), (u2, v2)):
        target[...] = source[...]
    scratch = (correction, (raised0, raised1, raised2))
    fields = [(received, 0, 2), (received, 1, 2), (first_received, 2, 3)]
    own = (sizes.rows // SUB, 2 * sizes.rows // SUB)
    span = (own, middle_rows(sizes)[1])
    state = ((v0, v1, v2), (f0, f1, f2), (d0, d1, d2), (None, uc1, uc2))
    ascend(sizes, ends, row_index, mixing, fields, state, scratch, span)
    column_index = lax.axis_index("gy")
    lane = lane_of()
    tile = column_index // 2
    index = (column_index % 2) * (LANES // 2) + lane // 2
    even = lane % 2 == 0
    for group in range(grids[0].groups):
        for member in range(2):
            for strip in range(*own):
                rows = pl.ds(strip * SUB, SUB)
                first = v0[group, member, tile, rows, :]
                second = v0[group, member, tile + sizes.tiles, rows, :]
                out[member, group, pl.ds(strip * SUB - sizes.rows, SUB), :] = jnp.where(
                    even, take_lanes(first, index), take_lanes(second, index)
                )


def shaped(shape):
    return jax.ShapeDtypeStruct(shape, jnp.float32)


def local(spectra, noise_weights, mixing):
    row_devices, column_devices = lax.axis_size("gx"), lax.axis_size("gy")
    _, slices, rows, columns = spectra.shape
    extents = (slices, rows, columns, row_devices, column_devices)
    sizes = Sizes(*extents)
    grids = sizes.grids
    flat = (2 * slices, rows, columns)
    raw = jnp.concatenate(
        [
            spectra.astype(jnp.float32).reshape(flat),
            noise_weights.astype(jnp.float32).reshape(flat),
        ]
    )
    near, far = [], []
    for i in range(row_devices - 1):
        (far if i % 2 else near).extend([(i, i + 1), (i + 1, i)])
    beside = [lax.ppermute(raw, "gx", far), lax.ppermute(raw, "gx", near)][::-1]
    tiles = jnp.stack([raw] + beside)
    if column_devices == 2:
        pieces = (tiles, lax.ppermute(tiles, "gy", [(0, 1), (1, 0)]))
    else:
        pieces = (lax.all_gather(tiles, "gy"),)

    def vmem(shape):
        return pltpu.VMEM(shape, jnp.float32)

    def message_shape(fields):
        share = sizes.join_tiles * fields * sizes.join_rows // column_devices
        group = next(g for g in (8, 4, 2, 1) if share % g == 0)
        return (row_devices * column_devices, share // group, group, LANES)

    fields = [grid.shape(2) for grid in grids]
    datas = [grid.shape(3) for grid in grids]

    def halved(shape):
        return shape[:2] + (shape[2] // 2,) + shape[3:]

    rests = [vmem(halved(fields[0])), vmem(fields[1]), vmem(fields[2])]
    rests.append(vmem((sizes.join_tiles * 3 * sizes.join_rows, LANES)))
    join_whole = row_devices * sizes.join_rows
    coarse = [
        vmem((sizes.join_tiles, join_whole + 3 * SUB, LANES)),
        vmem(halved(fields[0])),
        vmem(fields[1]),
        vmem(fields[2]),
    ]

    vmem_limit = min(16 * max(1, sizes.tiles), 60) << 20

    def call(body, outs, scratch):
        kernel = lambda *refs: body(Sizes(*extents), *refs)
        return pl.pallas_call(
            kernel,
            out_shape=[shaped(shape) for shape in outs],
            scratch_shapes=scratch,
            name=body.__name__,
            compiler_params=pltpu.CompilerParams(vmem_limit_bytes=vmem_limit),
        )

    outs = fields + fields + datas + fields[1:] + [message_shape(3)]
    weights = [
        vmem((slices, 2, sizes.tiles, rows, LANES)),
        vmem((slices, 2, sizes.tiles, grids[1].own, LANES)),
        vmem((1, 2, grids[2].tiles, max(grids[2].own, 2 * SUB), LANES)),
    ]
    spread = jnp.broadcast_to(mixing.reshape(-1, 1, 1), (mixing.size, SUB, LANES))
    u0, u1, u2, f0, f1, f2, d0, d1, d2, uc1, uc2, message = call(
        start_kernel, outs, [vmem((sizes.tiles,) + tiles.shape[:3] + (2 * LANES,))] + weights + rests
    )(spread, *pieces)
    first_received = lax.all_to_all(message, ("gx", "gy"), 0, 0, tiled=True).reshape(-1, LANES)
    outs = fields + fields[1:] + fields[1:] + [message_shape(2)]
    u0, u1, u2, f1, f2, uc1, uc2, message = call(middle_kernel, outs, coarse + rests)(
        spread, first_received, u0, u1, u2, f0, f1, f2, d0, d1, d2, uc1, uc2
    )
    received = lax.all_to_all(message, ("gx", "gy"), 0, 0, tiled=True).reshape(-1, LANES)
    outs = [(2, slices, rows, columns)]
    return call(last_kernel, outs, [vmem(shape) for shape in fields] + coarse)(
        spread, received, first_received, u0, u1, u2, f0, f1, f2, d0, d1, d2, uc1, uc2
    )[0]


def solution(mesh):
    return jax.shard_map(
        local,
        mesh=mesh,
        in_specs=(P(None, None, "gx", "gy"), P(None, None, "gx", "gy"), P()),
        out_specs=P(None, None, "gx", "gy"),
        check_vma=False,
    )
```

```python
import jax
import jax.numpy as jnp
from jax import lax
from jax.experimental import pallas as pl
from jax.experimental.pallas import tpu as pltpu
from jax.sharding import PartitionSpec as P

LEVELS = 6
COARSE_SWEEPS = 4
JOIN = 3

huber_delta = 0.05
relaxation = 0.8
smoothness = 256.0

LANES = 128
SUB = 8


def penalty_of(level):
    return smoothness / 4.0**level


def lane_of(shape=(SUB, LANES)):
    return lax.broadcasted_iota(jnp.int32, shape, 1)


def row_of(shape=(SUB, LANES)):
    return lax.broadcasted_iota(jnp.int32, shape, 0)


def roll_lanes(x, shift):
    return pltpu.roll(x, shift % LANES, axis=1)


def roll_rows(x, shift):
    return pltpu.roll(x, shift % x.shape[0], axis=0)


def take_lanes(x, index):
    return jnp.take_along_axis(x, index, axis=1)


def from_right(tiles, step=1):
    rolled = [roll_lanes(tile, -step) for tile in tiles]
    if len(tiles) == 1:
        return rolled
    inside = lane_of(tiles[0].shape) < LANES - step
    return [
        jnp.where(inside, rolled[k], rolled[(k + 1) % len(tiles)]) for k in range(len(tiles))
    ]


def from_left(tiles, step=1):
    rolled = [roll_lanes(tile, step) for tile in tiles]
    if len(tiles) == 1:
        return rolled
    inside = lane_of(tiles[0].shape) >= step
    return [jnp.where(inside, rolled[k], rolled[k - 1]) for k in range(len(tiles))]


def flux(gap, with_factor):
    if not with_factor:
        return jnp.clip(gap, -huber_delta, huber_delta), None
    factor = 1.0 / jnp.maximum(jnp.abs(gap), huber_delta)
    return factor * gap, factor


def scaled_penalty(level, with_factor):
    return penalty_of(level) * huber_delta if with_factor else penalty_of(level)


def keep(mask, value):
    return value if mask is None or value is None else jnp.where(mask, value, 0.0)


def row_sums(tiles, masks, with_factor, step=1):
    right = from_right(tiles, step)
    flows, factors = [], []
    for k, tile in enumerate(tiles):
        flow, factor = flux(right[k] - tile, with_factor)
        flows.append(keep(masks[k], flow))
        factors.append(keep(masks[k], factor))
    back = from_left(flows, step)
    flow_sum = [flows[k] - back[k] for k in range(len(tiles))]
    if not with_factor:
        return flow_sum, None
    back = from_left(factors, step)
    return flow_sum, [factors[k] + back[k] for k in range(len(tiles))]


def row_sums_split(tiles, masks, with_factor):
    half = len(tiles) // 2
    even, odd = tiles[:half], tiles[half:]
    after = from_right(even)
    inner = [flux(odd[k] - even[k], with_factor) for k in range(half)]
    outer = [flux(after[k] - odd[k], with_factor) for k in range(half)]
    outer = [tuple(keep(masks[k], part) for part in outer[k]) for k in range(half)]
    back = from_left([part[0] for part in outer])
    flow_sum = [inner[k][0] - back[k] for k in range(half)]
    flow_sum += [outer[k][0] - inner[k][0] for k in range(half)]
    if not with_factor:
        return flow_sum, None
    back = from_left([part[1] for part in outer])
    factor_sum = [inner[k][1] + back[k] for k in range(half)]
    factor_sum += [inner[k][1] + outer[k][1] for k in range(half)]
    return flow_sum, factor_sum


def column_masks(tiles, width, step=1):
    masks = []
    for k in range(tiles):
        place = (lane_of() + k * LANES) % width
        ends = any((k * LANES + n) % width >= width - step for n in range(LANES))
        masks.append(place < width - step if ends else None)
    return masks


class Grid:
    def __init__(self, level, sizes):
        self.level = level
        self.penalty = penalty_of(level)
        self.own = sizes.rows >> level
        self.rows = 3 * self.own
        self.split = level == 0
        self.masks = None
        if level == 0:
            self.groups, self.tiles = sizes.slices, 2 * sizes.tiles
            self.mask_place = (sizes.tiles, sizes.tiles * LANES)
        elif level == 1:
            self.groups, self.tiles = sizes.slices, sizes.tiles
            self.mask_place = (self.tiles, sizes.tiles * LANES)
        else:
            self.groups, self.tiles = 1, sizes.slices * sizes.tiles // 2
            self.mask_place = (self.tiles, sizes.tiles * LANES // 2)

    def shape(self, members):
        return (self.groups, members, self.tiles, self.rows + SUB, LANES)

    def across(self, tiles, with_factor):
        if self.masks is None:
            self.masks = column_masks(*self.mask_place)
        if self.split:
            return row_sums_split(tiles, self.masks, with_factor)
        return row_sums(tiles, self.masks, with_factor)

    def row_mask(self, start, ends):
        mask = None
        for edge, inside in zip((self.own - 1, 2 * self.own - 1), ends):
            if start <= edge < start + SUB:
                part = jnp.logical_or(row_of() != edge - start, inside)
                mask = part if mask is None else jnp.logical_and(mask, part)
        return mask


class Sizes:
    def __init__(self, slices, rows, columns, row_devices, column_devices):
        self.slices = slices
        self.rows = rows
        self.row_devices = row_devices
        self.column_devices = column_devices
        self.columns = columns
        self.tiles = column_devices * columns // (2 * LANES)
        self.join_rows = rows >> JOIN
        self.join_tiles = slices * self.tiles // 2
        self.join_width = self.tiles * LANES >> (JOIN - 1)
        self.join_halves = 2 if self.join_tiles == 1 else 1
        self.grids = [Grid(level, self) for level in range(JOIN)]


def sweep(grid, ends, field, first, last, with_factor, emit):
    strips = range(first, last)
    for group in range(grid.groups):

        def vertical(start, member, tile, center):
            below = field[group, member, tile, pl.ds(start + 1, SUB), :]
            flow, factor = flux(below - center, with_factor)
            mask = grid.row_mask(start, ends)
            return keep(mask, flow), keep(mask, factor)

        carry = {}
        for member in range(2):
            for tile in range(grid.tiles):
                if first > 0:
                    start = (first - 1) * SUB
                    center = field[group, member, tile, pl.ds(start, SUB), :]
                    parts = vertical(start, member, tile, center)
                    carry[member, tile] = [None if x is None else roll_rows(x, 1) for x in parts]
                else:
                    zero = jnp.zeros((SUB, LANES), jnp.float32)
                    carry[member, tile] = [zero, zero]
        top = row_of() == 0
        for strip in strips:
            start = strip * SUB
            centers, flows, factors = [], [], []
            for member in range(2):
                tiles = [
                    field[group, member, tile, pl.ds(start, SUB), :] for tile in range(grid.tiles)
                ]
                flow_sum, factor_sum = grid.across(tiles, with_factor)
                for tile in range(grid.tiles):
                    flow, factor = vertical(start, member, tile, tiles[tile])
                    rolled = roll_rows(flow, 1)
                    above = jnp.where(top, carry[member, tile][0], rolled)
                    flow_sum[tile] = flow_sum[tile] + (flow - above)
                    carry[member, tile][0] = rolled
                    if with_factor:
                        rolled = roll_rows(factor, 1)
                        above = jnp.where(top, carry[member, tile][1], rolled)
                        factor_sum[tile] = factor_sum[tile] + (factor + above)
                        carry[member, tile][1] = rolled
                centers.append(tiles)
                flows.append(flow_sum)
                factors.append(factor_sum)
            emit(group, start, centers, flows, factors)


def solve_pair(water, cross, bone, right_water, right_bone):
    scale = relaxation / (water * bone - cross * cross)
    return (
        scale * (bone * right_water - cross * right_bone),
        scale * (water * right_bone - cross * right_water),
    )


def relax_strips(grid, ends, field, source, data, first, last):
    p = scaled_penalty(grid.level, True)

    def emit(group, start, centers, flows, factors):
        rows = pl.ds(start, SUB)
        for tile in range(grid.tiles):
            water, cross, bone = (data[group, m, tile, rows, :] for m in range(3))
            u, v = centers[0][tile], centers[1][tile]
            right = [
                source[group, 0, tile, rows, :] - (water * u + cross * v) + p * flows[0][tile],
                source[group, 1, tile, rows, :] - (cross * u + bone * v) + p * flows[1][tile],
            ]
            du, dv = solve_pair(
                water + p * factors[0][tile], cross, bone + p * factors[1][tile], *right
            )
            field[group, 0, tile, rows, :] = u + du
            field[group, 1, tile, rows, :] = v + dv

    sweep(grid, ends, field, first, last, True, emit)


def first_relax_strips(grid, ends, field, source, data, first, last):
    p = scaled_penalty(grid.level, True)

    def emit(group, start, centers, flows, factors):
        rows = pl.ds(start, SUB)
        for tile in range(grid.tiles):
            water, cross, bone = (data[group, m, tile, rows, :] for m in range(3))
            u, v = centers[0][tile], centers[1][tile]
            right = [source[group, m, tile, rows, :] for m in range(2)]
            source[group, 0, tile, rows, :] = right[0] + (
                (water * u + cross * v) - p * flows[0][tile]
            )
            source[group, 1, tile, rows, :] = right[1] + (
                (cross * u + bone * v) - p * flows[1][tile]
            )
            du, dv = solve_pair(
                water + p * factors[0][tile], cross, bone + p * factors[1][tile], *right
            )
            field[group, 0, tile, rows, :] = u + du
            field[group, 1, tile, rows, :] = v + dv

    sweep(grid, ends, field, first, last, True, emit)


def residual_strips(grid, ends, field, source, data, out, first, last):
    p = scaled_penalty(grid.level, False)

    def emit(group, start, centers, flows, factors):
        rows = pl.ds(start, SUB)
        rests = [[], []]
        for tile in range(grid.tiles):
            water, cross, bone = (data[group, m, tile, rows, :] for m in range(3))
            u, v = centers[0][tile], centers[1][tile]
            rests[0].append(
                source[group, 0, tile, rows, :] - (water * u + cross * v) + p * flows[0][tile]
            )
            rests[1].append(
                source[group, 1, tile, rows, :] - (cross * u + bone * v) + p * flows[1][tile]
            )
        for member in range(2):
            parts = rests[member]
            if grid.split:
                half = grid.tiles // 2
                parts = [parts[k] + parts[half + k] for k in range(half)]
            for tile, part in enumerate(parts):
                out[group, member, tile, rows, :] = part

    sweep(grid, ends, field, first, last, False, emit)


def pair_rows(ref, group, member, tile, start):
    upper = ref[group, member, tile, pl.ds(2 * start, SUB, stride=2), :]
    lower = ref[group, member, tile, pl.ds(2 * start + 1, SUB, stride=2), :]
    return upper + lower


def merge_pair(first, second):
    index = (2 * lane_of()) % LANES
    halves = [take_lanes(x + roll_lanes(x, -1), index) for x in (first, second)]
    return jnp.where(lane_of() < LANES // 2, halves[0], halves[1])


def split_pair(value):
    index = lane_of() // 2
    return take_lanes(value, index), take_lanes(value, index + LANES // 2)


def restrict_first(grids, ref, out, members, first, last, summed=False):
    coarse = grids[1]
    for group in range(coarse.groups):
        for member in range(members):
            for tile in range(coarse.tiles):
                for strip in range(first, last):
                    start = strip * SUB
                    total = pair_rows(ref, group, member, tile, start)
                    if not summed:
                        total = total + pair_rows(ref, group, member, coarse.tiles + tile, start)
                    for target in out:
                        target[group, member, tile, pl.ds(start, SUB), :] = 0.25 * total


def restrict_second(grids, ref, out, members, first, last):
    fine, coarse = grids[1], grids[2]
    places = [(group, tile) for group in range(fine.groups) for tile in range(fine.tiles)]
    for member in range(members):
        for tile in range(coarse.tiles):
            for strip in range(first, last):
                start = strip * SUB
                pair = [
                    pair_rows(ref, g, member, t, start) for g, t in places[2 * tile : 2 * tile + 2]
                ]
                merged = 0.25 * merge_pair(*pair)
                for target in out:
                    target[0, member, tile, pl.ds(start, SUB), :] = merged


def join_tiles(grids, ref, start):
    grid = grids[2]
    flat = [
        pair_rows(ref, 0, member, tile, start) for member in range(2) for tile in range(grid.tiles)
    ]
    return [0.25 * merge_pair(flat[2 * k], flat[2 * k + 1]) for k in range(len(flat) // 2)]


def descend(sizes, ends, state, weights, message, first_rows):
    grids = sizes.grids
    u, f, d, uc, (*rest, outgoing) = state
    (a0, z0), (a1, z1) = first_rows
    residual_strips(grids[0], ends, u[0], f[0], d[0], rest[0], a0, z0)
    restrict_first(grids, u[0], (u[1], uc[1]), 2, a1, z1)
    restrict_first(grids, rest[0], (f[1],), 2, a1, z1, summed=True)
    first_relax_strips(grids[1], ends, u[1], f[1], d[1], a1, z1)
    residual_strips(grids[1], ends, u[1], f[1], d[1], rest[1], a1, z1)
    strips = grids[2].rows // SUB
    restrict_second(grids, u[1], (u[2], uc[2]), 2, 0, strips)
    restrict_second(grids, rest[1], (f[2],), 2, 0, strips)
    first_relax_strips(grids[2], ends, u[2], f[2], d[2], 0, strips)
    residual_strips(grids[2], ends, u[2], f[2], d[2], rest[2], 0, strips)
    h = sizes.join_rows
    fields = [join_tiles(grids, ref, grids[2].own // 2) for ref in (u[2], rest[2])]
    if weights is not None:
        fields.append(weights)
    for place, tiles in enumerate(fields):
        for k, tile in enumerate(tiles):
            outgoing[pl.ds((k * len(fields) + place) * h, h), :] = tile[:h]
    targets, parts, share, _ = message.shape
    base = lax.axis_index("gy") * (parts * share)
    for place in range(parts):
        part = outgoing[pl.ds(base + place * share, share), :]
        for target in range(targets):
            message[target, place] = part


def coarse_correction(sizes, mixing, fields):
    tiles = max(1, sizes.join_tiles // 2)
    width = sizes.join_width
    lane, row = lane_of(), row_of()
    low = lane < LANES // 2

    def each(function, *values):
        return [
            [function(*(value[k][v] for value in values)) for v in range(len(values[0][0]))]
            for k in range(tiles)
        ]

    cut = sizes.join_halves == 2

    def exchange(first, second):
        pairs = list(zip(first, second))
        low_lanes = [jnp.where(low, a, roll_lanes(b, LANES // 2)) for a, b in pairs]
        return low_lanes, [jnp.where(low, roll_lanes(a, LANES // 2), b) for a, b in pairs]

    def split(values):
        if not cut:
            return values[:tiles], values[tiles:]
        first, second = exchange(*values)
        return [first], [second]

    def join(first, second):
        return list(exchange(first[0], second[0])) if cut else first + second

    def mean(values, step):
        pair = (lane & step) == 0
        result = [[] for _ in range(tiles)]
        for v in range(0, len(values[0]), 2):
            added = [value[v] + value[v + 1] for value in values]
            right, left = from_right(added, step), from_left(added, step)
            for k in range(tiles):
                result[k].append(0.25 * (added[k] + jnp.where(pair, right[k], left[k])))
        return result

    def add(first, second):
        return each(lambda a, b: a + b, first, second)

    def subtract(first, second):
        return each(lambda a, b: a - b, first, second)

    estimate, rest, weights = fields
    _, *factors = normal_factors(mixing)
    means = split(weights)
    matrices = []
    for level in range(JOIN, LEVELS):
        if level > JOIN:
            means = [mean(part, 1 << (level - JOIN - 1)) for part in means]
        water, cross, bone = (
            each(lambda a, b, pair=pair: a * pair[0] + b * pair[1], *means) for pair in factors
        )
        matrices.append((water, bone, cross))

    def sums(level, values, with_factor):
        step = 1 << (level - JOIN)
        count = len(values[0])
        totals = [[[None] * count for _ in range(tiles)] for _ in range(2)]
        for v in range(count):
            line = [value[v] for value in values]
            for shifted, side in ((from_right(line, step), 1), (from_left(line, step), 0)):
                for k in range(tiles):
                    place = (lane + k * LANES) % width
                    inside = place < width - step if side else place >= step
                    for total, part in zip(totals, flux(shifted[k] - line[k], with_factor)):
                        part = keep(inside, part)
                        total[k][v] = part if side or part is None else total[k][v] + part
        for k, value in enumerate(values):
            edges = [
                flux(b - a, with_factor) for a, b in zip(value, value[1:])
            ]
            above, below = roll_rows(value[-1], 1), roll_rows(value[0], -1)
            has_above, has_below = row > 0, row < SUB - 1
            if cut:
                above = jnp.where(has_above, above, roll_lanes(above, LANES // 2))
                below = jnp.where(has_below, below, roll_lanes(below, LANES // 2))
                has_above = jnp.logical_or(has_above, jnp.logical_not(low))
                has_below = jnp.logical_or(has_below, low)
            first = flux(above - value[0], with_factor)
            last = flux(below - value[-1], with_factor)
            for place in range(2 if with_factor else 1):
                total = totals[place][k]
                for v, edge in enumerate(edges):
                    total[v] = total[v] + edge[place]
                    opposite = edge[place] if place else -edge[place]
                    total[v + 1] = total[v + 1] + opposite
                total[0] = total[0] + keep(has_above, first[place])
                total[-1] = total[-1] + keep(has_below, last[place])
        return totals

    def apply(level, values, flows, with_factor):
        p = scaled_penalty(level, with_factor)
        water, bone, cross = matrices[level - JOIN]
        take = lambda d, x, own, other, flow: d * own + x * other - p * flow
        return (
            each(take, water, cross, values[0], values[1], flows[0]),
            each(take, bone, cross, values[1], values[0], flows[1]),
        )

    def solve(level, values, factors, right):
        p = scaled_penalty(level, True)
        water, bone, cross = matrices[level - JOIN]
        water = each(lambda d, factor: d + p * factor, water, factors[0])
        bone = each(lambda d, factor: d + p * factor, bone, factors[1])
        scale = each(lambda a, b, x: relaxation / (a * b - x * x), water, bone, cross)
        move = lambda own, s, b, x, r, q: own + s * (b * r - x * q)
        return (
            each(move, values[0], scale, bone, cross, right[0], right[1]),
            each(move, values[1], scale, water, cross, right[1], right[0]),
        )

    def both(function, *pairs):
        return tuple(function(*(pair[m] for pair in pairs)) for m in range(2))

    def image_of(level, values, with_factor):
        totals = [sums(level, value, with_factor) for value in values]
        image = apply(level, values, [total[0] for total in totals], with_factor)
        return image, [total[1] for total in totals]

    def relax(level, values, source):
        image, factors = image_of(level, values, True)
        return solve(level, values, factors, both(subtract, source, image))

    def cycle(level, values, rest):
        image, factors = image_of(level, values, True)
        source = both(add, rest, image)
        start = values
        values = solve(level, values, factors, rest)
        if level == LEVELS - 1:
            for _ in range(COARSE_SWEEPS - 1):
                values = relax(level, values, source)
        else:
            step = 1 << (level - JOIN)
            image, _ = image_of(level, values, False)
            coarse_rest = [mean(part, step) for part in both(subtract, source, image)]
            coarse = [mean(part, step) for part in values]
            correction = cycle(level + 1, coarse, coarse_rest)
            raised = [
                [[part[v // 2] for v in range(2 * len(part))] for part in member]
                for member in correction
            ]
            values = relax(level, both(add, values, raised), source)
        return both(subtract, values, start)

    return join(*cycle(JOIN, split(estimate), split(rest)))


def ascend(sizes, ends, row_index, mixing, received, state, scratch, level_rows):
    grids = sizes.grids
    old, u, f, d, uc = state
    correction, raised = scratch
    h = sizes.join_rows
    whole = sizes.row_devices * h
    halves = sizes.join_halves
    count = whole // SUB // halves
    places = [(k, half) for k in range(sizes.join_tiles) for half in range(halves)]
    fields = []
    for ref, field, total in received:
        block = sizes.join_tiles * total * h

        def rows_of(k, half, v):
            start = (half * count * SUB + v) // h * block + (k * total + field) * h + v % h
            return ref[pl.ds(start, SUB, stride=count // h * block), :]

        fields.append([[rows_of(k, half, v) for v in range(count)] for k, half in places])
    values = coarse_correction(sizes, mixing, fields)
    for k in range(sizes.join_tiles):
        correction[k, :SUB, :] = jnp.zeros((SUB, LANES), jnp.float32)
        correction[k, pl.ds(SUB + whole, 2 * SUB), :] = jnp.zeros((2 * SUB, LANES), jnp.float32)
    for (k, half), lines in zip(places, values):
        for v in range(count):
            rows = pl.ds(SUB + half * count * SUB + v, SUB, stride=count)
            correction[k, rows, :] = lines[v]

    grid = grids[2]
    strips = grid.rows // SUB
    base = row_index * h + SUB - h
    for k in range(sizes.join_tiles):
        for start in range(0, 3 * h, SUB):
            parts = split_pair(correction[k, pl.ds(base + start, SUB), :])
            for side, part in enumerate(parts):
                member, tile = divmod(2 * k + side, grid.tiles)
                for odd in range(2):
                    raised[2][0, member, tile, pl.ds(2 * start + odd, SUB, stride=2), :] = part
    add_raised(grid, old[2], u[2], raised[2], 0, strips)
    relax_strips(grid, ends, u[2], f[2], d[2], 0, strips)

    fine = grids[1]
    places = [(group, tile) for group in range(fine.groups) for tile in range(fine.tiles)]
    for member in range(2):
        for tile in range(grid.tiles):
            for strip in range(strips):
                start = strip * SUB
                rows = pl.ds(start, SUB)
                parts = split_pair(u[2][0, member, tile, rows, :] - uc[2][0, member, tile, rows, :])
                for (g, t), part in zip(places[2 * tile : 2 * tile + 2], parts):
                    for odd in range(2):
                        raised[1][g, member, t, pl.ds(2 * start + odd, SUB, stride=2), :] = part
    (a0, z0), (a1, z1) = level_rows
    add_raised(fine, old[1], u[1], raised[1], a1 - 1, z1 + 1)
    relax_strips(fine, ends, u[1], f[1], d[1], a1, z1)

    for group in range(fine.groups):
        for member in range(2):
            for tile in range(fine.tiles):
                for strip in range(a1, z1):
                    start = strip * SUB
                    rows = pl.ds(start, SUB)
                    part = u[1][group, member, tile, rows, :] - uc[1][group, member, tile, rows, :]
                    for odd in range(2):
                        raised[0][group, member, tile, pl.ds(2 * start + odd, SUB, stride=2), :] = part
    span = max(2 * a1, a0 - 1), min(2 * z1, z0 + 1)
    add_raised(grids[0], old[0], u[0], raised[0], *span)
    relax_strips(grids[0], ends, u[0], f[0], d[0], a0, z0)


def add_raised(grid, before, field, raised, first, last):
    period = grid.tiles // 2 if grid.split else grid.tiles
    for group in range(grid.groups):
        for member in range(2):
            for tile in range(grid.tiles):
                for strip in range(first, last):
                    rows = pl.ds(strip * SUB, SUB)
                    field[group, member, tile, rows, :] = (
                        before[group, member, tile, rows, :]
                        + raised[group, member, tile % period, rows, :]
                    )


def zero_margin(grid, ref):
    for group in range(grid.groups):
        for member in range(2):
            for tile in range(grid.tiles):
                ref[group, member, tile, pl.ds(grid.rows, SUB), :] = jnp.zeros(
                    (SUB, LANES), jnp.float32
                )


def domain_ends(sizes):
    row_index = lax.axis_index("gx")
    return row_index, (row_index > 0, row_index < sizes.row_devices - 1)


def normal_factors(mixing):
    m = [[mixing[2 * i + j] for j in range(2)] for i in range(2)]
    water = [m[0][0] * m[0][0], m[1][0] * m[1][0]]
    cross = [m[0][0] * m[0][1], m[1][0] * m[1][1]]
    bone = [m[0][1] * m[0][1], m[1][1] * m[1][1]]
    return m, water, cross, bone


def split_columns(sizes, pieces, swapped, out):
    shape = (2 * LANES, 2 * LANES)
    source, target = row_of(shape), lane_of(shape)
    source = jnp.bitwise_xor(source, swapped * LANES)
    wanted = jnp.where(target < LANES, 2 * target, 2 * (target - LANES) + 1)
    select = (source == wanted).astype(jnp.float32).astype(jnp.bfloat16)
    for tile in range(sizes.tiles):
        for part in range(3):
            sides = [piece[part] for piece in pieces[2 * tile : 2 * tile + 2]]
            sides = [side.reshape(-1, LANES).astype(jnp.bfloat16) for side in sides]
            both = jnp.concatenate(sides, axis=1)
            result = jnp.dot(both, select, preferred_element_type=jnp.float32)
            out[tile, part] = result.reshape(out.shape[2:])


def start_kernel(sizes, mixing, *refs):
    if sizes.column_devices == 2:
        pieces, refs = refs[:2], refs[2:]
        swapped = lax.axis_index("gy")
    else:
        pieces, refs = [refs[0].at[k] for k in range(sizes.column_devices)], refs[1:]
        swapped = 0
    u0, u1, u2, f0, f1, f2, d0, d1, d2, uc1, uc2, message, ordered, w0, w1, w2, *rest = refs
    split_columns(sizes, pieces, swapped, ordered)
    grids = sizes.grids
    row_index, ends = domain_ends(sizes)
    for grid, ref in zip(grids, (u0, u1, u2)):
        zero_margin(grid, ref)
    m, water, cross, bone = normal_factors(mixing)
    odd_device = row_index % 2
    parts = (2 - odd_device, 0, 1 + odd_device)
    beyond = (
        jnp.where(ends[0], 0.0, 1.0),
        None,
        jnp.where(ends[1], 0.0, 1.0),
    )
    grid = grids[0]
    lane, row = lane_of(), row_of()
    half = sizes.tiles
    p = grid.penalty
    for group in range(grid.groups):
        for strip in range(grid.rows // SUB):
            start = strip * SUB
            part, inner = divmod(start, sizes.rows)

            def load(kind, energy, tile):
                plane = (2 * kind + energy) * sizes.slices + group
                rows = pl.ds(inner, SUB)
                sides = [
                    ordered[tile, parts[part], plane, rows, pl.ds(side * LANES, LANES)]
                    for side in range(2)
                ]
                if kind == 1 and beyond[part] is not None:
                    sides = [side + beyond[part] for side in sides]
                return sides

            vertical = jnp.full((SUB, LANES), 2.0, jnp.float32)
            for edge, inside in zip((grid.own - 1, 2 * grid.own - 1), ends):
                for place in (edge, edge + 1):
                    if start <= place < start + SUB:
                        missing = jnp.logical_and(row == place - start, jnp.logical_not(inside))
                        vertical = jnp.where(missing, vertical - 1.0, vertical)
            for tile in range(half):
                counts = [load(0, energy, tile) for energy in range(2)]
                weights = [load(1, energy, tile) for energy in range(2)]
                if part == 1:
                    for energy, pair in enumerate(weights):
                        w0[group, energy, tile, pl.ds(inner, SUB), :] = pair[0] + pair[1]
                for parity in range(2):
                    y = [counts[energy][parity] for energy in range(2)]
                    w = [weights[energy][parity] for energy in range(2)]
                    dw = w[0] * water[0] + w[1] * water[1]
                    dx = w[0] * cross[0] + w[1] * cross[1]
                    db = w[0] * bone[0] + w[1] * bone[1]
                    t = [w[energy] * y[energy] for energy in range(2)]
                    fw = t[0] * m[0][0] + t[1] * m[1][0]
                    fb = t[0] * m[0][1] + t[1] * m[1][1]
                    total = vertical + 2.0
                    if parity == 0 and tile == 0:
                        total = jnp.where(lane == 0, total - 1.0, total)
                    if parity == 1 and tile == half - 1:
                        total = jnp.where(lane == LANES - 1, total - 1.0, total)
                    total = p * total
                    uw, ub = solve_pair(dw + total, dx, db + total, fw, fb)
                    k = parity * half + tile
                    rows = pl.ds(start, SUB)
                    for member, value in enumerate((dw, dx, db)):
                        d0[group, member, k, rows, :] = value
                    for member, value in enumerate((fw, fb)):
                        f0[group, member, k, rows, :] = value
                    for member, value in enumerate((uw, ub)):
                        u0[group, member, k, rows, :] = value
    restrict_first(grids, d0, (d1,), 3, 0, grids[1].rows // SUB)
    restrict_second(grids, d1, (d2,), 3, 0, grids[2].rows // SUB)
    state = ((u0, u1, u2), (f0, f1, f2), (d0, d1, d2), (None, uc1, uc2), rest)
    all_rows = ((0, grids[0].rows // SUB), (0, grids[1].rows // SUB))
    restrict_first(grids, w0, (w1,), 2, 0, grids[1].own // SUB, summed=True)
    restrict_second(grids, w1, (w2,), 2, 0, grids[2].own // SUB)
    descend(sizes, ends, state, join_tiles(grids, w2, 0), message, all_rows)


def middle_rows(sizes):
    return (
        (sizes.rows // 2 // SUB, 5 * sizes.rows // 2 // SUB),
        (sizes.rows // 4 // SUB, 5 * sizes.rows // 4 // SUB),
    )


def middle_kernel(
    sizes, mixing, received, u0i, u1i, u2i, f0, f1i, f2i, d0, d1, d2, uc1i, uc2i,
    u0, u1, u2, f1, f2, uc1, uc2, message,
    correction, raised0, raised1, raised2, *rest,
):
    grids = sizes.grids
    row_index, ends = domain_ends(sizes)
    scratch = (correction, (raised0, raised1, raised2))
    fields = [(received, k, 3) for k in range(3)]
    span = middle_rows(sizes)
    old = (u0i, u1i, u2i)
    state = (old, (u0, u1, u2), (f0, f1i, f2i), (d0, d1, d2), (None, uc1i, uc2i))
    ascend(sizes, ends, row_index, mixing, fields, state, scratch, span)
    (a0, z0), _ = span
    relax_strips(grids[0], ends, u0, f0, d0, a0, z0)
    zero_margin(grids[1], u1)
    zero_margin(grids[2], u2)
    state = ((u0, u1, u2), (f0, f1, f2), (d0, d1, d2), (None, uc1, uc2), rest)
    descend(sizes, ends, state, None, message, span)


def last_kernel(
    sizes, mixing, received, first_received, u0, u1, u2, f0, f1, f2, d0, d1, d2, uc1, uc2,
    out,
    v0, v1, v2, correction, raised0, raised1, raised2,
):
    grids = sizes.grids
    row_index, ends = domain_ends(sizes)
    scratch = (correction, (raised0, raised1, raised2))
    fields = [(received, 0, 2), (received, 1, 2), (first_received, 2, 3)]
    own = (sizes.rows // SUB, 2 * sizes.rows // SUB)
    span = (own, middle_rows(sizes)[1])
    old = (u0, u1, u2)
    state = (old, (v0, v1, v2), (f0, f1, f2), (d0, d1, d2), (None, uc1, uc2))
    ascend(sizes, ends, row_index, mixing, fields, state, scratch, span)
    column_index = lax.axis_index("gy")
    lane = lane_of()
    tile = column_index // 2
    index = (column_index % 2) * (LANES // 2) + lane // 2
    even = lane % 2 == 0
    for group in range(grids[0].groups):
        for member in range(2):
            for strip in range(*own):
                rows = pl.ds(strip * SUB, SUB)
                first = v0[group, member, tile, rows, :]
                second = v0[group, member, tile + sizes.tiles, rows, :]
                out[member, group, pl.ds(strip * SUB - sizes.rows, SUB), :] = jnp.where(
                    even, take_lanes(first, index), take_lanes(second, index)
                )


def shaped(shape):
    return jax.ShapeDtypeStruct(shape, jnp.float32)


def local(spectra, noise_weights, mixing):
    row_devices, column_devices = lax.axis_size("gx"), lax.axis_size("gy")
    _, slices, rows, columns = spectra.shape
    extents = (slices, rows, columns, row_devices, column_devices)
    sizes = Sizes(*extents)
    grids = sizes.grids
    flat = (2 * slices, rows, columns)
    raw = jnp.concatenate(
        [
            spectra.astype(jnp.float32).reshape(flat),
            noise_weights.astype(jnp.float32).reshape(flat),
        ]
    )
    near, far = [], []
    for i in range(row_devices - 1):
        (far if i % 2 else near).extend([(i, i + 1), (i + 1, i)])
    beside = [lax.ppermute(raw, "gx", far), lax.ppermute(raw, "gx", near)][::-1]
    tiles = jnp.stack([raw] + beside)
    if column_devices == 2:
        pieces = (tiles, lax.ppermute(tiles, "gy", [(0, 1), (1, 0)]))
    else:
        pieces = (lax.all_gather(tiles, "gy"),)

    def vmem(shape):
        return pltpu.VMEM(shape, jnp.float32)

    def message_shape(fields):
        share = sizes.join_tiles * fields * sizes.join_rows // column_devices
        group = next(g for g in (8, 4, 2, 1) if share % g == 0)
        return (row_devices * column_devices, share // group, group, LANES)

    fields = [grid.shape(2) for grid in grids]
    datas = [grid.shape(3) for grid in grids]

    def halved(shape):
        return shape[:2] + (shape[2] // 2,) + shape[3:]

    rests = [vmem(halved(fields[0])), vmem(fields[1]), vmem(fields[2])]
    rests.append(vmem((sizes.join_tiles * 3 * sizes.join_rows, LANES)))
    join_whole = row_devices * sizes.join_rows
    coarse = [
        vmem((sizes.join_tiles, join_whole + 3 * SUB, LANES)),
        vmem(halved(fields[0])),
        vmem(fields[1]),
        vmem(fields[2]),
    ]

    vmem_limit = min(16 * max(1, sizes.tiles), 60) << 20

    def call(body, outs, scratch):
        kernel = lambda *refs: body(Sizes(*extents), *refs)
        return pl.pallas_call(
            kernel,
            out_shape=[shaped(shape) for shape in outs],
            scratch_shapes=scratch,
            name=body.__name__,
            compiler_params=pltpu.CompilerParams(vmem_limit_bytes=vmem_limit),
        )

    outs = fields + fields + datas + fields[1:] + [message_shape(3)]
    weights = [
        vmem((slices, 2, sizes.tiles, rows, LANES)),
        vmem((slices, 2, sizes.tiles, grids[1].own, LANES)),
        vmem((1, 2, grids[2].tiles, max(grids[2].own, 2 * SUB), LANES)),
    ]
    spread = jnp.broadcast_to(mixing.reshape(-1, 1, 1), (mixing.size, SUB, LANES))
    u0, u1, u2, f0, f1, f2, d0, d1, d2, uc1, uc2, message = call(
        start_kernel, outs, [vmem((sizes.tiles,) + tiles.shape[:3] + (2 * LANES,))] + weights + rests
    )(spread, *pieces)
    first_received = lax.all_to_all(message, ("gx", "gy"), 0, 0, tiled=True).reshape(-1, LANES)
    outs = fields + fields[1:] + fields[1:] + [message_shape(2)]
    u0, u1, u2, f1, f2, uc1, uc2, message = call(middle_kernel, outs, coarse + rests)(
        spread, first_received, u0, u1, u2, f0, f1, f2, d0, d1, d2, uc1, uc2
    )
    received = lax.all_to_all(message, ("gx", "gy"), 0, 0, tiled=True).reshape(-1, LANES)
    outs = [(2, slices, rows, columns)]
    return call(last_kernel, outs, [vmem(shape) for shape in fields] + coarse)(
        spread, received, first_received, u0, u1, u2, f0, f1, f2, d0, d1, d2, uc1, uc2
    )[0]


def solution(mesh):
    return jax.shard_map(
        local,
        mesh=mesh,
        in_specs=(P(None, None, "gx", "gy"), P(None, None, "gx", "gy"), P()),
        out_specs=P(None, None, "gx", "gy"),
        check_vma=False,
    )
```

```python
import jax
import jax.numpy as jnp
from jax import lax
from jax.experimental import pallas as pl
from jax.experimental.pallas import tpu as pltpu
from jax.sharding import PartitionSpec as P

LEVELS = 6
COARSE_SWEEPS = 4
JOIN = 3

huber_delta = 0.05
relaxation = 0.8
smoothness = 256.0

LANES = 128
SUB = 8


def penalty_of(level):
    return smoothness / 4.0**level


def lane_of(shape=(SUB, LANES)):
    return lax.broadcasted_iota(jnp.int32, shape, 1)


def row_of(shape=(SUB, LANES)):
    return lax.broadcasted_iota(jnp.int32, shape, 0)


def roll_lanes(x, shift):
    return pltpu.roll(x, shift % LANES, axis=1)


def roll_rows(x, shift):
    return pltpu.roll(x, shift % x.shape[0], axis=0)


def take_lanes(x, index):
    return jnp.take_along_axis(x, index, axis=1)


def from_right(tiles, step=1):
    rolled = [roll_lanes(tile, -step) for tile in tiles]
    if len(tiles) == 1:
        return rolled
    inside = lane_of(tiles[0].shape) < LANES - step
    return [
        jnp.where(inside, rolled[k], rolled[(k + 1) % len(tiles)]) for k in range(len(tiles))
    ]


def from_left(tiles, step=1):
    rolled = [roll_lanes(tile, step) for tile in tiles]
    if len(tiles) == 1:
        return rolled
    inside = lane_of(tiles[0].shape) >= step
    return [jnp.where(inside, rolled[k], rolled[k - 1]) for k in range(len(tiles))]


def flux(gap, with_factor):
    if not with_factor:
        return jnp.clip(gap, -huber_delta, huber_delta), None
    factor = 1.0 / jnp.maximum(jnp.abs(gap), huber_delta)
    return factor * gap, factor


def scaled_penalty(level, with_factor):
    return penalty_of(level) * huber_delta if with_factor else penalty_of(level)


def keep(mask, value):
    return value if mask is None or value is None else jnp.where(mask, value, 0.0)


def row_sums(tiles, masks, with_factor, step=1):
    right = from_right(tiles, step)
    flows, factors = [], []
    for k, tile in enumerate(tiles):
        flow, factor = flux(right[k] - tile, with_factor)
        flows.append(keep(masks[k], flow))
        factors.append(keep(masks[k], factor))
    back = from_left(flows, step)
    flow_sum = [flows[k] - back[k] for k in range(len(tiles))]
    if not with_factor:
        return flow_sum, None
    back = from_left(factors, step)
    return flow_sum, [factors[k] + back[k] for k in range(len(tiles))]


def row_sums_split(tiles, masks, with_factor):
    half = len(tiles) // 2
    even, odd = tiles[:half], tiles[half:]
    after = from_right(even)
    inner = [flux(odd[k] - even[k], with_factor) for k in range(half)]
    outer = [flux(after[k] - odd[k], with_factor) for k in range(half)]
    outer = [tuple(keep(masks[k], part) for part in outer[k]) for k in range(half)]
    back = from_left([part[0] for part in outer])
    flow_sum = [inner[k][0] - back[k] for k in range(half)]
    flow_sum += [outer[k][0] - inner[k][0] for k in range(half)]
    if not with_factor:
        return flow_sum, None
    back = from_left([part[1] for part in outer])
    factor_sum = [inner[k][1] + back[k] for k in range(half)]
    factor_sum += [inner[k][1] + outer[k][1] for k in range(half)]
    return flow_sum, factor_sum


def column_masks(tiles, width, step=1):
    masks = []
    for k in range(tiles):
        place = (lane_of() + k * LANES) % width
        ends = any((k * LANES + n) % width >= width - step for n in range(LANES))
        masks.append(place < width - step if ends else None)
    return masks


class Grid:
    def __init__(self, level, sizes):
        self.level = level
        self.penalty = penalty_of(level)
        self.own = sizes.rows >> level
        self.rows = 3 * self.own
        self.split = level == 0
        self.masks = None
        if level == 0:
            self.groups, self.tiles = sizes.slices, 2 * sizes.tiles
            self.mask_place = (sizes.tiles, sizes.tiles * LANES)
        elif level == 1:
            self.groups, self.tiles = sizes.slices, sizes.tiles
            self.mask_place = (self.tiles, sizes.tiles * LANES)
        else:
            self.groups, self.tiles = 1, sizes.slices * sizes.tiles // 2
            self.mask_place = (self.tiles, sizes.tiles * LANES // 2)

    def shape(self, members):
        return (self.groups, members, self.tiles, self.rows + SUB, LANES)

    def across(self, tiles, with_factor):
        if self.masks is None:
            self.masks = column_masks(*self.mask_place)
        if self.split:
            return row_sums_split(tiles, self.masks, with_factor)
        return row_sums(tiles, self.masks, with_factor)

    def row_mask(self, start, ends):
        mask = None
        for edge, inside in zip((self.own - 1, 2 * self.own - 1), ends):
            if start <= edge < start + SUB:
                part = jnp.logical_or(row_of() != edge - start, inside)
                mask = part if mask is None else jnp.logical_and(mask, part)
        return mask


class Sizes:
    def __init__(self, slices, rows, columns, row_devices, column_devices):
        self.slices = slices
        self.rows = rows
        self.row_devices = row_devices
        self.column_devices = column_devices
        self.columns = columns
        self.tiles = column_devices * columns // (2 * LANES)
        self.join_rows = rows >> JOIN
        self.join_tiles = slices * self.tiles // 2
        self.join_width = self.tiles * LANES >> (JOIN - 1)
        self.join_halves = 2 if self.join_tiles == 1 else 1
        self.grids = [Grid(level, self) for level in range(JOIN)]


def sweep(grid, ends, field, first, last, with_factor, emit):
    strips = range(first, last)
    for group in range(grid.groups):

        def vertical(start, member, tile, center):
            below = field[group, member, tile, pl.ds(start + 1, SUB), :]
            flow, factor = flux(below - center, with_factor)
            mask = grid.row_mask(start, ends)
            return keep(mask, flow), keep(mask, factor)

        carry = {}
        for member in range(2):
            for tile in range(grid.tiles):
                if first > 0:
                    start = (first - 1) * SUB
                    center = field[group, member, tile, pl.ds(start, SUB), :]
                    parts = vertical(start, member, tile, center)
                    carry[member, tile] = [None if x is None else roll_rows(x, 1) for x in parts]
                else:
                    zero = jnp.zeros((SUB, LANES), jnp.float32)
                    carry[member, tile] = [zero, zero]
        top = row_of() == 0
        for strip in strips:
            start = strip * SUB
            centers, flows, factors = [], [], []
            for member in range(2):
                tiles = [
                    field[group, member, tile, pl.ds(start, SUB), :] for tile in range(grid.tiles)
                ]
                flow_sum, factor_sum = grid.across(tiles, with_factor)
                for tile in range(grid.tiles):
                    flow, factor = vertical(start, member, tile, tiles[tile])
                    rolled = roll_rows(flow, 1)
                    above = jnp.where(top, carry[member, tile][0], rolled)
                    flow_sum[tile] = flow_sum[tile] + (flow - above)
                    carry[member, tile][0] = rolled
                    if with_factor:
                        rolled = roll_rows(factor, 1)
                        above = jnp.where(top, carry[member, tile][1], rolled)
                        factor_sum[tile] = factor_sum[tile] + (factor + above)
                        carry[member, tile][1] = rolled
                centers.append(tiles)
                flows.append(flow_sum)
                factors.append(factor_sum)
            emit(group, start, centers, flows, factors)


def solve_pair(water, cross, bone, right_water, right_bone):
    scale = relaxation / (water * bone - cross * cross)
    return (
        scale * (bone * right_water - cross * right_bone),
        scale * (water * right_bone - cross * right_water),
    )


def relax_strips(grid, ends, field, source, data, first, last):
    p = scaled_penalty(grid.level, True)

    def emit(group, start, centers, flows, factors):
        rows = pl.ds(start, SUB)
        for tile in range(grid.tiles):
            water, cross, bone = (data[group, m, tile, rows, :] for m in range(3))
            u, v = centers[0][tile], centers[1][tile]
            right = [
                source[group, 0, tile, rows, :] - (water * u + cross * v) + p * flows[0][tile],
                source[group, 1, tile, rows, :] - (cross * u + bone * v) + p * flows[1][tile],
            ]
            du, dv = solve_pair(
                water + p * factors[0][tile], cross, bone + p * factors[1][tile], *right
            )
            field[group, 0, tile, rows, :] = u + du
            field[group, 1, tile, rows, :] = v + dv

    sweep(grid, ends, field, first, last, True, emit)


def first_relax_strips(grid, ends, field, source, data, first, last):
    p = scaled_penalty(grid.level, True)

    def emit(group, start, centers, flows, factors):
        rows = pl.ds(start, SUB)
        for tile in range(grid.tiles):
            water, cross, bone = (data[group, m, tile, rows, :] for m in range(3))
            u, v = centers[0][tile], centers[1][tile]
            right = [source[group, m, tile, rows, :] for m in range(2)]
            source[group, 0, tile, rows, :] = right[0] + (
                (water * u + cross * v) - p * flows[0][tile]
            )
            source[group, 1, tile, rows, :] = right[1] + (
                (cross * u + bone * v) - p * flows[1][tile]
            )
            du, dv = solve_pair(
                water + p * factors[0][tile], cross, bone + p * factors[1][tile], *right
            )
            field[group, 0, tile, rows, :] = u + du
            field[group, 1, tile, rows, :] = v + dv

    sweep(grid, ends, field, first, last, True, emit)


def residual_strips(grid, ends, field, source, data, out, first, last):
    p = scaled_penalty(grid.level, False)

    def emit(group, start, centers, flows, factors):
        rows = pl.ds(start, SUB)
        rests = [[], []]
        for tile in range(grid.tiles):
            water, cross, bone = (data[group, m, tile, rows, :] for m in range(3))
            u, v = centers[0][tile], centers[1][tile]
            rests[0].append(
                source[group, 0, tile, rows, :] - (water * u + cross * v) + p * flows[0][tile]
            )
            rests[1].append(
                source[group, 1, tile, rows, :] - (cross * u + bone * v) + p * flows[1][tile]
            )
        for member in range(2):
            parts = rests[member]
            if grid.split:
                half = grid.tiles // 2
                parts = [parts[k] + parts[half + k] for k in range(half)]
            for tile, part in enumerate(parts):
                out[group, member, tile, rows, :] = part

    sweep(grid, ends, field, first, last, False, emit)


def pair_rows(ref, group, member, tile, start):
    upper = ref[group, member, tile, pl.ds(2 * start, SUB, stride=2), :]
    lower = ref[group, member, tile, pl.ds(2 * start + 1, SUB, stride=2), :]
    return upper + lower


def merge_pair(first, second):
    index = (2 * lane_of()) % LANES
    halves = [take_lanes(x + roll_lanes(x, -1), index) for x in (first, second)]
    return jnp.where(lane_of() < LANES // 2, halves[0], halves[1])


def split_pair(value):
    index = lane_of() // 2
    return take_lanes(value, index), take_lanes(value, index + LANES // 2)


def restrict_first(grids, ref, out, members, first, last, summed=False):
    coarse = grids[1]
    for group in range(coarse.groups):
        for member in range(members):
            for tile in range(coarse.tiles):
                for strip in range(first, last):
                    start = strip * SUB
                    total = pair_rows(ref, group, member, tile, start)
                    if not summed:
                        total = total + pair_rows(ref, group, member, coarse.tiles + tile, start)
                    for target in out:
                        target[group, member, tile, pl.ds(start, SUB), :] = 0.25 * total


def restrict_second(grids, ref, out, members, first, last):
    fine, coarse = grids[1], grids[2]
    places = [(group, tile) for group in range(fine.groups) for tile in range(fine.tiles)]
    for member in range(members):
        for tile in range(coarse.tiles):
            for strip in range(first, last):
                start = strip * SUB
                pair = [
                    pair_rows(ref, g, member, t, start) for g, t in places[2 * tile : 2 * tile + 2]
                ]
                merged = 0.25 * merge_pair(*pair)
                for target in out:
                    target[0, member, tile, pl.ds(start, SUB), :] = merged


def join_tiles(grids, ref, start):
    grid = grids[2]
    flat = [
        pair_rows(ref, 0, member, tile, start) for member in range(2) for tile in range(grid.tiles)
    ]
    return [0.25 * merge_pair(flat[2 * k], flat[2 * k + 1]) for k in range(len(flat) // 2)]


def descend(sizes, ends, state, weights, message, first_rows):
    grids = sizes.grids
    u, f, d, uc, (*rest, outgoing) = state
    (a0, z0), (a1, z1) = first_rows
    residual_strips(grids[0], ends, u[0], f[0], d[0], rest[0], a0, z0)
    restrict_first(grids, u[0], (u[1], uc[1]), 2, a1, z1)
    restrict_first(grids, rest[0], (f[1],), 2, a1, z1, summed=True)
    first_relax_strips(grids[1], ends, u[1], f[1], d[1], a1, z1)
    residual_strips(grids[1], ends, u[1], f[1], d[1], rest[1], a1, z1)
    strips = grids[2].rows // SUB
    restrict_second(grids, u[1], (u[2], uc[2]), 2, 0, strips)
    restrict_second(grids, rest[1], (f[2],), 2, 0, strips)
    first_relax_strips(grids[2], ends, u[2], f[2], d[2], 0, strips)
    residual_strips(grids[2], ends, u[2], f[2], d[2], rest[2], 0, strips)
    h = sizes.join_rows
    fields = [join_tiles(grids, ref, grids[2].own // 2) for ref in (u[2], rest[2])]
    if weights is not None:
        fields.append(weights)
    for place, tiles in enumerate(fields):
        for k, tile in enumerate(tiles):
            outgoing[pl.ds((k * len(fields) + place) * h, h), :] = tile[:h]
    targets, parts, share, _ = message.shape
    base = lax.axis_index("gy") * (parts * share)
    for place in range(parts):
        part = outgoing[pl.ds(base + place * share, share), :]
        for target in range(targets):
            message[target, place] = part


def coarse_correction(sizes, mixing, fields):
    tiles = max(1, sizes.join_tiles // 2)
    width = sizes.join_width
    lane, row = lane_of(), row_of()
    low = lane < LANES // 2

    def each(function, *values):
        return [
            [function(*(value[k][v] for value in values)) for v in range(len(values[0][0]))]
            for k in range(tiles)
        ]

    cut = sizes.join_halves == 2

    def exchange(first, second):
        pairs = list(zip(first, second))
        low_lanes = [jnp.where(low, a, roll_lanes(b, LANES // 2)) for a, b in pairs]
        return low_lanes, [jnp.where(low, roll_lanes(a, LANES // 2), b) for a, b in pairs]

    def split(values):
        if not cut:
            return values[:tiles], values[tiles:]
        first, second = exchange(*values)
        return [first], [second]

    def join(first, second):
        return list(exchange(first[0], second[0])) if cut else first + second

    def mean(values, step):
        pair = (lane & step) == 0
        result = [[] for _ in range(tiles)]
        for v in range(0, len(values[0]), 2):
            added = [value[v] + value[v + 1] for value in values]
            right, left = from_right(added, step), from_left(added, step)
            for k in range(tiles):
                result[k].append(0.25 * (added[k] + jnp.where(pair, right[k], left[k])))
        return result

    def add(first, second):
        return each(lambda a, b: a + b, first, second)

    def subtract(first, second):
        return each(lambda a, b: a - b, first, second)

    estimate, rest, weights = fields
    _, *factors = normal_factors(mixing)
    means = split(weights)
    matrices = []
    for level in range(JOIN, LEVELS):
        if level > JOIN:
            means = [mean(part, 1 << (level - JOIN - 1)) for part in means]
        water, cross, bone = (
            each(lambda a, b, pair=pair: a * pair[0] + b * pair[1], *means) for pair in factors
        )
        matrices.append((water, bone, cross))

    def sums(level, values, with_factor):
        step = 1 << (level - JOIN)
        count = len(values[0])
        totals = [[[None] * count for _ in range(tiles)] for _ in range(2)]
        for v in range(count):
            line = [value[v] for value in values]
            for shifted, side in ((from_right(line, step), 1), (from_left(line, step), 0)):
                for k in range(tiles):
                    place = (lane + k * LANES) % width
                    inside = place < width - step if side else place >= step
                    for total, part in zip(totals, flux(shifted[k] - line[k], with_factor)):
                        part = keep(inside, part)
                        total[k][v] = part if side or part is None else total[k][v] + part
        for k, value in enumerate(values):
            edges = [
                flux(b - a, with_factor) for a, b in zip(value, value[1:])
            ]
            above, below = roll_rows(value[-1], 1), roll_rows(value[0], -1)
            has_above, has_below = row > 0, row < SUB - 1
            if cut:
                above = jnp.where(has_above, above, roll_lanes(above, LANES // 2))
                below = jnp.where(has_below, below, roll_lanes(below, LANES // 2))
                has_above = jnp.logical_or(has_above, jnp.logical_not(low))
                has_below = jnp.logical_or(has_below, low)
            first = flux(above - value[0], with_factor)
            last = flux(below - value[-1], with_factor)
            for place in range(2 if with_factor else 1):
                total = totals[place][k]
                for v, edge in enumerate(edges):
                    total[v] = total[v] + edge[place]
                    opposite = edge[place] if place else -edge[place]
                    total[v + 1] = total[v + 1] + opposite
                total[0] = total[0] + keep(has_above, first[place])
                total[-1] = total[-1] + keep(has_below, last[place])
        return totals

    def apply(level, values, flows, with_factor):
        p = scaled_penalty(level, with_factor)
        water, bone, cross = matrices[level - JOIN]
        take = lambda d, x, own, other, flow: d * own + x * other - p * flow
        return (
            each(take, water, cross, values[0], values[1], flows[0]),
            each(take, bone, cross, values[1], values[0], flows[1]),
        )

    def solve(level, values, factors, right):
        p = scaled_penalty(level, True)
        water, bone, cross = matrices[level - JOIN]
        water = each(lambda d, factor: d + p * factor, water, factors[0])
        bone = each(lambda d, factor: d + p * factor, bone, factors[1])
        scale = each(lambda a, b, x: relaxation / (a * b - x * x), water, bone, cross)
        move = lambda own, s, b, x, r, q: own + s * (b * r - x * q)
        return (
            each(move, values[0], scale, bone, cross, right[0], right[1]),
            each(move, values[1], scale, water, cross, right[1], right[0]),
        )

    def both(function, *pairs):
        return tuple(function(*(pair[m] for pair in pairs)) for m in range(2))

    def image_of(level, values, with_factor):
        totals = [sums(level, value, with_factor) for value in values]
        image = apply(level, values, [total[0] for total in totals], with_factor)
        return image, [total[1] for total in totals]

    def relax(level, values, source):
        image, factors = image_of(level, values, True)
        return solve(level, values, factors, both(subtract, source, image))

    def cycle(level, values, rest):
        image, factors = image_of(level, values, True)
        source = both(add, rest, image)
        start = values
        values = solve(level, values, factors, rest)
        if level == LEVELS - 1:
            for _ in range(COARSE_SWEEPS - 1):
                values = relax(level, values, source)
        else:
            step = 1 << (level - JOIN)
            image, _ = image_of(level, values, False)
            coarse_rest = [mean(part, step) for part in both(subtract, source, image)]
            coarse = [mean(part, step) for part in values]
            correction = cycle(level + 1, coarse, coarse_rest)
            raised = [
                [[part[v // 2] for v in range(2 * len(part))] for part in member]
                for member in correction
            ]
            values = relax(level, both(add, values, raised), source)
        return both(subtract, values, start)

    return join(*cycle(JOIN, split(estimate), split(rest)))


def ascend(sizes, ends, row_index, mixing, received, state, scratch, level_rows):
    grids = sizes.grids
    old, u, f, d, uc = state
    correction, raised = scratch
    h = sizes.join_rows
    whole = sizes.row_devices * h
    halves = sizes.join_halves
    count = whole // SUB // halves
    places = [(k, half) for k in range(sizes.join_tiles) for half in range(halves)]
    fields = []
    for ref, field, total in received:
        block = sizes.join_tiles * total * h

        def rows_of(k, half, v):
            start = (half * count * SUB + v) // h * block + (k * total + field) * h + v % h
            return ref[pl.ds(start, SUB, stride=count // h * block), :]

        fields.append([[rows_of(k, half, v) for v in range(count)] for k, half in places])
    values = coarse_correction(sizes, mixing, fields)
    for k in range(sizes.join_tiles):
        correction[k, :SUB, :] = jnp.zeros((SUB, LANES), jnp.float32)
        correction[k, pl.ds(SUB + whole, 2 * SUB), :] = jnp.zeros((2 * SUB, LANES), jnp.float32)
    for (k, half), lines in zip(places, values):
        for v in range(count):
            rows = pl.ds(SUB + half * count * SUB + v, SUB, stride=count)
            correction[k, rows, :] = lines[v]

    grid = grids[2]
    strips = grid.rows // SUB
    base = row_index * h + SUB - h
    for k in range(sizes.join_tiles):
        for start in range(0, 3 * h, SUB):
            parts = split_pair(correction[k, pl.ds(base + start, SUB), :])
            for side, part in enumerate(parts):
                member, tile = divmod(2 * k + side, grid.tiles)
                for odd in range(2):
                    raised[2][0, member, tile, pl.ds(2 * start + odd, SUB, stride=2), :] = part
    add_raised(grid, old[2], u[2], raised[2], 0, strips)
    relax_strips(grid, ends, u[2], f[2], d[2], 0, strips)

    fine = grids[1]
    places = [(group, tile) for group in range(fine.groups) for tile in range(fine.tiles)]
    for member in range(2):
        for tile in range(grid.tiles):
            for strip in range(strips):
                start = strip * SUB
                rows = pl.ds(start, SUB)
                parts = split_pair(u[2][0, member, tile, rows, :] - uc[2][0, member, tile, rows, :])
                for (g, t), part in zip(places[2 * tile : 2 * tile + 2], parts):
                    for odd in range(2):
                        raised[1][g, member, t, pl.ds(2 * start + odd, SUB, stride=2), :] = part
    (a0, z0), (a1, z1) = level_rows
    add_raised(fine, old[1], u[1], raised[1], a1 - 1, z1 + 1)
    relax_strips(fine, ends, u[1], f[1], d[1], a1, z1)

    for group in range(fine.groups):
        for member in range(2):
            for tile in range(fine.tiles):
                for strip in range(a1, z1):
                    start = strip * SUB
                    rows = pl.ds(start, SUB)
                    part = u[1][group, member, tile, rows, :] - uc[1][group, member, tile, rows, :]
                    for odd in range(2):
                        raised[0][group, member, tile, pl.ds(2 * start + odd, SUB, stride=2), :] = part
    span = max(2 * a1, a0 - 1), min(2 * z1, z0 + 1)
    add_raised(grids[0], old[0], u[0], raised[0], *span)
    relax_strips(grids[0], ends, u[0], f[0], d[0], a0, z0)


def add_raised(grid, before, field, raised, first, last):
    period = grid.tiles // 2 if grid.split else grid.tiles
    for group in range(grid.groups):
        for member in range(2):
            for tile in range(grid.tiles):
                for strip in range(first, last):
                    rows = pl.ds(strip * SUB, SUB)
                    field[group, member, tile, rows, :] = (
                        before[group, member, tile, rows, :]
                        + raised[group, member, tile % period, rows, :]
                    )


def zero_margin(grid, ref):
    for group in range(grid.groups):
        for member in range(2):
            for tile in range(grid.tiles):
                ref[group, member, tile, pl.ds(grid.rows, SUB), :] = jnp.zeros(
                    (SUB, LANES), jnp.float32
                )


def domain_ends(sizes):
    row_index = lax.axis_index("gx")
    return row_index, (row_index > 0, row_index < sizes.row_devices - 1)


def normal_factors(mixing):
    m = [[mixing[2 * i + j] for j in range(2)] for i in range(2)]
    water = [m[0][0] * m[0][0], m[1][0] * m[1][0]]
    cross = [m[0][0] * m[0][1], m[1][0] * m[1][1]]
    bone = [m[0][1] * m[0][1], m[1][1] * m[1][1]]
    return m, water, cross, bone


def split_columns(sizes, pieces, swapped, out):
    shape = (2 * LANES, 2 * LANES)
    source, target = row_of(shape), lane_of(shape)
    source = jnp.bitwise_xor(source, swapped * LANES)
    wanted = jnp.where(target < LANES, 2 * target, 2 * (target - LANES) + 1)
    select = (source == wanted).astype(jnp.float32).astype(jnp.bfloat16)
    for tile in range(sizes.tiles):
        for part in range(3):
            sides = [piece[part][...] for piece in pieces[2 * tile : 2 * tile + 2]]
            sides = [side.reshape(-1, LANES).astype(jnp.bfloat16) for side in sides]
            both = jnp.concatenate(sides, axis=1)
            result = jnp.dot(both, select, preferred_element_type=jnp.float32)
            out[tile, part] = result.reshape(out.shape[2:])


def start_kernel(sizes, mixing, *refs):
    if sizes.column_devices == 2:
        mine, early, late, *refs = refs
        pieces = [
            [mine.at[part] for part in range(3)],
            [early.at[0], early.at[1], late],
        ]
        swapped = lax.axis_index("gy")
    else:
        pieces = [
            [refs[0].at[k, part] for part in range(3)] for k in range(sizes.column_devices)
        ]
        refs = refs[1:]
        swapped = 0
    u0, u1, u2, f0, f1, f2, d0, d1, d2, uc1, uc2, message, ordered, w0, w1, w2, *rest = refs
    split_columns(sizes, pieces, swapped, ordered)
    grids = sizes.grids
    row_index, ends = domain_ends(sizes)
    for grid, ref in zip(grids, (u0, u1, u2)):
        zero_margin(grid, ref)
    m, water, cross, bone = normal_factors(mixing)
    odd_device = row_index % 2
    parts = (2 - odd_device, 0, 1 + odd_device)
    beyond = (
        jnp.where(ends[0], 0.0, 1.0),
        None,
        jnp.where(ends[1], 0.0, 1.0),
    )
    grid = grids[0]
    lane, row = lane_of(), row_of()
    half = sizes.tiles
    p = grid.penalty
    for group in range(grid.groups):
        for strip in range(grid.rows // SUB):
            start = strip * SUB
            part, inner = divmod(start, sizes.rows)

            def load(kind, energy, tile):
                plane = (2 * kind + energy) * sizes.slices + group
                rows = pl.ds(inner, SUB)
                sides = [
                    ordered[tile, parts[part], plane, rows, pl.ds(side * LANES, LANES)]
                    for side in range(2)
                ]
                if kind == 1 and beyond[part] is not None:
                    sides = [side + beyond[part] for side in sides]
                return sides

            vertical = jnp.full((SUB, LANES), 2.0, jnp.float32)
            for edge, inside in zip((grid.own - 1, 2 * grid.own - 1), ends):
                for place in (edge, edge + 1):
                    if start <= place < start + SUB:
                        missing = jnp.logical_and(row == place - start, jnp.logical_not(inside))
                        vertical = jnp.where(missing, vertical - 1.0, vertical)
            for tile in range(half):
                counts = [load(0, energy, tile) for energy in range(2)]
                weights = [load(1, energy, tile) for energy in range(2)]
                if part == 1:
                    for energy, pair in enumerate(weights):
                        w0[group, energy, tile, pl.ds(inner, SUB), :] = pair[0] + pair[1]
                for parity in range(2):
                    y = [counts[energy][parity] for energy in range(2)]
                    w = [weights[energy][parity] for energy in range(2)]
                    dw = w[0] * water[0] + w[1] * water[1]
                    dx = w[0] * cross[0] + w[1] * cross[1]
                    db = w[0] * bone[0] + w[1] * bone[1]
                    t = [w[energy] * y[energy] for energy in range(2)]
                    fw = t[0] * m[0][0] + t[1] * m[1][0]
                    fb = t[0] * m[0][1] + t[1] * m[1][1]
                    total = vertical + 2.0
                    if parity == 0 and tile == 0:
                        total = jnp.where(lane == 0, total - 1.0, total)
                    if parity == 1 and tile == half - 1:
                        total = jnp.where(lane == LANES - 1, total - 1.0, total)
                    total = p * total
                    uw, ub = solve_pair(dw + total, dx, db + total, fw, fb)
                    k = parity * half + tile
                    rows = pl.ds(start, SUB)
                    for member, value in enumerate((dw, dx, db)):
                        d0[group, member, k, rows, :] = value
                    for member, value in enumerate((fw, fb)):
                        f0[group, member, k, rows, :] = value
                    for member, value in enumerate((uw, ub)):
                        u0[group, member, k, rows, :] = value
    restrict_first(grids, d0, (d1,), 3, 0, grids[1].rows // SUB)
    restrict_second(grids, d1, (d2,), 3, 0, grids[2].rows // SUB)
    state = ((u0, u1, u2), (f0, f1, f2), (d0, d1, d2), (None, uc1, uc2), rest)
    all_rows = ((0, grids[0].rows // SUB), (0, grids[1].rows // SUB))
    restrict_first(grids, w0, (w1,), 2, 0, grids[1].own // SUB, summed=True)
    restrict_second(grids, w1, (w2,), 2, 0, grids[2].own // SUB)
    descend(sizes, ends, state, join_tiles(grids, w2, 0), message, all_rows)


def middle_rows(sizes):
    return (
        (sizes.rows // 2 // SUB, 5 * sizes.rows // 2 // SUB),
        (sizes.rows // 4 // SUB, 5 * sizes.rows // 4 // SUB),
    )


def middle_kernel(
    sizes, mixing, received, u0i, u1i, u2i, f0, f1i, f2i, d0, d1, d2, uc1i, uc2i,
    u0, u1, u2, f1, f2, uc1, uc2, message,
    correction, raised0, raised1, raised2, *rest,
):
    grids = sizes.grids
    row_index, ends = domain_ends(sizes)
    scratch = (correction, (raised0, raised1, raised2))
    fields = [(received, k, 3) for k in range(3)]
    span = middle_rows(sizes)
    old = (u0i, u1i, u2i)
    state = (old, (u0, u1, u2), (f0, f1i, f2i), (d0, d1, d2), (None, uc1i, uc2i))
    ascend(sizes, ends, row_index, mixing, fields, state, scratch, span)
    (a0, z0), _ = span
    relax_strips(grids[0], ends, u0, f0, d0, a0, z0)
    zero_margin(grids[1], u1)
    zero_margin(grids[2], u2)
    state = ((u0, u1, u2), (f0, f1, f2), (d0, d1, d2), (None, uc1, uc2), rest)
    descend(sizes, ends, state, None, message, span)


def last_kernel(
    sizes, mixing, received, first_received, u0, u1, u2, f0, f1, f2, d0, d1, d2, uc1, uc2,
    out,
    v0, v1, v2, correction, raised0, raised1, raised2,
):
    grids = sizes.grids
    row_index, ends = domain_ends(sizes)
    scratch = (correction, (raised0, raised1, raised2))
    fields = [(received, 0, 2), (received, 1, 2), (first_received, 2, 3)]
    own = (sizes.rows // SUB, 2 * sizes.rows // SUB)
    span = (own, middle_rows(sizes)[1])
    old = (u0, u1, u2)
    state = (old, (v0, v1, v2), (f0, f1, f2), (d0, d1, d2), (None, uc1, uc2))
    ascend(sizes, ends, row_index, mixing, fields, state, scratch, span)
    column_index = lax.axis_index("gy")
    lane = lane_of()
    tile = column_index // 2
    index = (column_index % 2) * (LANES // 2) + lane // 2
    even = lane % 2 == 0
    for group in range(grids[0].groups):
        for member in range(2):
            for strip in range(*own):
                rows = pl.ds(strip * SUB, SUB)
                first = v0[group, member, tile, rows, :]
                second = v0[group, member, tile + sizes.tiles, rows, :]
                out[member, group, pl.ds(strip * SUB - sizes.rows, SUB), :] = jnp.where(
                    even, take_lanes(first, index), take_lanes(second, index)
                )


def shaped(shape):
    return jax.ShapeDtypeStruct(shape, jnp.float32)


def local(spectra, noise_weights, mixing):
    row_devices, column_devices = lax.axis_size("gx"), lax.axis_size("gy")
    _, slices, rows, columns = spectra.shape
    extents = (slices, rows, columns, row_devices, column_devices)
    sizes = Sizes(*extents)
    grids = sizes.grids
    flat = (2 * slices, rows, columns)
    raw = jnp.concatenate(
        [
            spectra.astype(jnp.float32).reshape(flat),
            noise_weights.astype(jnp.float32).reshape(flat),
        ]
    )
    near, far = [], []
    for i in range(row_devices - 1):
        (far if i % 2 else near).extend([(i, i + 1), (i + 1, i)])
    beside = [lax.ppermute(raw, "gx", far), lax.ppermute(raw, "gx", near)][::-1]
    tiles = jnp.stack([raw] + beside)
    if column_devices == 2:
        swap = lambda value: lax.ppermute(value, "gy", [(0, 1), (1, 0)])
        pieces = (tiles, swap(jnp.stack([raw, beside[0]])), swap(beside[1]))
    else:
        pieces = (lax.all_gather(tiles, "gy"),)

    def vmem(shape):
        return pltpu.VMEM(shape, jnp.float32)

    def message_shape(fields):
        share = sizes.join_tiles * fields * sizes.join_rows // column_devices
        group = next(g for g in (8, 4, 2, 1) if share % g == 0)
        return (row_devices * column_devices, share // group, group, LANES)

    fields = [grid.shape(2) for grid in grids]
    datas = [grid.shape(3) for grid in grids]

    def halved(shape):
        return shape[:2] + (shape[2] // 2,) + shape[3:]

    rests = [vmem(halved(fields[0])), vmem(fields[1]), vmem(fields[2])]
    rests.append(vmem((sizes.join_tiles * 3 * sizes.join_rows, LANES)))
    join_whole = row_devices * sizes.join_rows
    coarse = [
        vmem((sizes.join_tiles, join_whole + 3 * SUB, LANES)),
        vmem(halved(fields[0])),
        vmem(fields[1]),
        vmem(fields[2]),
    ]

    vmem_limit = min(16 * max(1, sizes.tiles), 60) << 20

    def call(body, outs, scratch):
        kernel = lambda *refs: body(Sizes(*extents), *refs)
        return pl.pallas_call(
            kernel,
            out_shape=[shaped(shape) for shape in outs],
            scratch_shapes=scratch,
            name=body.__name__,
            compiler_params=pltpu.CompilerParams(vmem_limit_bytes=vmem_limit),
        )

    outs = fields + fields + datas + fields[1:] + [message_shape(3)]
    weights = [
        vmem((slices, 2, sizes.tiles, rows, LANES)),
        vmem((slices, 2, sizes.tiles, grids[1].own, LANES)),
        vmem((1, 2, grids[2].tiles, max(grids[2].own, 2 * SUB), LANES)),
    ]
    spread = jnp.broadcast_to(mixing.reshape(-1, 1, 1), (mixing.size, SUB, LANES))
    u0, u1, u2, f0, f1, f2, d0, d1, d2, uc1, uc2, message = call(
        start_kernel, outs, [vmem((sizes.tiles,) + tiles.shape[:3] + (2 * LANES,))] + weights + rests
    )(spread, *pieces)
    first_received = lax.all_to_all(message, ("gx", "gy"), 0, 0, tiled=True).reshape(-1, LANES)
    outs = fields + fields[1:] + fields[1:] + [message_shape(2)]
    u0, u1, u2, f1, f2, uc1, uc2, message = call(middle_kernel, outs, coarse + rests)(
        spread, first_received, u0, u1, u2, f0, f1, f2, d0, d1, d2, uc1, uc2
    )
    received = lax.all_to_all(message, ("gx", "gy"), 0, 0, tiled=True).reshape(-1, LANES)
    outs = [(2, slices, rows, columns)]
    return call(last_kernel, outs, [vmem(shape) for shape in fields] + coarse)(
        spread, received, first_received, u0, u1, u2, f0, f1, f2, d0, d1, d2, uc1, uc2
    )[0]


def solution(mesh):
    return jax.shard_map(
        local,
        mesh=mesh,
        in_specs=(P(None, None, "gx", "gy"), P(None, None, "gx", "gy"), P()),
        out_specs=P(None, None, "gx", "gy"),
        check_vma=False,
    )
```
